32 devices in a mesh: dom: 8 (over z, y), kb: 4 (over x, core).
Axes of the slice: x: 2, y: 2, z: 4, core: 2. Of those that a mesh axis runs over, the one named last changes fastest.
Arguments:
- features: bfloat16 [64, 4096], P(None, ('dom', 'kb')), may hold values from -6 to 6
- vectors: bfloat16 [3, 64, 4096], P(None, None, ('dom', 'kb')), may hold values from -6 to 6
- positions: float32 [3, 4096], P(None, ('dom', 'kb')), may hold values from 0 to 1, as said below
- neighbours: int32 [16, 4096], P(None, ('dom', 'kb')), may hold values from 0 to 384, as said below
- halo_lists: int32 [2, 4096], P(None, ('dom', 'kb')), may hold values from 0 to 127, as said below
- lattice: int32 [3, 2048], replicated, may hold values from -1024 to 1024, as said below
- kspace_filter: float32 [64, 2048], P(None, 'kb'), may hold values from -6 to 6
- node_weight: bfloat16 [64, 64], replicated, may hold values from -0.75 to 0.75
- node_bias: float32 [64], replicated, may hold values from -4 to 4
- message_weight: bfloat16 [64, 192], replicated, may hold values from -0.75 to 0.75
- radial_weight: bfloat16 [20, 192], replicated, may hold values from -3 to 3
- ewald_weight: bfloat16 [64, 64], replicated, may hold values from -0.75 to 0.75
Outputs:
- new_features: bfloat16 [64, 4096], P(None, ('dom', 'kb'))
- new_vectors: bfloat16 [3, 64, 4096], P(None, None, ('dom', 'kb'))
The draws below stay inside these ranges and needn't reach their ends.
Inputs may be any that keep to these rules, and one draw needn't show every extreme that they name: `neighbours`: entry j of column a names atom a's neighbour in the numbering of E = 385 columns: own atoms, then the atoms received from the device below, then those from the device above; 384 marks an empty slot. Empty slots come last in a column, and each atom has 8 or more filled slots. `halo_lists`: for each device, 128 different local atom numbers in each row. `positions`: atom a's third coordinate times 8 * 4 lies between a // 128 and the next integer. `lattice`: rows 0 and 1 lie between -16 and 16.
All inputs are finite; a program needn't handle non-finite values.
Results may differ from the reference program's by a relative error of at most 0.01.
Values may be sent and summed in bfloat16 or wider, within the bound.
A program may use at most 64 MiB of HBM per device.

```python
import math
import jax
import jax.numpy as jnp
from jax import lax

F = 64
NRBF = 20
NBR = 16
HALO = 128
ATOM_DEV = 128
ATOMS = 4096
KVEC = 2048
N_DOM = 8
N_KB = 4


def draw_positions(key, part):
    slab_count = ATOMS // ATOM_DEV
    across = jax.random.uniform(jax.random.fold_in(key, 11), (2, ATOMS), jnp.float32)
    within = jax.random.uniform(jax.random.fold_in(key, 12), (ATOMS,), jnp.float32)
    slab_number = (jnp.arange(ATOMS) // ATOM_DEV).astype(jnp.float32)
    height = (slab_number + within) / slab_count
    return jnp.concatenate([across, height[None, :]], axis=0)


def draw_neighbours(key, part):
    counts = jax.random.randint(jax.random.fold_in(key, 21), (1, ATOMS), NBR // 2, NBR + 1)
    chosen = jax.random.randint(jax.random.fold_in(key, 22), (NBR, ATOMS), 0, ATOM_DEV + 2 * HALO)
    slot_number = jnp.arange(NBR)[:, None]
    return jnp.where(slot_number < counts, chosen, ATOM_DEV + 2 * HALO).astype(jnp.int32)


def draw_halo_lists(key, part):
    slab_count = ATOMS // ATOM_DEV
    split_keys = jax.random.split(jax.random.fold_in(key, 31), 2 * slab_count)

    def choose(one_key):
        return jax.random.permutation(one_key, ATOM_DEV)[:HALO]
    chosen = jax.vmap(choose)(split_keys)
    return chosen.reshape(2, slab_count * HALO).astype(jnp.int32)


def draw_lattice(key, part):
    across = jax.random.randint(jax.random.fold_in(key, 41), (2, KVEC), -16, 17)
    depth = jax.random.randint(jax.random.fold_in(key, 42), (1, KVEC), -1024, 1025)
    return jnp.concatenate([across, depth], axis=0).astype(jnp.int32)


def levels(own_key, dims, pieces, low, top_value):
    loudness, own = 1.0, jax.random.fold_in(own_key, 6)
    for dim, blocks in pieces:
        steps = jnp.exp(jax.random.uniform(jax.random.fold_in(own, dim), (blocks,), jnp.float32, low / len(pieces), top_value / len(pieces)))
        loudness = loudness * jnp.repeat(steps, dims[dim] // blocks).reshape([-1 if axis == dim else 1 for axis in range(len(dims))])
    return loudness


def noise(own_key, extent, scale, most, shards=(), dtype=jnp.bfloat16):
    level = levels(own_key, extent, shards, -0.22, 0.18) if shards else 1.0
    result = jax.random.normal(own_key, extent, jnp.float32) * scale * level
    return jnp.minimum(jnp.maximum(result, -most), most).astype(dtype)


def setup_inputs(seed: int = 0) -> dict:
    seeds = jax.random.split(jax.random.key(seed), 13)
    features = noise(seeds[0], (F, ATOMS), 1.0, 6.0, ((1, 32),))
    vectors = noise(seeds[1], (3, F, ATOMS), 1.0, 6.0, ((2, 32),))
    positions = draw_positions(jax.random.fold_in(seeds[12], 71), 0)
    neighbours = draw_neighbours(jax.random.fold_in(seeds[12], 71), 0)
    halo_lists = draw_halo_lists(jax.random.fold_in(seeds[12], 71), 0)
    lattice = draw_lattice(jax.random.fold_in(seeds[12], 71), 0)
    kspace_filter = noise(seeds[6], (F, KVEC), 1.0, 6.0, ((1, 4),), jnp.float32)
    node_weight = noise(seeds[7], (F, F), F ** -0.5, 0.75)
    node_bias = noise(seeds[8], (F,), 1.0, 4.0, (), jnp.float32)
    message_weight = noise(seeds[9], (F, 3 * F), F ** -0.5, 0.75)
    radial_weight = noise(seeds[10], (NRBF, 3 * F), 4 ** -0.5, 3.0)
    ewald_weight = noise(seeds[11], (F, F), F ** -0.5, 0.75)
    return {"features": features, "vectors": vectors, "positions": positions, "neighbours": neighbours, "halo_lists": halo_lists, "lattice": lattice, "kspace_filter": kspace_filter, "node_weight": node_weight, "node_bias": node_bias, "message_weight": message_weight, "radial_weight": radial_weight, "ewald_weight": ewald_weight}


full_turn = 2.0 * math.pi
side_length = 6.0
slab_depth = 6.0
radial_reach = 6.0
distance_floor = 1.0

def over_first(first_operand, second_operand):
    return lax.dot_general(first_operand, second_operand, (((0,), (0,)), ((), ())), preferred_element_type=jnp.float32)

def over_last(first_operand, second_operand):
    return lax.dot_general(first_operand, second_operand, (((1,), (1,)), ((), ())), preferred_element_type=jnp.float32)

def phase_tables(coords, lattice_rows):
    phase_angle = (coords[0][:, None] * lattice_rows[0][None, :] + coords[1][:, None] * lattice_rows[1][None, :] + coords[2][:, None] * lattice_rows[2][None, :]) * full_turn
    return (jnp.cos(phase_angle).astype(jnp.bfloat16), jnp.sin(phase_angle).astype(jnp.bfloat16))

def short_range(own_feat, own_vec, own_pos, neighbour_ids, side_feat, side_vec, side_pos, node_weight, node_bias, message_weight, radial_weight, slab_count):
    channels = own_feat.shape[0]
    own_count = own_feat.shape[1]
    slot_count = neighbour_ids.shape[0]
    radial_count = radial_weight.shape[0]
    ext_feat = jnp.concatenate([own_feat, side_feat, jnp.zeros((channels, 1), jnp.bfloat16)], axis=1)
    ext_vec = jnp.concatenate([own_vec, side_vec, jnp.zeros((3, channels, 1), jnp.bfloat16)], axis=2)
    ext_pos = jnp.concatenate([own_pos, side_pos, jnp.zeros((3, 1), jnp.float32)], axis=1)
    empty_slot = ext_feat.shape[1] - 1
    hidden = jax.nn.silu(over_first(node_weight, ext_feat) + node_bias[:, None]).astype(jnp.bfloat16)
    message_in = over_first(message_weight, hidden).astype(jnp.bfloat16)
    flat_ids = neighbour_ids.reshape(-1)
    weights_on = (flat_ids < empty_slot).astype(jnp.float32)
    offsets = jnp.take(ext_pos, flat_ids, axis=1).reshape(3, slot_count, own_count) - own_pos[:, None, :]
    offsets = offsets - jnp.floor(offsets + 0.5)
    box_sides = jnp.array([side_length, side_length, slab_depth * slab_count], jnp.float32)
    cartesian = offsets * box_sides[:, None, None]
    distance = jnp.sqrt(lax.optimization_barrier(jnp.sum(cartesian * cartesian, axis=0)))
    direction = cartesian / jnp.maximum(distance, distance_floor)
    centers = jnp.arange(radial_count).astype(jnp.float32) * (radial_reach / (radial_count - 1))
    spread = 1.5 * radial_reach / radial_count
    radial = jnp.exp(-jnp.square((distance[None] - centers[:, None, None]) / spread)).astype(jnp.bfloat16)
    edge_filter = over_first(radial_weight, radial.reshape(radial_count, -1))
    edge_terms = jnp.take(message_in, flat_ids, axis=1).astype(jnp.float32) * edge_filter * weights_on
    edge_terms = edge_terms.reshape(3 * channels, slot_count, own_count)
    scalar_part = lax.optimization_barrier(jnp.sum(edge_terms[:channels], axis=1))
    neighbour_vec = jnp.take(ext_vec, flat_ids, axis=2).reshape(3, channels, slot_count, own_count).astype(jnp.float32)
    vector_part = lax.optimization_barrier(jnp.sum(neighbour_vec * edge_terms[channels:2 * channels][None] + edge_terms[2 * channels:][None] * direction[:, None], axis=2))
    return (scalar_part, vector_part)

def take_columns(source, chosen):
    return jnp.take(source, chosen, axis=1)

def take_vector_columns(source, chosen):
    return jnp.take(source, chosen, axis=2)

def reference(features, vectors, positions, neighbours, halo_lists, lattice, kspace_filter, node_weight, node_bias, message_weight, radial_weight, ewald_weight):
    slab_count = N_DOM * N_KB
    channels = features.shape[0]
    own_feat = features.reshape(channels, slab_count, ATOM_DEV).transpose(1, 0, 2)
    own_vec = vectors.reshape(3, channels, slab_count, ATOM_DEV).transpose(2, 0, 1, 3)
    own_pos = positions.reshape(3, slab_count, ATOM_DEV).transpose(1, 0, 2)
    own_ids = neighbours.reshape(NBR, slab_count, ATOM_DEV).transpose(1, 0, 2)
    halo_rows = halo_lists.reshape(2, slab_count, HALO)

    def picked(index_rows):
        sent_feat = jax.vmap(take_columns)(own_feat, index_rows)
        sent_vec = jax.vmap(take_vector_columns)(own_vec, index_rows)
        sent_pos = jax.vmap(take_columns)(own_pos, index_rows)
        return (sent_feat, sent_vec, sent_pos)
    up_feat, up_vec, up_pos = picked(halo_rows[0])
    down_feat, down_vec, down_pos = picked(halo_rows[1])
    side_feat = jnp.concatenate([jnp.roll(up_feat, 1, axis=0), jnp.roll(down_feat, -1, axis=0)], axis=2)
    side_vec = jnp.concatenate([jnp.roll(up_vec, 1, axis=0), jnp.roll(down_vec, -1, axis=0)], axis=3)
    side_pos = jnp.concatenate([jnp.roll(up_pos, 1, axis=0), jnp.roll(down_pos, -1, axis=0)], axis=2)

    def per_device(device_group):
        return short_range(device_group[0], device_group[1], device_group[2], device_group[3], device_group[4], device_group[5], device_group[6], node_weight, node_bias, message_weight, radial_weight, slab_count)
    scalar_part, vector_part = lax.map(per_device, (own_feat, own_vec, own_pos, own_ids, side_feat, side_vec, side_pos))
    scalar_all = scalar_part.transpose(1, 0, 2).reshape(channels, -1)
    vector_all = vector_part.transpose(1, 2, 0, 3).reshape(3, channels, -1)
    ewald_in = over_first(ewald_weight, features).astype(jnp.bfloat16)
    lattice_rows = lattice.astype(jnp.float32)
    block_size = 4 * ATOM_DEV
    block_count = ATOMS // block_size
    in_blocks = ewald_in.reshape(channels, block_count, block_size).transpose(1, 0, 2)
    pos_blocks = positions.reshape(3, block_count, block_size).transpose(1, 0, 2)

    def accumulate(totals, device_group):
        cosine_table, sine_table = phase_tables(device_group[1], lattice_rows)
        return ((totals[0] + jnp.dot(device_group[0], cosine_table, preferred_element_type=jnp.float32), totals[1] + jnp.dot(device_group[0], sine_table, preferred_element_type=jnp.float32)), None)
    zero_sums = jnp.zeros((channels, KVEC), jnp.float32)
    totals, ignored = lax.scan(accumulate, (zero_sums, zero_sums), (in_blocks, pos_blocks))
    norm_scale = 1.0 / math.sqrt(KVEC * ATOMS)
    filt_re = (kspace_filter * totals[0] * norm_scale).astype(jnp.bfloat16)
    filt_im = (kspace_filter * totals[1] * norm_scale).astype(jnp.bfloat16)

    def project(coords):
        cosine_table, sine_table = phase_tables(coords, lattice_rows)
        return over_last(filt_re, cosine_table) + over_last(filt_im, sine_table)
    message = lax.map(project, pos_blocks).transpose(1, 0, 2).reshape(channels, -1)
    new_features = (features.astype(jnp.float32) + scalar_all + message).astype(jnp.bfloat16)
    new_vectors = (vectors.astype(jnp.float32) + vector_all).astype(jnp.bfloat16)
    return (new_features, new_vectors)
```

```python
import functools
import math

import jax
import jax.numpy as jnp
import numpy as np
from jax import lax
from jax.experimental import pallas as pl
from jax.experimental.pallas import tpu as pltpu
from jax.sharding import PartitionSpec as P

side_length = 6.0
slab_depth = 6.0
radial_reach = 6.0
distance_floor = 1.0
MESH = pl.DeviceIdType.MESH
f32 = jnp.float32
bf16 = jnp.bfloat16


def polynomial(function, degree):
    nodes = (np.cos((np.arange(degree + 1) + 0.5) * np.pi / (degree + 1)) + 1.0) / 2.0
    fitted = np.polynomial.polynomial.polyfit(nodes, function(nodes / 16.0), degree)
    return [float(value * 16.0**power) for power, value in enumerate(fitted)]


cos_terms = polynomial(lambda w: np.cos(2 * np.pi * np.sqrt(w)), 4)
sin_terms = polynomial(lambda w: np.sin(2 * np.pi * np.sqrt(w)) / np.sqrt(w), 4)


def evaluate(terms, w):
    value = terms[-1] * w + terms[-2]
    for term in terms[-3::-1]:
        value = value * w + term
    return value


def turn_tables(turns):
    part = turns - jnp.floor(turns + 0.5)
    shifted = 0.25 - jnp.abs(part)
    w = shifted * shifted
    cosine = shifted * evaluate(sin_terms, w)
    sine = evaluate(cos_terms, w)
    sine = jnp.where(part < 0.0, -sine, sine)
    return cosine.astype(bf16), sine.astype(bf16)


def over_first(first_operand, second_operand):
    return lax.dot_general(
        first_operand, second_operand, (((0,), (0,)), ((), ())), preferred_element_type=f32
    )


def three_parts(value):
    high = value.astype(bf16)
    rest = value - high.astype(f32)
    middle = rest.astype(bf16)
    low = (rest - middle.astype(f32)).astype(bf16)
    return high.astype(f32), middle.astype(f32), low.astype(f32)


def kernel(
    sizes,
    feat,
    vec,
    pos,
    nbr,
    halo,
    lat,
    kfilter,
    node_weight,
    node_bias,
    message_weight,
    radial_weight,
    ewald_weight,
    out_all,
    group_feat,
    group_pos,
    side_feat,
    side_vec,
    side_pos,
    side_halo,
    cosines,
    sines,
    totals,
    totals_out,
    totals_in,
    filtered,
    filter_rows,
    message_own,
    message_out,
    message_in_slots,
    source_rows,
    group_sems,
    side_sems,
    totals_sems,
    filtered_sems,
    message_sems,
):
    n_dom, n_kb, low_count, norm_scale = sizes
    high_count = n_dom // low_count
    members = low_count * n_kb
    dom, kb = lax.axis_index("dom"), lax.axis_index("kb")
    high, low = lax.div(dom, low_count), lax.rem(dom, low_count)
    me = low * n_kb + kb
    rank = dom * n_kb + kb
    slab_count = n_dom * n_kb
    channels, own = feat.shape
    slots = nbr.shape[0]
    width = kfilter.shape[1] // low_count
    chunk = width // high_count

    def member(steps):
        number = lax.rem(me + steps + members, members)
        return {
            "dom": high * low_count + lax.div(number, n_kb),
            "kb": lax.rem(number, n_kb),
        }

    def level(steps):
        number = lax.rem(high + steps + high_count, high_count)
        return number, {"dom": number * low_count + low, "kb": kb}

    def slab(steps):
        number = lax.rem(rank + steps + slab_count, slab_count)
        return {"dom": lax.div(number, n_kb), "kb": lax.rem(number, n_kb)}

    def remote(source, target, sems, index, device):
        return pltpu.make_async_remote_copy(
            src_ref=source,
            dst_ref=target,
            send_sem=sems.at[(0,) + index],
            recv_sem=sems.at[(1,) + index],
            device_id=device,
            device_id_type=MESH,
        )

    barrier = pltpu.get_barrier_semaphore()
    greeted = [member(d) for d in range(1, members)]
    greeted += [level(d)[1] for d in range(1, high_count)]
    greeted += [slab(1), slab(-1)]
    for device in greeted:
        pl.semaphore_signal(barrier, inc=1, device_id=device, device_id_type=MESH)

    start = pl.multiple_of(kb * (width * low_count) + low * width, math.gcd(width, 128))
    lattice = lat[:, pl.ds(start, width)].astype(f32)
    lattice_high = jnp.floor(lattice[2:3] * 0.0625) * 16.0
    lattice_low = lattice[2:3] - lattice_high
    lattice_parts = jnp.concatenate(
        [lattice[0:1]] * 3
        + [lattice[1:2]] * 3
        + [lattice_high] * 3
        + [lattice_low] * 3
        + [jnp.zeros((4, width), f32)],
        axis=0,
    ).astype(bf16)

    def position_parts(coords):
        rows = []
        for axis in (0, 1, 2, 2):
            rows += list(three_parts(coords[axis : axis + 1]))
        rows.append(jnp.zeros((4, own), f32))
        return jnp.concatenate(rows, axis=0).astype(bf16)

    def tables(slot, coords):
        turns = over_first(lattice_parts, position_parts(coords))
        cosine, sine = turn_tables(turns)
        cosines[:, slot * own : (slot + 1) * own] = cosine
        sines[:, slot * own : (slot + 1) * own] = sine
        return cosine, sine

    def add_totals(slot, cosine, sine, features):
        projected = over_first(features, ewald_weight[...]).astype(bf16)
        both = jnp.concatenate(
            [
                jnp.dot(cosine, projected, preferred_element_type=f32),
                jnp.dot(sine, projected, preferred_element_type=f32),
            ],
            axis=1,
        )
        if slot == 0:
            totals[...] = both
        else:
            totals[...] += both

    pl.semaphore_wait(barrier, len(greeted))
    group_copies = []
    for d in range(1, members):
        device = member(d)
        group_copies.append(remote(pos, group_pos.at[d], group_sems, (0, d), device))
        group_copies.append(remote(feat, group_feat.at[d], group_sems, (1, d), device))
    for copy in group_copies:
        copy.start()
    side_copies = []
    for side, steps in ((0, 1), (1, -1)):
        device = slab(steps)
        side_copies.append(remote(feat, side_feat.at[side], side_sems, (0, side), device))
        side_copies.append(remote(vec, side_vec.at[side], side_sems, (1, side), device))
        side_copies.append(remote(pos, side_pos.at[side], side_sems, (2, side), device))
        side_copies.append(remote(halo, side_halo.at[side], side_sems, (3, side), device))
    for copy in side_copies:
        copy.start()

    transposed = kfilter[...].T
    filter_rows[...] = jnp.concatenate([transposed, transposed], axis=1) * norm_scale
    cosine, sine = tables(0, pos[...])
    add_totals(0, cosine, sine, feat[...])
    for d in range(1, members):
        group_copies[2 * d - 2].wait_recv()
        cosine, sine = tables(d, group_pos[d])
        group_copies[2 * d - 1].wait_recv()
        add_totals(d, cosine, sine, group_feat[d])
    totals_out[...] = totals[...].astype(bf16)

    totals_copies = []
    for d in range(1, high_count):
        number, device = level(d)
        rows = pl.ds(pl.multiple_of(number * chunk, chunk), chunk)
        totals_copies.append(
            remote(totals_out.at[rows], totals_in.at[d], totals_sems, (d,), device)
        )
    near_first = sorted(range(1, high_count), key=lambda d: min(d, high_count - d))
    for d in near_first:
        totals_copies[d - 1].start()

    for copy in side_copies:
        copy.wait_recv()
    bias = jnp.broadcast_to(node_bias[...], (own, channels)).T
    for index, (one_feat, one_vec) in enumerate(
        ((feat, vec), (side_feat.at[0], side_vec.at[0]), (side_feat.at[1], side_vec.at[1]))
    ):
        columns = slice(index * own, (index + 1) * own)
        value = over_first(node_weight[...], one_feat[...]) + bias
        hidden = (value / (1.0 + jnp.exp(-value))).astype(bf16)
        source_rows[: 3 * channels, columns] = over_first(message_weight[...], hidden).astype(bf16)
        source_rows[3 * channels :, columns] = one_vec[...].reshape(3 * channels, own)

    ids = nbr[...]
    reach = halo.shape[1]

    def picked(row, index):
        return jnp.take_along_axis(
            jnp.broadcast_to(row, (slots, row.shape[1])), index, axis=1, mode="promise_in_bounds"
        )

    below_slot = jnp.clip(ids - own, 0, reach - 1)
    above_slot = jnp.clip(ids - (own + reach), 0, reach - 1)
    own_atom = jnp.clip(ids, 0, own - 1)
    below_atom = picked(side_halo[0, 0:1], below_slot)
    above_atom = picked(side_halo[1, 1:2], above_slot)
    is_own = ids < own
    is_below = ids < own + reach
    used = ids < own + 2 * reach
    atoms = jnp.where(
        is_own,
        ids,
        jnp.where(is_below, below_atom + own, jnp.where(used, above_atom + 2 * own, 3 * own)),
    )
    cartesian = []
    for axis in range(3):
        taken = jnp.where(
            is_own,
            picked(pos[axis : axis + 1], own_atom),
            jnp.where(
                is_below,
                picked(side_pos[0, axis : axis + 1], below_atom),
                picked(side_pos[1, axis : axis + 1], above_atom),
            ),
        )
        taken = jnp.where(used, taken, 0.0)
        offset = taken - pos[axis : axis + 1]
        offset = offset - jnp.floor(offset + 0.5)
        cartesian.append(offset * (side_length if axis < 2 else slab_depth * slab_count))
    distance = jnp.sqrt(
        cartesian[0] * cartesian[0] + cartesian[1] * cartesian[1] + cartesian[2] * cartesian[2]
    )
    limit = jnp.maximum(distance, distance_floor)
    direction = [part / limit for part in cartesian]

    radial_count = radial_weight.shape[0]
    spread = 1.5 * radial_reach / radial_count
    centers = lax.broadcasted_iota(jnp.int32, (radial_count, own), 0).astype(f32) * (
        radial_reach / (radial_count - 1)
    )
    numbers = lax.broadcasted_iota(jnp.int32, (3 * own, own), 0)

    def edges(j, sums):
        row = slice(j, j + 1)
        chosen = jnp.where(numbers == atoms[row], 1.0, 0.0).astype(bf16)
        gathered = jnp.dot(source_rows[...], chosen, preferred_element_type=f32)
        scaled = (distance[row] - centers) * (1.0 / spread)
        radial = jnp.exp(-(scaled * scaled)).astype(bf16)
        terms = gathered[: 3 * channels] * over_first(radial_weight[...], radial)
        first = terms[:channels]
        second = terms[channels : 2 * channels]
        third = terms[2 * channels :]
        new = [sums[0] + first]
        for axis in range(3):
            begin = (3 + axis) * channels
            new.append(
                sums[1 + axis]
                + gathered[begin : begin + channels] * second
                + third * direction[axis][row]
            )
        return new

    sums = [jnp.zeros((channels, own), f32)] * 4
    half = slots // 2
    for j in range(half):
        sums = edges(j, sums)

    own_rows = pl.ds(pl.multiple_of(high * chunk, chunk), chunk)
    total = totals[own_rows, :]
    for d in range(1, high_count):
        totals_copies[d - 1].wait_recv()
        total = total + totals_in[d].astype(f32)
    filter_start = pl.multiple_of(low * width + high * chunk, chunk)
    filtered[own_rows, :] = (filter_rows[pl.ds(filter_start, chunk), :] * total).astype(bf16)
    filtered_copies = []
    for d in range(1, high_count):
        filtered_copies.append(
            remote(
                filtered.at[own_rows], filtered.at[own_rows], filtered_sems, (d,), level(d)[1]
            )
        )
    for d in near_first:
        filtered_copies[d - 1].start()

    for j in range(half, slots):
        sums = edges(j, sums)
    for axis in range(3):
        out_all[1 + axis] = (vec[axis].astype(f32) + sums[1 + axis]).astype(bf16)
    message_own[...] = feat[...].astype(f32) + sums[0]

    for copy in filtered_copies:
        copy.wait_recv()
    spectrum = filtered[...]
    real_rows = spectrum.T[:channels]
    imag_rows = spectrum.T[channels:]

    def message_of(d):
        columns = slice(d * own, (d + 1) * own)
        return jnp.dot(
            real_rows, cosines[:, columns], preferred_element_type=f32
        ) + jnp.dot(imag_rows, sines[:, columns], preferred_element_type=f32)

    message_copies = []
    for d in range(1, members):
        message_out[d] = message_of(d).astype(bf16)
        message_copies.append(
            remote(message_out.at[d], message_in_slots.at[d], message_sems, (d,), member(-d))
        )
        message_copies[-1].start()
    result = message_own[...] + message_of(0)
    for copy in message_copies:
        copy.wait_recv()
    for d in range(1, members):
        result = result + message_in_slots[d].astype(f32)
    out_all[0] = result.astype(bf16)
    for copy in group_copies + side_copies + totals_copies + filtered_copies + message_copies:
        copy.wait_send()


def split_kernel(both, out_feat, out_vec, sems):
    feat_copy = pltpu.make_async_copy(both.at[0], out_feat, sems.at[0])
    vec_copy = pltpu.make_async_copy(both.at[pl.ds(1, 3)], out_vec, sems.at[1])
    feat_copy.start()
    vec_copy.start()
    feat_copy.wait()
    vec_copy.wait()


def shards(
    features,
    vectors,
    positions,
    neighbours,
    halo_lists,
    lattice,
    kspace_filter,
    node_weight,
    node_bias,
    message_weight,
    radial_weight,
    ewald_weight,
):
    n_dom, n_kb = lax.axis_size("dom"), lax.axis_size("kb")
    low_count = 1
    high_count = n_dom // low_count
    members = low_count * n_kb
    channels, own = features.shape
    reach = halo_lists.shape[1]
    width = kspace_filter.shape[1] // low_count
    chunk = width // high_count
    norm_scale = 1.0 / math.sqrt(lattice.shape[1] * own * n_dom * n_kb)
    vmem = pl.BlockSpec(memory_space=pltpu.VMEM)
    dma = pltpu.SemaphoreType.DMA
    both = pl.pallas_call(
        functools.partial(kernel, (n_dom, n_kb, low_count, norm_scale)),
        out_shape=pltpu.VMEM((4, channels, own), bf16),
        in_specs=[vmem] * 12,
        out_specs=vmem,
        scratch_shapes=[
            pltpu.VMEM((members, channels, own), bf16),
            pltpu.VMEM((members, 3, own), f32),
            pltpu.VMEM((2, channels, own), bf16),
            pltpu.VMEM((2, 3, channels, own), bf16),
            pltpu.VMEM((2, 3, own), f32),
            pltpu.VMEM((2, 2, reach), jnp.int32),
            pltpu.VMEM((width, members * own), bf16),
            pltpu.VMEM((width, members * own), bf16),
            pltpu.VMEM((width, 2 * channels), f32),
            pltpu.VMEM((width, 2 * channels), bf16),
            pltpu.VMEM((high_count, chunk, 2 * channels), bf16),
            pltpu.VMEM((width, 2 * channels), bf16),
            pltpu.VMEM((kspace_filter.shape[1], 2 * channels), f32),
            pltpu.VMEM((channels, own), f32),
            pltpu.VMEM((members, channels, own), bf16),
            pltpu.VMEM((members, channels, own), bf16),
            pltpu.VMEM((6 * channels, 3 * own), bf16),
            dma((2, 2, members)),
            dma((2, 4, 2)),
            dma((2, high_count)),
            dma((2, high_count)),
            dma((2, members)),
        ],
        compiler_params=pltpu.CompilerParams(collective_id=0, has_side_effects=True),
    )(
        features,
        vectors,
        positions,
        neighbours,
        halo_lists,
        lattice,
        kspace_filter,
        node_weight,
        node_bias[None, :],
        message_weight,
        radial_weight,
        ewald_weight,
    )
    return pl.pallas_call(
        split_kernel,
        out_shape=(
            jax.ShapeDtypeStruct(features.shape, bf16),
            jax.ShapeDtypeStruct(vectors.shape, bf16),
        ),
        in_specs=[vmem],
        out_specs=(pl.BlockSpec(memory_space=pl.ANY),) * 2,
        scratch_shapes=[dma((2,))],
    )(pltpu.with_memory_space_constraint(both, pltpu.VMEM))


def solution(mesh):
    atoms = P(None, ("dom", "kb"))
    placed = (
        atoms,
        P(None, None, ("dom", "kb")),
        atoms,
        atoms,
        atoms,
        P(),
        P(None, "kb"),
        P(),
        P(),
        P(),
        P(),
        P(),
    )
    return jax.shard_map(
        shards,
        mesh=mesh,
        in_specs=placed,
        out_specs=(atoms, P(None, None, ("dom", "kb"))),
        check_vma=False,
    )
```

```python
import functools
import math

import jax
import jax.numpy as jnp
import numpy as np
from jax import lax
from jax.experimental import pallas as pl
from jax.experimental.pallas import tpu as pltpu
from jax.sharding import PartitionSpec as P

side_length = 6.0
slab_depth = 6.0
radial_reach = 6.0
distance_floor = 1.0
MESH = pl.DeviceIdType.MESH
f32 = jnp.float32
bf16 = jnp.bfloat16


def polynomial(function, degree):
    nodes = (np.cos((np.arange(degree + 1) + 0.5) * np.pi / (degree + 1)) + 1.0) / 2.0
    fitted = np.polynomial.polynomial.polyfit(nodes, function(nodes / 4.0), degree)
    return [float(value * 4.0**power) for power, value in enumerate(fitted)]


half_cos = polynomial(lambda w: np.sqrt(2.0) * np.cos(np.pi * np.sqrt(w)), 3)
half_sin = polynomial(lambda w: np.sqrt(2.0) * np.sin(np.pi * np.sqrt(w)) / np.sqrt(w), 3)


def evaluate(terms, w):
    value = terms[-1] * w + terms[-2]
    for term in terms[-3::-1]:
        value = value * w + term
    return value


def turn_tables(turns):
    part = turns - jnp.round(turns)
    w = part * part
    sine = part * evaluate(half_sin, w)
    cosine = evaluate(half_cos, w)
    return (1.0 - sine * sine).astype(bf16), (sine * cosine).astype(bf16)


def over_first(first_operand, second_operand):
    return lax.dot_general(
        first_operand, second_operand, (((0,), (0,)), ((), ())), preferred_element_type=f32
    )


def three_parts(value):
    high = value.astype(bf16)
    rest = value - high.astype(f32)
    middle = rest.astype(bf16)
    low = (rest - middle.astype(f32)).astype(bf16)
    return high.astype(f32), middle.astype(f32), low.astype(f32)


def kernel(
    sizes,
    feat_hbm,
    vec_hbm,
    pos_hbm,
    nbr_hbm,
    halo_hbm,
    lat_hbm,
    kfilter_hbm,
    node_weight_hbm,
    node_bias_hbm,
    message_weight_hbm,
    radial_weight_hbm,
    ewald_weight_hbm,
    out_all,
    feat,
    vec,
    pos,
    nbr,
    lat,
    kfilter,
    node_weight,
    node_bias,
    message_weight,
    radial_weight,
    ewald_weight,
    own_projected,
    group_feat,
    group_pos,
    side_rows,
    side_pos,
    side_halo,
    tables,
    near_totals,
    totals_out,
    totals_in,
    filtered,
    message_out,
    message_in_slots,
    source_rows,
    round_sems,
    local_sems,
    pos_sems,
    feat_sems,
    side_sems,
    stage_sems,
):
    n_dom, n_kb, low_count, norm_scale = sizes
    dom, kb = lax.axis_index("dom"), lax.axis_index("kb")
    rank = dom * n_kb + kb
    slab_count = n_dom * n_kb
    channels, own = feat.shape
    slots = nbr.shape[0]
    width = kfilter.shape[1]
    members = n_dom // low_count
    pair = 2 if n_kb % 2 == 0 else 1
    pairs = n_kb // pair
    high, low = lax.div(dom, low_count), lax.rem(dom, low_count)
    peers = n_kb * low_count
    chunk = width // members

    def slot_between(target, source):
        return 1 + source - jnp.where(source > target, 1, 0)

    def member(number):
        return {"dom": number * low_count + low, "kb": kb}

    def peer(slot, sign=1):
        core, across, side = slot % pair, slot // pair % pairs, slot // n_kb
        place = lax.rem(lax.div(kb, pair) + sign * across + pairs, pairs)
        return {
            "dom": high * low_count + lax.rem(low + side, low_count),
            "kb": place * pair + lax.rem(lax.rem(kb, pair) + core, pair),
        }

    others = list(range(1, peers))

    def slab(steps):
        number = lax.rem(rank + steps + slab_count, slab_count)
        return {"dom": lax.div(number, n_kb), "kb": lax.rem(number, n_kb)}

    def remote(source, target, send_sem, recv_sem, device):
        return pltpu.make_async_remote_copy(
            src_ref=source,
            dst_ref=target,
            send_sem=send_sem,
            recv_sem=recv_sem,
            device_id=device,
            device_id_type=MESH,
        )

    def wait_bytes(ref, sem):
        pltpu.make_async_copy(ref, ref, sem).wait()

    barrier = pltpu.get_barrier_semaphore()
    targets = [
        jnp.where(high == 0, members - 1 - index, index + jnp.where(index >= high, 1, 0))
        for index in range(members - 1)
    ]
    greeted = [peer(slot) for slot in range(peers - 1, 0, -1)]
    beside = [(-1, high > 0), (1, high < members - 1)]
    beside_count = sum(jnp.where(there, 1, 0) for steps, there in beside)

    def tell_beside(sem):
        for steps, there in beside:

            @pl.when(there)
            def _(steps=steps):
                pl.semaphore_signal(
                    sem, inc=1, device_id=member(high + steps), device_id_type=MESH
                )

    tell_beside(barrier)
    for device in greeted:
        pl.semaphore_signal(barrier, inc=1, device_id=device, device_id_type=MESH)
    is_last = rank == slab_count - 1

    @pl.when(rank == 0)
    def _():
        pl.semaphore_signal(barrier, inc=1, device_id=slab(-1), device_id_type=MESH)

    start = pl.multiple_of(kb * (width * low_count) + low * width, math.gcd(width, 128))
    filter_start = pl.multiple_of(low * width, math.gcd(width, 128))
    staged = [
        (feat_hbm, feat),
        (ewald_weight_hbm, ewald_weight),
        (pos_hbm, pos),
        (lat_hbm.at[:, pl.ds(start, width)], lat),
        (kfilter_hbm.at[:, pl.ds(filter_start, width)], kfilter),
        (node_weight_hbm, node_weight),
        (node_bias_hbm, node_bias),
        (message_weight_hbm, message_weight),
        (nbr_hbm, nbr),
        (radial_weight_hbm, radial_weight),
        (vec_hbm, vec),
    ]
    local = [
        pltpu.make_async_copy(source, target, local_sems.at[i])
        for i, (source, target) in enumerate(staged)
    ]
    for copy in local:
        copy.start()

    local[0].wait()
    local[1].wait()
    own_projected[...] = over_first(ewald_weight[...], feat[...]).astype(bf16)
    pl.semaphore_wait(barrier, len(greeted) + beside_count + jnp.where(is_last, 1, 0))
    pos_copies = [
        remote(pos_hbm, group_pos.at[slot], pos_sems.at[0], pos_sems.at[1 + slot // pair], peer(slot))
        for slot in others
    ]
    feat_copies = [
        remote(
            own_projected,
            group_feat.at[slot],
            feat_sems.at[0],
            feat_sems.at[1 + slot // pair],
            peer(slot),
        )
        for slot in others
    ]
    for copy in pos_copies + feat_copies[::-1]:
        copy.start()
    rounds = members - 1
    tell_beside(round_sems.at[0])

    def pass_round(number):
        pl.semaphore_wait(round_sems.at[number], beside_count)
        if number + 1 < rounds:
            tell_beside(round_sems.at[number + 1])

    around = [(0, 1, is_last), (1, -1, rank == 0)]
    inside = [
        (side, steps, lax.div(rank + steps + peers, peers) == high + 1)
        for side, steps in ((0, 1), (1, -1))
    ]
    across = [
        (side, steps, jnp.logical_not(jnp.logical_or(ends, within)))
        for (side, steps, ends), (_, _, within) in zip(around, inside)
    ]

    def send_sides(cases):
        for side, steps, chosen in cases:

            @pl.when(chosen)
            def _(side=side, steps=steps):
                send_side(side, steps)


    def send_side(side, steps):
        device = slab(steps)
        for copy in (
            remote(feat_hbm, side_rows.at[side, 0], side_sems.at[0], side_sems.at[3], device),
            remote(
                vec_hbm,
                side_rows.at[side, pl.ds(1, 3)],
                side_sems.at[0],
                side_sems.at[3],
                device,
            ),
            remote(pos_hbm, side_pos.at[side], side_sems.at[1], side_sems.at[4], device),
            remote(halo_hbm, side_halo.at[side], side_sems.at[2], side_sems.at[5], device),
        ):
            copy.start()

    send_sides(around[:1])
    local[2].wait()
    local[3].wait()
    lattice = lat[...].astype(f32)
    lattice_high = jnp.floor(lattice[2:3] * 0.0625) * 16.0
    lattice_low = lattice[2:3] - lattice_high
    lattice_parts = jnp.concatenate(
        [lattice[0:1]] * 3
        + [lattice[1:2]] * 3
        + [lattice_high] * 3
        + [lattice_low] * 3
        + [jnp.zeros((4, width), f32)],
        axis=0,
    ).astype(bf16)

    def position_parts(coords):
        rows = []
        for axis in (0, 1, 2, 2):
            rows += list(three_parts(coords[axis : axis + 1]))
        rows.append(jnp.zeros((4, coords.shape[1]), f32))
        return jnp.concatenate(rows, axis=0).astype(bf16)

    def make_tables(first, coords):
        turns = over_first(lattice_parts, position_parts(coords))
        cosine, sine = turn_tables(turns)
        columns = slice(first * own, first * own + coords.shape[1])
        for number in range(members):
            rows = slice(number * chunk, (number + 1) * chunk)
            tables[2 * number * chunk : (2 * number + 1) * chunk, columns] = cosine[rows]
            tables[(2 * number + 1) * chunk : 2 * (number + 1) * chunk, columns] = sine[rows]

    def totals_of(first, features):
        return lax.dot_general(
            features,
            tables[:, first * own : first * own + features.shape[1]],
            (((1,), (1,)), ((), ())),
            preferred_element_type=f32,
        )

    make_tables(0, pos[...])
    def batch_features(first, count):
        return jnp.concatenate(
            [own_projected[...] if slot == 0 else group_feat[slot] for slot in range(first, first + count)],
            axis=1,
        )

    def wait_features(first, count):
        for slot in range(first - first % pair, first + count, pair):
            begin = max(slot, 1)
            if slot + pair > begin:
                wait_bytes(
                    group_feat.at[pl.ds(begin, slot + pair - begin)], feat_sems.at[1 + slot // pair]
                )

    for slot in range(1, pair):
        wait_bytes(group_pos.at[slot], pos_sems.at[1])
        make_tables(slot, group_pos[slot])
    wait_features(0, pair)
    near_totals[...] = totals_of(0, batch_features(0, pair))
    pass_round(0)
    send_sides(across)
    for first in range(pair, peers, pair):
        wait_bytes(group_pos.at[pl.ds(first, pair)], pos_sems.at[1 + first // pair])
        make_tables(
            first,
            jnp.concatenate([group_pos[slot] for slot in range(first, first + pair)], axis=1),
        )
    wait_features(pair, peers - pair)
    totals = near_totals[...] + totals_of(pair, batch_features(pair, peers - pair))
    for number in range(members):
        totals_out[number] = totals[:, 2 * number * chunk : 2 * (number + 1) * chunk].astype(bf16)
    for number in range(1, rounds - 1):
        pass_round(number)
    for number in targets:
        remote(
            totals_out.at[number],
            totals_in.at[slot_between(number, high)],
            stage_sems.at[0],
            stage_sems.at[1],
            member(number),
        ).start()
    send_sides(inside)
    if rounds > 1:
        pass_round(rounds - 1)
    send_sides(around[1:])

    local[4].wait()
    own_filter = jnp.zeros((channels, chunk), f32)
    for number in range(members):
        part = kfilter[:, number * chunk : (number + 1) * chunk]
        own_filter = jnp.where(high == number, part, own_filter)
    own_filter = jnp.concatenate([own_filter, own_filter], axis=1) * norm_scale
    for copy in local[5:]:
        copy.wait()
    bias = jnp.broadcast_to(node_bias[...], (own, channels)).T

    def fill_sources(index, one_feat, one_vec):
        columns = slice(index * own, (index + 1) * own)
        value = over_first(node_weight[...], one_feat[...]) + bias
        hidden = (value / (1.0 + jnp.exp(-value))).astype(bf16)
        source_rows[: 3 * channels, columns] = over_first(message_weight[...], hidden).astype(bf16)
        source_rows[3 * channels :, columns] = one_vec[...].reshape(3 * channels, own)

    fill_sources(0, feat, vec)
    wait_bytes(totals_in.at[pl.ds(1, members - 1)], stage_sems.at[1])
    total = totals_out[high].astype(f32)
    for slot in range(1, members):
        total = total + totals_in[slot].astype(f32)
    filtered[high] = (own_filter * total).astype(bf16)
    for number in targets:
        remote(
            filtered.at[high],
            filtered.at[high],
            stage_sems.at[4],
            stage_sems.at[5],
            member(number),
        ).start()

    wait_bytes(side_rows, side_sems.at[3])
    wait_bytes(side_pos, side_sems.at[4])
    wait_bytes(side_halo, side_sems.at[5])
    for side in range(2):
        fill_sources(1 + side, side_rows.at[side, 0], side_rows.at[side, pl.ds(1, 3)])
    ids = nbr[...]
    reach = side_halo.shape[2]

    def picked(row, index):
        return jnp.take_along_axis(
            jnp.broadcast_to(row, (slots, row.shape[1])), index, axis=1, mode="promise_in_bounds"
        )

    below_slot = jnp.clip(ids - own, 0, reach - 1)
    above_slot = jnp.clip(ids - (own + reach), 0, reach - 1)
    own_atom = jnp.clip(ids, 0, own - 1)
    below_atom = picked(side_halo[0, 0:1], below_slot)
    above_atom = picked(side_halo[1, 1:2], above_slot)
    is_own = ids < own
    is_below = ids < own + reach
    used = ids < own + 2 * reach
    atoms = jnp.where(
        is_own,
        ids,
        jnp.where(is_below, below_atom + own, jnp.where(used, above_atom + 2 * own, 3 * own)),
    )
    cartesian = []
    for axis in range(3):
        taken = jnp.where(
            is_own,
            picked(pos[axis : axis + 1], own_atom),
            jnp.where(
                is_below,
                picked(side_pos[0, axis : axis + 1], below_atom),
                picked(side_pos[1, axis : axis + 1], above_atom),
            ),
        )
        taken = jnp.where(used, taken, 0.0)
        offset = taken - pos[axis : axis + 1]
        offset = offset - jnp.floor(offset + 0.5)
        cartesian.append(offset * (side_length if axis < 2 else slab_depth * slab_count))
    distance = jnp.sqrt(
        cartesian[0] * cartesian[0] + cartesian[1] * cartesian[1] + cartesian[2] * cartesian[2]
    )
    limit = jnp.maximum(distance, distance_floor)
    direction = [part / limit for part in cartesian]

    radial_count = radial_weight.shape[0]
    spread = 1.5 * radial_reach / radial_count
    centers = lax.broadcasted_iota(jnp.int32, (radial_count, own), 0).astype(f32) * (
        radial_reach / (radial_count - 1)
    )
    numbers = lax.broadcasted_iota(jnp.int32, (3 * own, own), 0)

    def edges(j, sums):
        row = slice(j, j + 1)
        chosen = jnp.where(numbers == atoms[row], 1.0, 0.0).astype(bf16)
        gathered = jnp.dot(source_rows[...], chosen, preferred_element_type=f32)
        scaled = (distance[row] - centers) * (1.0 / spread)
        radial = jnp.exp(-(scaled * scaled)).astype(bf16)
        terms = gathered[: 3 * channels] * over_first(radial_weight[...], radial)
        first = terms[:channels]
        second = terms[channels : 2 * channels]
        third = terms[2 * channels :]
        new = [sums[0] + first]
        for axis in range(3):
            begin = (3 + axis) * channels
            new.append(
                sums[1 + axis]
                + gathered[begin : begin + channels] * second
                + third * direction[axis][row]
            )
        return new

    wait_bytes(filtered.at[pl.ds(1, members - 1)], stage_sems.at[5])
    spectrum = jnp.concatenate([filtered[number] for number in range(members)], axis=1)
    def messages_of(first, last):
        return jnp.dot(
            spectrum, tables[:, first * own : last * own], preferred_element_type=f32
        )

    def send_message(slot, value):
        message_out[slot] = value.astype(bf16)
        remote(
            message_out.at[slot],
            message_in_slots.at[slot],
            stage_sems.at[2],
            stage_sems.at[3],
            peer(slot, -1),
        ).start()

    group = pair * (2 if peers % (2 * pair) == 0 else 1)
    for first in range(peers - group, -1, -group):
        values = messages_of(first, first + group)
        for slot in range(first + group - 1, first - 1, -1):
            value = values[:, (slot - first) * own : (slot - first + 1) * own]
            if slot > 0:
                send_message(slot, value)
            else:
                result = value
    sums = [jnp.zeros((channels, own), f32)] * 4
    half = slots // 2
    for j in range(half):
        sums = edges(j, sums)

    for j in range(half, slots):
        sums = edges(j, sums)
    for axis in range(3):
        out_all[1 + axis] = (vec[axis].astype(f32) + sums[1 + axis]).astype(bf16)
    result = result + feat[...].astype(f32) + sums[0]

    wait_bytes(message_in_slots.at[pl.ds(1, peers - 1)], stage_sems.at[3])
    for d in range(1, peers):
        result = result + message_in_slots[d].astype(f32)
    out_all[0] = result.astype(bf16)
    wait_bytes(group_pos.at[pl.ds(1, peers - 1)], pos_sems.at[0])
    wait_bytes(group_feat.at[pl.ds(1, peers - 1)], feat_sems.at[0])
    wait_bytes(side_rows, side_sems.at[0])
    wait_bytes(side_pos, side_sems.at[1])
    wait_bytes(side_halo, side_sems.at[2])
    wait_bytes(totals_in.at[pl.ds(1, members - 1)], stage_sems.at[0])
    wait_bytes(filtered.at[pl.ds(1, members - 1)], stage_sems.at[4])
    wait_bytes(message_in_slots.at[pl.ds(1, peers - 1)], stage_sems.at[2])


def split_kernel(both, out_feat, out_vec, sems):
    feat_copy = pltpu.make_async_copy(both.at[0], out_feat, sems.at[0])
    vec_copy = pltpu.make_async_copy(both.at[pl.ds(1, 3)], out_vec, sems.at[1])
    feat_copy.start()
    vec_copy.start()
    feat_copy.wait()
    vec_copy.wait()


def shards(
    features,
    vectors,
    positions,
    neighbours,
    halo_lists,
    lattice,
    kspace_filter,
    node_weight,
    node_bias,
    message_weight,
    radial_weight,
    ewald_weight,
):
    n_dom, n_kb = lax.axis_size("dom"), lax.axis_size("kb")
    channels, own = features.shape
    reach = halo_lists.shape[1]
    width = kspace_filter.shape[1]
    low_count = 2 if n_dom % 2 == 0 else 1
    members, peers = n_dom // low_count, n_kb * low_count
    width = width // low_count
    chunk = width // members
    pair = 2 if n_kb % 2 == 0 else 1
    norm_scale = 1.0 / math.sqrt(lattice.shape[1] * own * n_dom * n_kb)
    vmem = pl.BlockSpec(memory_space=pltpu.VMEM)
    hbm = pl.BlockSpec(memory_space=pltpu.HBM)
    dma = pltpu.SemaphoreType.DMA
    bias_row = node_bias[None, :]

    def like(array):
        return pltpu.VMEM(array.shape, array.dtype)

    both = pl.pallas_call(
        functools.partial(kernel, (n_dom, n_kb, low_count, norm_scale)),
        out_shape=pltpu.VMEM((4, channels, own), bf16),
        in_specs=[hbm] * 12,
        out_specs=vmem,
        scratch_shapes=[
            like(features),
            like(vectors),
            like(positions),
            like(neighbours),
            pltpu.VMEM((3, width), jnp.int32),
            pltpu.VMEM((channels, width), f32),
            like(node_weight),
            like(bias_row),
            like(message_weight),
            like(radial_weight),
            like(ewald_weight),
            like(features),
            pltpu.VMEM((peers, channels, own), bf16),
            pltpu.VMEM((peers, 3, own), f32),
            pltpu.VMEM((2, 4, channels, own), bf16),
            pltpu.VMEM((2, 3, own), f32),
            pltpu.VMEM((2, 2, reach), jnp.int32),
            pltpu.VMEM((2 * width, peers * own), bf16),
            pltpu.VMEM((channels, 2 * width), f32),
            pltpu.VMEM((members, channels, 2 * chunk), bf16),
            pltpu.VMEM((members, channels, 2 * chunk), bf16),
            pltpu.VMEM((members, channels, 2 * chunk), bf16),
            pltpu.VMEM((peers, channels, own), bf16),
            pltpu.VMEM((peers, channels, own), bf16),
            pltpu.VMEM((6 * channels, 3 * own), bf16),
            pltpu.SemaphoreType.REGULAR((members - 1,)),
            dma((11,)),
            dma((1 + peers // pair,)),
            dma((1 + peers // pair,)),
            dma((6,)),
            dma((6,)),
        ],
        compiler_params=pltpu.CompilerParams(collective_id=0, has_side_effects=True),
    )(
        features,
        vectors,
        positions,
        neighbours,
        halo_lists,
        lattice,
        kspace_filter,
        node_weight,
        bias_row,
        message_weight,
        radial_weight,
        ewald_weight,
    )
    return pl.pallas_call(
        split_kernel,
        out_shape=(
            jax.ShapeDtypeStruct(features.shape, bf16),
            jax.ShapeDtypeStruct(vectors.shape, bf16),
        ),
        in_specs=[vmem],
        out_specs=(pl.BlockSpec(memory_space=pl.ANY),) * 2,
        scratch_shapes=[dma((2,))],
    )(pltpu.with_memory_space_constraint(both, pltpu.VMEM))


def solution(mesh):
    atoms = P(None, ("dom", "kb"))
    placed = (
        atoms,
        P(None, None, ("dom", "kb")),
        atoms,
        atoms,
        atoms,
        P(),
        P(None, "kb"),
        P(),
        P(),
        P(),
        P(),
        P(),
    )
    return jax.shard_map(
        shards,
        mesh=mesh,
        in_specs=placed,
        out_specs=(atoms, P(None, None, ("dom", "kb"))),
        check_vma=False,
    )
```

```python
import functools
import math

import jax
import jax.numpy as jnp
import numpy as np
from jax import lax
from jax.experimental import pallas as pl
from jax.experimental.pallas import tpu as pltpu
from jax.sharding import PartitionSpec as P

side_length = 6.0
slab_depth = 6.0
radial_reach = 6.0
distance_floor = 1.0
MESH = pl.DeviceIdType.MESH
f32 = jnp.float32
bf16 = jnp.bfloat16


def polynomial(function, degree):
    nodes = (np.cos((np.arange(degree + 1) + 0.5) * np.pi / (degree + 1)) + 1.0) / 2.0
    fitted = np.polynomial.polynomial.polyfit(nodes, function(nodes / 4.0), degree)
    return [float(value * 4.0**power) for power, value in enumerate(fitted)]


half_cos = polynomial(lambda w: np.sqrt(2.0) * np.cos(np.pi * np.sqrt(w)), 3)
half_sin = polynomial(lambda w: np.sqrt(2.0) * np.sin(np.pi * np.sqrt(w)) / np.sqrt(w), 3)


def evaluate(terms, w):
    value = terms[-1] * w + terms[-2]
    for term in terms[-3::-1]:
        value = value * w + term
    return value


def turn_tables(turns):
    part = turns - jnp.round(turns)
    w = part * part
    sine = part * evaluate(half_sin, w)
    cosine = evaluate(half_cos, w)
    return (1.0 - sine * sine).astype(bf16), (sine * cosine).astype(bf16)


def over_first(first_operand, second_operand):
    return lax.dot_general(
        first_operand, second_operand, (((0,), (0,)), ((), ())), preferred_element_type=f32
    )


def three_parts(value):
    high = value.astype(bf16)
    rest = value - high.astype(f32)
    middle = rest.astype(bf16)
    low = (rest - middle.astype(f32)).astype(bf16)
    return high.astype(f32), middle.astype(f32), low.astype(f32)


def kernel(
    sizes,
    feat_hbm,
    vec_hbm,
    pos_hbm,
    nbr_hbm,
    halo_hbm,
    lat_hbm,
    kfilter_hbm,
    node_weight_hbm,
    node_bias_hbm,
    message_weight_hbm,
    radial_weight_hbm,
    ewald_weight_hbm,
    out_all,
    feat,
    vec,
    pos,
    nbr,
    lat,
    kfilter,
    node_weight,
    node_bias,
    message_weight,
    radial_weight,
    ewald_weight,
    own_projected,
    group_feat,
    group_pos,
    side_rows,
    side_pos,
    side_halo,
    tables,
    near_totals,
    totals_out,
    totals_in,
    filtered,
    message_out,
    message_in_slots,
    source_rows,
    side_total,
    sent_total,
    stage_total,
    round_sems,
    local_sems,
    pos_sems,
    feat_sems,
    side_sem,
    stage_sems,
    send_sem,
):
    n_dom, n_kb, low_count, norm_scale = sizes
    dom, kb = lax.axis_index("dom"), lax.axis_index("kb")
    rank = dom * n_kb + kb
    slab_count = n_dom * n_kb
    channels, own = feat.shape
    slots = nbr.shape[0]
    width = kfilter.shape[1]
    members = n_dom // low_count
    pair = 2 if n_kb % 2 == 0 else 1
    pairs = n_kb // pair
    high, low = lax.div(dom, low_count), lax.rem(dom, low_count)
    peers = n_kb * low_count
    chunk = width // members

    def slot_between(target, source):
        return 1 + source - jnp.where(source > target, 1, 0)

    def member(number):
        return {"dom": number * low_count + low, "kb": kb}

    def peer(slot, sign=1):
        core, across, side = slot % pair, slot // pair % pairs, slot // n_kb
        place = lax.rem(lax.div(kb, pair) + sign * across + pairs, pairs)
        return {
            "dom": high * low_count + lax.rem(low + side, low_count),
            "kb": place * pair + lax.rem(lax.rem(kb, pair) + core, pair),
        }

    others = list(range(1, peers))

    def slab(steps):
        number = lax.rem(rank + steps + slab_count, slab_count)
        return {"dom": lax.div(number, n_kb), "kb": lax.rem(number, n_kb)}

    def remote(source, target, send_sem, recv_sem, device):
        return pltpu.make_async_remote_copy(
            src_ref=source,
            dst_ref=target,
            send_sem=send_sem,
            recv_sem=recv_sem,
            device_id=device,
            device_id_type=MESH,
        )

    def wait_bytes(ref, sem):
        pltpu.make_async_copy(ref, ref, sem).wait()

    barrier = pltpu.get_barrier_semaphore()
    targets = [
        jnp.where(high == 0, members - 1 - index, index + jnp.where(index >= high, 1, 0))
        for index in range(members - 1)
    ]
    greeted = [peer(slot) for slot in range(peers - 1, 0, -1)]
    beside = [(-1, high > 0), (1, high < members - 1)]
    beside_count = sum(jnp.where(there, 1, 0) for steps, there in beside)

    def tell_beside(sem):
        for steps, there in beside:

            @pl.when(there)
            def _(steps=steps):
                pl.semaphore_signal(
                    sem, inc=1, device_id=member(high + steps), device_id_type=MESH
                )

    for device in greeted:
        pl.semaphore_signal(barrier, inc=1, device_id=device, device_id_type=MESH)
    tell_beside(barrier)
    is_last = rank == slab_count - 1

    @pl.when(rank == 0)
    def _():
        pl.semaphore_signal(barrier, inc=1, device_id=slab(-1), device_id_type=MESH)

    start = pl.multiple_of(kb * (width * low_count) + low * width, math.gcd(width, 128))
    filter_start = pl.multiple_of(low * width, math.gcd(width, 128))
    staged = [
        (feat_hbm, feat),
        (ewald_weight_hbm, ewald_weight),
        (pos_hbm, pos),
        (lat_hbm.at[:, pl.ds(start, width)], lat),
        (kfilter_hbm.at[:, pl.ds(filter_start, width)], kfilter),
        (node_weight_hbm, node_weight),
        (node_bias_hbm, node_bias),
        (message_weight_hbm, message_weight),
        (nbr_hbm, nbr),
        (radial_weight_hbm, radial_weight),
        (vec_hbm, vec),
    ]
    local = [
        pltpu.make_async_copy(source, target, local_sems.at[0 if i < 4 else 1])
        for i, (source, target) in enumerate(staged)
    ]
    for copy in local:
        copy.start()

    for copy in local[:4]:
        copy.wait()
    own_projected[...] = over_first(ewald_weight[...], feat[...]).astype(bf16)
    pl.semaphore_wait(barrier, len(greeted) + beside_count + jnp.where(is_last, 1, 0))
    pos_copies = [
        remote(pos, group_pos.at[slot], send_sem.at[0], pos_sems.at[slot // pair], peer(slot))
        for slot in others
    ]
    feat_copies = [
        remote(
            own_projected,
            group_feat.at[slot],
            send_sem.at[0],
            feat_sems.at[0 if slot < pair else 1],
            peer(slot),
        )
        for slot in others
    ]
    for copy in pos_copies[::-1] + feat_copies[::-1]:
        copy.start()
    rounds = members - 1
    tell_beside(round_sems.at[0])

    def pass_round(number):
        pl.semaphore_wait(round_sems.at[number], beside_count)
        if number + 1 < rounds:
            tell_beside(round_sems.at[number + 1])

    around = [(0, 1, is_last), (1, -1, rank == 0)]
    inside = [
        (side, steps, lax.div(rank + steps + peers, peers) == high + 1)
        for side, steps in ((0, 1), (1, -1))
    ]
    across = [
        (side, steps, jnp.logical_not(jnp.logical_or(ends, within)))
        for (side, steps, ends), (_, _, within) in zip(around, inside)
    ]

    def send_sides(cases):
        for side, steps, chosen in cases:

            @pl.when(chosen)
            def _(side=side, steps=steps):
                send_side(side, steps)


    def send_side(side, steps):
        device = slab(steps)
        for copy in (
            remote(feat_hbm, side_rows.at[side, 0], send_sem.at[0], side_sem.at[0], device),
            remote(
                vec_hbm,
                side_rows.at[side, pl.ds(1, 3)],
                send_sem.at[0],
                side_sem.at[0],
                device,
            ),
            remote(pos_hbm, side_pos.at[side], send_sem.at[0], side_sem.at[0], device),
            remote(halo_hbm, side_halo.at[side], send_sem.at[0], side_sem.at[0], device),
        ):
            copy.start()

    send_sides(around[:1])
    lattice = lat[...].astype(f32)
    lattice_high = jnp.floor(lattice[2:3] * 0.0625) * 16.0
    lattice_low = lattice[2:3] - lattice_high
    lattice_parts = jnp.concatenate(
        [lattice[0:1]] * 3
        + [lattice[1:2]] * 3
        + [lattice_high] * 3
        + [lattice_low] * 3
        + [jnp.zeros((4, width), f32)],
        axis=0,
    ).astype(bf16)

    def position_parts(coords):
        rows = []
        for axis in (0, 1, 2, 2):
            rows += list(three_parts(coords[axis : axis + 1]))
        rows.append(jnp.zeros((4, coords.shape[1]), f32))
        return jnp.concatenate(rows, axis=0).astype(bf16)

    def make_tables(first, coords):
        turns = over_first(lattice_parts, position_parts(coords))
        cosine, sine = turn_tables(turns)
        columns = slice(first * own, first * own + coords.shape[1])
        for number in range(members):
            rows = slice(number * chunk, (number + 1) * chunk)
            tables[2 * number * chunk : (2 * number + 1) * chunk, columns] = cosine[rows]
            tables[(2 * number + 1) * chunk : 2 * (number + 1) * chunk, columns] = sine[rows]

    def totals_of(first, features):
        return lax.dot_general(
            features,
            tables[:, first * own : first * own + features.shape[1]],
            (((1,), (1,)), ((), ())),
            preferred_element_type=f32,
        )

    make_tables(0, pos[...])
    def batch_features(first, count):
        return jnp.concatenate(
            [own_projected[...] if slot == 0 else group_feat[slot] for slot in range(first, first + count)],
            axis=1,
        )

    def wait_features(first, count):
        begin = max(first, 1)
        wait_bytes(
            group_feat.at[pl.ds(begin, first + count - begin)], feat_sems.at[0 if first < pair else 1]
        )

    for slot in range(1, pair):
        wait_bytes(group_pos.at[slot], pos_sems.at[0])
        make_tables(slot, group_pos[slot])
    if pair > 1:
        wait_features(0, pair)
    near_totals[...] = totals_of(0, batch_features(0, pair))
    pass_round(0)
    send_sides(across)
    for first in range(pair, peers, pair):
        wait_bytes(group_pos.at[pl.ds(first, pair)], pos_sems.at[first // pair])
        make_tables(
            first,
            jnp.concatenate([group_pos[slot] for slot in range(first, first + pair)], axis=1),
        )
    wait_features(pair, peers - pair)
    totals = near_totals[...] + totals_of(pair, batch_features(pair, peers - pair))
    for number in range(members):
        totals_out[number] = totals[:, 2 * number * chunk : 2 * (number + 1) * chunk].astype(bf16)
    for number in range(1, rounds - 1):
        pass_round(number)
    for index in range(members - 1):
        number = jnp.where(index < high, high - 1 - index, index + 1)
        remote(
            totals_out.at[number],
            totals_in.at[slot_between(number, high)],
            send_sem.at[1],
            stage_sems.at[0],
            member(number),
        ).start()
    send_sides(inside)
    if rounds > 1:
        pass_round(rounds - 1)
    send_sides(around[1:])

    for copy in local[4:]:
        copy.wait()
    own_filter = jnp.zeros((channels, chunk), f32)
    for number in range(members):
        part = kfilter[:, number * chunk : (number + 1) * chunk]
        own_filter = jnp.where(high == number, part, own_filter)
    own_filter = jnp.concatenate([own_filter, own_filter], axis=1) * norm_scale
    bias = jnp.broadcast_to(node_bias[...], (own, channels)).T

    def fill_sources(index, one_feat, one_vec):
        columns = slice(index * own, (index + 1) * own)
        value = over_first(node_weight[...], one_feat[...]) + bias
        hidden = (value / (1.0 + jnp.exp(-value))).astype(bf16)
        source_rows[: 3 * channels, columns] = over_first(message_weight[...], hidden).astype(bf16)
        source_rows[3 * channels :, columns] = one_vec[...].reshape(3 * channels, own)

    fill_sources(0, feat, vec)
    wait_bytes(totals_in.at[pl.ds(1, members - 1)], stage_sems.at[0])
    total = totals_out[high].astype(f32)
    for slot in range(1, members):
        total = total + totals_in[slot].astype(f32)
    filtered[high] = (own_filter * total).astype(bf16)
    for number in targets:
        remote(
            filtered.at[high],
            filtered.at[high],
            send_sem.at[1],
            stage_sems.at[1],
            member(number),
        ).start()

    wait_bytes(side_total, side_sem.at[0])
    for side in range(2):
        fill_sources(1 + side, side_rows.at[side, 0], side_rows.at[side, pl.ds(1, 3)])
    ids = nbr[...]
    reach = side_halo.shape[2]

    def picked(row, index):
        return jnp.take_along_axis(
            jnp.broadcast_to(row, (slots, row.shape[1])), index, axis=1, mode="promise_in_bounds"
        )

    below_slot = jnp.clip(ids - own, 0, reach - 1)
    above_slot = jnp.clip(ids - (own + reach), 0, reach - 1)
    own_atom = jnp.clip(ids, 0, own - 1)
    below_atom = picked(side_halo[0, 0:1], below_slot)
    above_atom = picked(side_halo[1, 1:2], above_slot)
    is_own = ids < own
    is_below = ids < own + reach
    used = ids < own + 2 * reach
    atoms = jnp.where(
        is_own,
        ids,
        jnp.where(is_below, below_atom + own, jnp.where(used, above_atom + 2 * own, 3 * own)),
    )
    cartesian = []
    for axis in range(3):
        taken = jnp.where(
            is_own,
            picked(pos[axis : axis + 1], own_atom),
            jnp.where(
                is_below,
                picked(side_pos[0, axis : axis + 1], below_atom),
                picked(side_pos[1, axis : axis + 1], above_atom),
            ),
        )
        taken = jnp.where(used, taken, 0.0)
        offset = taken - pos[axis : axis + 1]
        offset = offset - jnp.floor(offset + 0.5)
        cartesian.append(offset * (side_length if axis < 2 else slab_depth * slab_count))
    distance = jnp.sqrt(
        cartesian[0] * cartesian[0] + cartesian[1] * cartesian[1] + cartesian[2] * cartesian[2]
    )
    limit = jnp.maximum(distance, distance_floor)
    direction = [part / limit for part in cartesian]

    radial_count = radial_weight.shape[0]
    spread = 1.5 * radial_reach / radial_count
    centers = lax.broadcasted_iota(jnp.int32, (radial_count, own), 0).astype(f32) * (
        radial_reach / (radial_count - 1)
    )
    numbers = lax.broadcasted_iota(jnp.int32, (3 * own, own), 0)

    def edges(j, sums):
        row = slice(j, j + 1)
        chosen = jnp.where(numbers == atoms[row], 1.0, 0.0).astype(bf16)
        gathered = jnp.dot(source_rows[...], chosen, preferred_element_type=f32)
        scaled = (distance[row] - centers) * (1.0 / spread)
        radial = jnp.exp(-(scaled * scaled)).astype(bf16)
        terms = gathered[: 3 * channels] * over_first(radial_weight[...], radial)
        first = terms[:channels]
        second = terms[channels : 2 * channels]
        third = terms[2 * channels :]
        new = [sums[0] + first]
        for axis in range(3):
            begin = (3 + axis) * channels
            new.append(
                sums[1 + axis]
                + gathered[begin : begin + channels] * second
                + third * direction[axis][row]
            )
        return new

    wait_bytes(filtered.at[pl.ds(1, members - 1)], stage_sems.at[1])
    spectrum = jnp.concatenate([filtered[number] for number in range(members)], axis=1)
    def messages_of(first, last):
        return jnp.dot(
            spectrum, tables[:, first * own : last * own], preferred_element_type=f32
        )

    def send_message(slot, value):
        message_out[slot] = value.astype(bf16)
        remote(
            message_out.at[slot],
            message_in_slots.at[slot],
            send_sem.at[0],
            stage_sems.at[2],
            peer(slot, -1),
        ).start()

    group = pair * (2 if peers % (2 * pair) == 0 else 1)
    for first in range(peers - group, -1, -group):
        values = messages_of(first, first + group)
        for slot in range(first + group - 1, first - 1, -1):
            value = values[:, (slot - first) * own : (slot - first + 1) * own]
            if slot > 0:
                send_message(slot, value)
            else:
                result = value
    sums = [jnp.zeros((channels, own), f32)] * 4
    half = slots // 2
    for j in range(half):
        sums = edges(j, sums)

    for j in range(half, slots):
        sums = edges(j, sums)
    for axis in range(3):
        out_all[1 + axis] = (vec[axis].astype(f32) + sums[1 + axis]).astype(bf16)
    result = result + feat[...].astype(f32) + sums[0]

    wait_bytes(message_in_slots.at[pl.ds(1, peers - 1)], stage_sems.at[2])
    for d in range(1, peers):
        result = result + message_in_slots[d].astype(f32)
    out_all[0] = result.astype(bf16)
    wait_bytes(sent_total, send_sem.at[0])
    wait_bytes(stage_total, send_sem.at[1])


def split_kernel(both, out_feat, out_vec, sems):
    feat_copy = pltpu.make_async_copy(both.at[0], out_feat, sems.at[0])
    vec_copy = pltpu.make_async_copy(both.at[pl.ds(1, 3)], out_vec, sems.at[0])
    feat_copy.start()
    vec_copy.start()
    feat_copy.wait()
    vec_copy.wait()


def shards(
    features,
    vectors,
    positions,
    neighbours,
    halo_lists,
    lattice,
    kspace_filter,
    node_weight,
    node_bias,
    message_weight,
    radial_weight,
    ewald_weight,
):
    n_dom, n_kb = lax.axis_size("dom"), lax.axis_size("kb")
    channels, own = features.shape
    reach = halo_lists.shape[1]
    width = kspace_filter.shape[1]
    low_count = 2 if n_dom % 2 == 0 else 1
    members, peers = n_dom // low_count, n_kb * low_count
    width = width // low_count
    chunk = width // members
    pair = 2 if n_kb % 2 == 0 else 1
    norm_scale = 1.0 / math.sqrt(lattice.shape[1] * own * n_dom * n_kb)
    row_bytes = 128 * 4
    block_bytes = channels * own * 2
    side_bytes = 2 * (4 * block_bytes + 3 * own * 4 + 2 * reach * 4)
    sent_bytes = side_bytes + (peers - 1) * (3 * own * 4 + 2 * block_bytes)
    vmem = pl.BlockSpec(memory_space=pltpu.VMEM)
    hbm = pl.BlockSpec(memory_space=pltpu.HBM)
    dma = pltpu.SemaphoreType.DMA
    bias_row = node_bias[None, :]

    def like(array):
        return pltpu.VMEM(array.shape, array.dtype)

    both = pl.pallas_call(
        functools.partial(kernel, (n_dom, n_kb, low_count, norm_scale)),
        out_shape=pltpu.VMEM((4, channels, own), bf16),
        in_specs=[hbm] * 12,
        out_specs=vmem,
        scratch_shapes=[
            like(features),
            like(vectors),
            like(positions),
            like(neighbours),
            pltpu.VMEM((3, width), jnp.int32),
            pltpu.VMEM((channels, width), f32),
            like(node_weight),
            like(bias_row),
            like(message_weight),
            like(radial_weight),
            like(ewald_weight),
            like(features),
            pltpu.VMEM((peers, channels, own), bf16),
            pltpu.VMEM((peers, 3, own), f32),
            pltpu.VMEM((2, 4, channels, own), bf16),
            pltpu.VMEM((2, 3, own), f32),
            pltpu.VMEM((2, 2, reach), jnp.int32),
            pltpu.VMEM((2 * width, peers * own), bf16),
            pltpu.VMEM((channels, 2 * width), f32),
            pltpu.VMEM((members, channels, 2 * chunk), bf16),
            pltpu.VMEM((members, channels, 2 * chunk), bf16),
            pltpu.VMEM((members, channels, 2 * chunk), bf16),
            pltpu.VMEM((peers, channels, own), bf16),
            pltpu.VMEM((peers, channels, own), bf16),
            pltpu.VMEM((6 * channels, 3 * own), bf16),
            pltpu.VMEM((side_bytes // row_bytes, 1, 128), f32),
            pltpu.VMEM((sent_bytes // row_bytes, 1, 128), f32),
            pltpu.VMEM((2 * (members - 1), channels, 2 * chunk), bf16),
            pltpu.SemaphoreType.REGULAR((members - 1,)),
            dma((2,)),
            dma((peers // pair,)),
            dma((2,)),
            dma((1,)),
            dma((3,)),
            dma((2,)),
        ],
        compiler_params=pltpu.CompilerParams(collective_id=0, has_side_effects=True),
    )(
        features,
        vectors,
        positions,
        neighbours,
        halo_lists,
        lattice,
        kspace_filter,
        node_weight,
        bias_row,
        message_weight,
        radial_weight,
        ewald_weight,
    )
    return pl.pallas_call(
        split_kernel,
        out_shape=(
            jax.ShapeDtypeStruct(features.shape, bf16),
            jax.ShapeDtypeStruct(vectors.shape, bf16),
        ),
        in_specs=[vmem],
        out_specs=(pl.BlockSpec(memory_space=pl.ANY),) * 2,
        scratch_shapes=[dma((1,))],
    )(pltpu.with_memory_space_constraint(both, pltpu.VMEM))


def solution(mesh):
    atoms = P(None, ("dom", "kb"))
    placed = (
        atoms,
        P(None, None, ("dom", "kb")),
        atoms,
        atoms,
        atoms,
        P(),
        P(None, "kb"),
        P(),
        P(),
        P(),
        P(),
        P(),
    )
    return jax.shard_map(
        shards,
        mesh=mesh,
        in_specs=placed,
        out_specs=(atoms, P(None, None, ("dom", "kb"))),
        check_vma=False,
    )
```

```python
import functools
import math

import jax
import jax.numpy as jnp
import numpy as np
from jax import lax
from jax.experimental import pallas as pl
from jax.experimental.pallas import tpu as pltpu
from jax.sharding import PartitionSpec as P

side_length = 6.0
slab_depth = 6.0
radial_reach = 6.0
distance_floor = 1.0
MESH = pl.DeviceIdType.MESH
f32 = jnp.float32
bf16 = jnp.bfloat16


def polynomial(function, degree):
    nodes = (np.cos((np.arange(degree + 1) + 0.5) * np.pi / (degree + 1)) + 1.0) / 2.0
    fitted = np.polynomial.polynomial.polyfit(nodes, function(nodes / 4.0), degree)
    return [float(value * 4.0**power) for power, value in enumerate(fitted)]


half_cos = polynomial(lambda w: np.sqrt(2.0) * np.cos(np.pi * np.sqrt(w)), 3)
half_sin = polynomial(lambda w: np.sqrt(2.0) * np.sin(np.pi * np.sqrt(w)) / np.sqrt(w), 3)


def evaluate(terms, w):
    value = terms[-1] * w + terms[-2]
    for term in terms[-3::-1]:
        value = value * w + term
    return value


def turn_tables(turns):
    part = turns - jnp.round(turns)
    w = part * part
    sine = part * evaluate(half_sin, w)
    cosine = evaluate(half_cos, w)
    return (1.0 - sine * sine).astype(bf16), (sine * cosine).astype(bf16)


def over_first(first_operand, second_operand):
    return lax.dot_general(
        first_operand, second_operand, (((0,), (0,)), ((), ())), preferred_element_type=f32
    )


def three_parts(value):
    high = value.astype(bf16)
    rest = value - high.astype(f32)
    middle = rest.astype(bf16)
    low = (rest - middle.astype(f32)).astype(bf16)
    return high.astype(f32), middle.astype(f32), low.astype(f32)


def kernel(
    sizes,
    feat_hbm,
    vec_hbm,
    pos_hbm,
    nbr_hbm,
    halo_hbm,
    lat_hbm,
    kfilter_hbm,
    node_weight_hbm,
    node_bias_hbm,
    message_weight_hbm,
    radial_weight_hbm,
    ewald_weight_hbm,
    out_all,
    feat,
    vec,
    pos,
    nbr,
    lat,
    kfilter,
    node_weight,
    node_bias,
    message_weight,
    radial_weight,
    ewald_weight,
    own_projected,
    group_feat,
    group_pos,
    side_rows,
    side_pos,
    side_halo,
    tables,
    near_totals,
    totals_out,
    totals_in,
    totals_all,
    chunk_filters,
    filtered,
    message_out,
    message_in_slots,
    source_rows,
    side_total,
    sent_total,
    stage_total,
    round_sems,
    local_sems,
    pos_sems,
    feat_sems,
    side_sem,
    stage_sems,
    send_sem,
):
    n_dom, n_kb, low_count, norm_scale = sizes
    dom, kb = lax.axis_index("dom"), lax.axis_index("kb")
    rank = dom * n_kb + kb
    slab_count = n_dom * n_kb
    channels, own = feat.shape
    slots = nbr.shape[0]
    width = kfilter.shape[1]
    members = n_dom // low_count
    pair = 2 if n_kb % 2 == 0 else 1
    pairs = n_kb // pair
    high, low = lax.div(dom, low_count), lax.rem(dom, low_count)
    peers = n_kb * low_count
    chunk = width // members

    def slot_between(target, source):
        return 1 + source - jnp.where(source > target, 1, 0)

    def member(number):
        return {"dom": number * low_count + low, "kb": kb}

    def peer(slot, sign=1):
        core, across, side = slot % pair, slot // pair % pairs, slot // n_kb
        place = lax.rem(lax.div(kb, pair) + sign * across + pairs, pairs)
        return {
            "dom": high * low_count + lax.rem(low + side, low_count),
            "kb": place * pair + lax.rem(lax.rem(kb, pair) + core, pair),
        }

    others = list(range(1, peers))

    def slab(steps):
        number = lax.rem(rank + steps + slab_count, slab_count)
        return {"dom": lax.div(number, n_kb), "kb": lax.rem(number, n_kb)}

    def remote(source, target, send_sem, recv_sem, device):
        return pltpu.make_async_remote_copy(
            src_ref=source,
            dst_ref=target,
            send_sem=send_sem,
            recv_sem=recv_sem,
            device_id=device,
            device_id_type=MESH,
        )

    def wait_bytes(ref, sem):
        pltpu.make_async_copy(ref, ref, sem).wait()

    barrier = pltpu.get_barrier_semaphore()
    targets = [
        jnp.where(high == 0, members - 1 - index, index + jnp.where(index >= high, 1, 0))
        for index in range(members - 1)
    ]
    greeted = [peer(slot) for slot in range(peers - 1, 0, -1)]
    beside = [(-1, high > 0), (1, high < members - 1)]
    beside_count = sum(jnp.where(there, 1, 0) for steps, there in beside)

    def tell_beside(sem):
        for steps, there in beside:

            @pl.when(there)
            def _(steps=steps):
                pl.semaphore_signal(
                    sem, inc=1, device_id=member(high + steps), device_id_type=MESH
                )

    for device in greeted:
        pl.semaphore_signal(barrier, inc=1, device_id=device, device_id_type=MESH)
    tell_beside(barrier)
    is_last = rank == slab_count - 1

    @pl.when(rank == 0)
    def _():
        pl.semaphore_signal(barrier, inc=1, device_id=slab(-1), device_id_type=MESH)

    start = pl.multiple_of(kb * (width * low_count) + low * width, math.gcd(width, 128))
    filter_start = pl.multiple_of(low * width, math.gcd(width, 128))
    staged = [
        (feat_hbm, feat),
        (ewald_weight_hbm, ewald_weight),
        (pos_hbm, pos),
        (lat_hbm.at[:, pl.ds(start, width)], lat),
        (kfilter_hbm.at[:, pl.ds(filter_start, width)], kfilter),
        (node_weight_hbm, node_weight),
        (node_bias_hbm, node_bias),
        (message_weight_hbm, message_weight),
        (nbr_hbm, nbr),
        (radial_weight_hbm, radial_weight),
        (vec_hbm, vec),
    ]
    local = [
        pltpu.make_async_copy(source, target, local_sems.at[0 if i < 4 else 1])
        for i, (source, target) in enumerate(staged)
    ]
    for copy in local:
        copy.start()

    for copy in local[:4]:
        copy.wait()
    own_projected[...] = over_first(ewald_weight[...], feat[...]).astype(bf16)
    pl.semaphore_wait(barrier, len(greeted) + beside_count + jnp.where(is_last, 1, 0))
    pos_copies = [
        remote(pos, group_pos.at[slot], send_sem.at[0], pos_sems.at[slot // pair], peer(slot))
        for slot in others
    ]
    feat_copies = [
        remote(
            own_projected,
            group_feat.at[slot],
            send_sem.at[0],
            feat_sems.at[0 if slot < pair else 1],
            peer(slot),
        )
        for slot in others
    ]
    for copy in pos_copies[::-1] + feat_copies[::-1]:
        copy.start()
    rounds = members - 1
    tell_beside(round_sems.at[0])

    def pass_round(number):
        pl.semaphore_wait(round_sems.at[number], beside_count)
        if number + 1 < rounds:
            tell_beside(round_sems.at[number + 1])

    around = [(0, 1, is_last), (1, -1, rank == 0)]
    inside = [
        (side, steps, lax.div(rank + steps + peers, peers) == high + 1)
        for side, steps in ((0, 1), (1, -1))
    ]
    across = [
        (side, steps, jnp.logical_not(jnp.logical_or(ends, within)))
        for (side, steps, ends), (_, _, within) in zip(around, inside)
    ]

    def send_sides(cases):
        for side, steps, chosen in cases:

            @pl.when(chosen)
            def _(side=side, steps=steps):
                send_side(side, steps)


    def send_side(side, steps):
        device = slab(steps)
        for copy in (
            remote(feat_hbm, side_rows.at[side, 0], send_sem.at[0], side_sem.at[0], device),
            remote(
                vec_hbm,
                side_rows.at[side, pl.ds(1, 3)],
                send_sem.at[0],
                side_sem.at[0],
                device,
            ),
            remote(pos_hbm, side_pos.at[side], send_sem.at[0], side_sem.at[0], device),
            remote(halo_hbm, side_halo.at[side], send_sem.at[0], side_sem.at[0], device),
        ):
            copy.start()

    send_sides(around[:1])
    lattice = lat[...].astype(f32)
    lattice_high = jnp.floor(lattice[2:3] * 0.0625) * 16.0
    lattice_low = lattice[2:3] - lattice_high
    lattice_parts = jnp.concatenate(
        [lattice[0:1]] * 3
        + [lattice[1:2]] * 3
        + [lattice_high] * 3
        + [lattice_low] * 3
        + [jnp.zeros((4, width), f32)],
        axis=0,
    ).astype(bf16)

    def position_parts(coords):
        rows = []
        for axis in (0, 1, 2, 2):
            rows += list(three_parts(coords[axis : axis + 1]))
        rows.append(jnp.zeros((4, coords.shape[1]), f32))
        return jnp.concatenate(rows, axis=0).astype(bf16)

    def make_tables(first, coords):
        turns = over_first(lattice_parts, position_parts(coords))
        cosine, sine = turn_tables(turns)
        columns = slice(first * own, first * own + coords.shape[1])
        for number in range(members):
            rows = slice(number * chunk, (number + 1) * chunk)
            tables[2 * number * chunk : (2 * number + 1) * chunk, columns] = cosine[rows]
            tables[(2 * number + 1) * chunk : 2 * (number + 1) * chunk, columns] = sine[rows]

    def totals_of(first, features):
        return lax.dot_general(
            features,
            tables[:, first * own : first * own + features.shape[1]],
            (((1,), (1,)), ((), ())),
            preferred_element_type=f32,
        )

    make_tables(0, pos[...])
    def batch_features(first, count):
        return jnp.concatenate(
            [own_projected[...] if slot == 0 else group_feat[slot] for slot in range(first, first + count)],
            axis=1,
        )

    def wait_features(first, count):
        begin = max(first, 1)
        wait_bytes(
            group_feat.at[pl.ds(begin, first + count - begin)], feat_sems.at[0 if first < pair else 1]
        )

    for slot in range(1, pair):
        wait_bytes(group_pos.at[slot], pos_sems.at[0])
        make_tables(slot, group_pos[slot])
    if pair > 1:
        wait_features(0, pair)
    near_totals[...] = totals_of(0, batch_features(0, pair))
    pass_round(0)
    send_sides(across)
    for first in range(pair, peers, pair):
        wait_bytes(group_pos.at[pl.ds(first, pair)], pos_sems.at[first // pair])
        make_tables(
            first,
            jnp.concatenate([group_pos[slot] for slot in range(first, first + pair)], axis=1),
        )
    wait_features(pair, peers - pair)
    totals = near_totals[...] + totals_of(pair, batch_features(pair, peers - pair))
    for number in range(members):
        totals_out[number] = totals[:, 2 * number * chunk : 2 * (number + 1) * chunk].astype(bf16)
    for number in range(1, rounds - 1):
        pass_round(number)
    for index in range(members - 1):
        number = jnp.where(index < high, high - 1 - index, index + 1)
        remote(
            totals_out.at[number],
            totals_in.at[slot_between(number, high)],
            send_sem.at[1],
            stage_sems.at[0],
            member(number),
        ).start()

    @pl.when(high > 0)
    def _():
        remote(
            totals_out.at[pl.ds(1, members - 1)],
            totals_all.at[high - 1],
            send_sem.at[1],
            stage_sems.at[3],
            member(0),
        ).start()

    send_sides(inside)
    if rounds > 1:
        pass_round(rounds - 1)
    send_sides(around[1:])

    for copy in local[4:]:
        copy.wait()
    for number in range(members):
        part = kfilter[:, number * chunk : (number + 1) * chunk] * norm_scale
        chunk_filters[number] = jnp.concatenate([part, part], axis=1)
    bias = jnp.broadcast_to(node_bias[...], (own, channels)).T

    def fill_sources(index, one_feat, one_vec):
        columns = slice(index * own, (index + 1) * own)
        value = over_first(node_weight[...], one_feat[...]) + bias
        hidden = (value / (1.0 + jnp.exp(-value))).astype(bf16)
        source_rows[: 3 * channels, columns] = over_first(message_weight[...], hidden).astype(bf16)
        source_rows[3 * channels :, columns] = one_vec[...].reshape(3 * channels, own)

    fill_sources(0, feat, vec)
    def send_filtered(number):
        remote(
            filtered.at[high],
            filtered.at[high],
            send_sem.at[1],
            stage_sems.at[1],
            member(number),
        ).start()

    wait_bytes(totals_in.at[pl.ds(1, members - 1)], stage_sems.at[0])
    total = totals_out[high].astype(f32)
    for slot in range(1, members):
        total = total + totals_in[slot].astype(f32)
    filtered[high] = (chunk_filters[high] * total).astype(bf16)

    @pl.when(high > 0)
    def _():
        for index in range(members - 2):
            send_filtered(1 + index + jnp.where(index + 1 >= high, 1, 0))

    @pl.when(high == 0)
    def _():
        for number in range(members - 1, 0, -1):
            send_filtered(number)

    @pl.when(high == 0)
    def _():
        wait_bytes(totals_all, stage_sems.at[3])
        for number in range(1, members):
            total = totals_out[number].astype(f32)
            for source in range(members - 1):
                total = total + totals_all[source, number - 1].astype(f32)
            filtered[number] = (chunk_filters[number] * total).astype(bf16)

    @pl.when(high > 0)
    def _():
        wait_bytes(filtered.at[pl.ds(1, members - 1)], stage_sems.at[1])

    spectrum = jnp.concatenate([filtered[number] for number in range(members)], axis=1)
    def messages_of(first, last):
        return jnp.dot(
            spectrum, tables[:, first * own : last * own], preferred_element_type=f32
        )

    def send_message(slot, value):
        message_out[slot] = value.astype(bf16)
        remote(
            message_out.at[slot],
            message_in_slots.at[slot],
            send_sem.at[0],
            stage_sems.at[2],
            peer(slot, -1),
        ).start()

    group = pair * (2 if peers % (2 * pair) == 0 else 1)
    for first in range(peers - group, -1, -group):
        values = messages_of(first, first + group)
        for slot in range(first + group - 1, first - 1, -1):
            value = values[:, (slot - first) * own : (slot - first + 1) * own]
            if slot > 0:
                send_message(slot, value)
            else:
                result = value
    wait_bytes(side_total, side_sem.at[0])
    for side in range(2):
        fill_sources(1 + side, side_rows.at[side, 0], side_rows.at[side, pl.ds(1, 3)])
    ids = nbr[...]
    reach = side_halo.shape[2]

    def picked(row, index):
        return jnp.take_along_axis(
            jnp.broadcast_to(row, (slots, row.shape[1])), index, axis=1, mode="promise_in_bounds"
        )

    below_slot = jnp.clip(ids - own, 0, reach - 1)
    above_slot = jnp.clip(ids - (own + reach), 0, reach - 1)
    own_atom = jnp.clip(ids, 0, own - 1)
    below_atom = picked(side_halo[0, 0:1], below_slot)
    above_atom = picked(side_halo[1, 1:2], above_slot)
    is_own = ids < own
    is_below = ids < own + reach
    used = ids < own + 2 * reach
    atoms = jnp.where(
        is_own,
        ids,
        jnp.where(is_below, below_atom + own, jnp.where(used, above_atom + 2 * own, 3 * own)),
    )
    cartesian = []
    for axis in range(3):
        taken = jnp.where(
            is_own,
            picked(pos[axis : axis + 1], own_atom),
            jnp.where(
                is_below,
                picked(side_pos[0, axis : axis + 1], below_atom),
                picked(side_pos[1, axis : axis + 1], above_atom),
            ),
        )
        taken = jnp.where(used, taken, 0.0)
        offset = taken - pos[axis : axis + 1]
        offset = offset - jnp.floor(offset + 0.5)
        cartesian.append(offset * (side_length if axis < 2 else slab_depth * slab_count))
    distance = jnp.sqrt(
        cartesian[0] * cartesian[0] + cartesian[1] * cartesian[1] + cartesian[2] * cartesian[2]
    )
    limit = jnp.maximum(distance, distance_floor)
    direction = [part / limit for part in cartesian]

    radial_count = radial_weight.shape[0]
    spread = 1.5 * radial_reach / radial_count
    centers = lax.broadcasted_iota(jnp.int32, (radial_count, own), 0).astype(f32) * (
        radial_reach / (radial_count - 1)
    )
    numbers = lax.broadcasted_iota(jnp.int32, (3 * own, own), 0)

    def edges(j, sums):
        row = slice(j, j + 1)
        chosen = jnp.where(numbers == atoms[row], 1.0, 0.0).astype(bf16)
        gathered = jnp.dot(source_rows[...], chosen, preferred_element_type=f32)
        scaled = (distance[row] - centers) * (1.0 / spread)
        radial = jnp.exp(-(scaled * scaled)).astype(bf16)
        terms = gathered[: 3 * channels] * over_first(radial_weight[...], radial)
        first = terms[:channels]
        second = terms[channels : 2 * channels]
        third = terms[2 * channels :]
        new = [sums[0] + first]
        for axis in range(3):
            begin = (3 + axis) * channels
            new.append(
                sums[1 + axis]
                + gathered[begin : begin + channels] * second
                + third * direction[axis][row]
            )
        return new

    sums = [jnp.zeros((channels, own), f32)] * 4
    half = slots // 2
    for j in range(half):
        sums = edges(j, sums)

    for j in range(half, slots):
        sums = edges(j, sums)
    for axis in range(3):
        out_all[1 + axis] = (vec[axis].astype(f32) + sums[1 + axis]).astype(bf16)
    result = result + feat[...].astype(f32) + sums[0]

    wait_bytes(message_in_slots.at[pl.ds(1, peers - 1)], stage_sems.at[2])
    for d in range(1, peers):
        result = result + message_in_slots[d].astype(f32)
    out_all[0] = result.astype(bf16)
    wait_bytes(sent_total, send_sem.at[0])
    @pl.when(high > 0)
    def _():
        wait_bytes(stage_total.at[pl.ds(0, 3 * members - 4)], send_sem.at[1])

    @pl.when(high == 0)
    def _():
        wait_bytes(stage_total.at[pl.ds(0, 2 * members - 2)], send_sem.at[1])


def split_kernel(both, out_feat, out_vec, sems):
    feat_copy = pltpu.make_async_copy(both.at[0], out_feat, sems.at[0])
    vec_copy = pltpu.make_async_copy(both.at[pl.ds(1, 3)], out_vec, sems.at[0])
    feat_copy.start()
    vec_copy.start()
    feat_copy.wait()
    vec_copy.wait()


def shards(
    features,
    vectors,
    positions,
    neighbours,
    halo_lists,
    lattice,
    kspace_filter,
    node_weight,
    node_bias,
    message_weight,
    radial_weight,
    ewald_weight,
):
    n_dom, n_kb = lax.axis_size("dom"), lax.axis_size("kb")
    channels, own = features.shape
    reach = halo_lists.shape[1]
    width = kspace_filter.shape[1]
    low_count = 2 if n_dom % 2 == 0 else 1
    members, peers = n_dom // low_count, n_kb * low_count
    width = width // low_count
    chunk = width // members
    pair = 2 if n_kb % 2 == 0 else 1
    norm_scale = 1.0 / math.sqrt(lattice.shape[1] * own * n_dom * n_kb)
    row_bytes = 128 * 4
    block_bytes = channels * own * 2
    side_bytes = 2 * (4 * block_bytes + 3 * own * 4 + 2 * reach * 4)
    sent_bytes = side_bytes + (peers - 1) * (3 * own * 4 + 2 * block_bytes)
    vmem = pl.BlockSpec(memory_space=pltpu.VMEM)
    hbm = pl.BlockSpec(memory_space=pltpu.HBM)
    dma = pltpu.SemaphoreType.DMA
    bias_row = node_bias[None, :]

    def like(array):
        return pltpu.VMEM(array.shape, array.dtype)

    both = pl.pallas_call(
        functools.partial(kernel, (n_dom, n_kb, low_count, norm_scale)),
        out_shape=pltpu.VMEM((4, channels, own), bf16),
        in_specs=[hbm] * 12,
        out_specs=vmem,
        scratch_shapes=[
            like(features),
            like(vectors),
            like(positions),
            like(neighbours),
            pltpu.VMEM((3, width), jnp.int32),
            pltpu.VMEM((channels, width), f32),
            like(node_weight),
            like(bias_row),
            like(message_weight),
            like(radial_weight),
            like(ewald_weight),
            like(features),
            pltpu.VMEM((peers, channels, own), bf16),
            pltpu.VMEM((peers, 3, own), f32),
            pltpu.VMEM((2, 4, channels, own), bf16),
            pltpu.VMEM((2, 3, own), f32),
            pltpu.VMEM((2, 2, reach), jnp.int32),
            pltpu.VMEM((2 * width, peers * own), bf16),
            pltpu.VMEM((channels, 2 * width), f32),
            pltpu.VMEM((members, channels, 2 * chunk), bf16),
            pltpu.VMEM((members, channels, 2 * chunk), bf16),
            pltpu.VMEM((members - 1, members - 1, channels, 2 * chunk), bf16),
            pltpu.VMEM((members, channels, 2 * chunk), f32),
            pltpu.VMEM((members, channels, 2 * chunk), bf16),
            pltpu.VMEM((peers, channels, own), bf16),
            pltpu.VMEM((peers, channels, own), bf16),
            pltpu.VMEM((6 * channels, 3 * own), bf16),
            pltpu.VMEM((side_bytes // row_bytes, 1, 128), f32),
            pltpu.VMEM((sent_bytes // row_bytes, 1, 128), f32),
            pltpu.VMEM((3 * members, channels, 2 * chunk), bf16),
            pltpu.SemaphoreType.REGULAR((members - 1,)),
            dma((2,)),
            dma((peers // pair,)),
            dma((2,)),
            dma((1,)),
            dma((4,)),
            dma((2,)),
        ],
        compiler_params=pltpu.CompilerParams(collective_id=0, has_side_effects=True),
    )(
        features,
        vectors,
        positions,
        neighbours,
        halo_lists,
        lattice,
        kspace_filter,
        node_weight,
        bias_row,
        message_weight,
        radial_weight,
        ewald_weight,
    )
    return pl.pallas_call(
        split_kernel,
        out_shape=(
            jax.ShapeDtypeStruct(features.shape, bf16),
            jax.ShapeDtypeStruct(vectors.shape, bf16),
        ),
        in_specs=[vmem],
        out_specs=(pl.BlockSpec(memory_space=pl.ANY),) * 2,
        scratch_shapes=[dma((1,))],
    )(pltpu.with_memory_space_constraint(both, pltpu.VMEM))


def solution(mesh):
    atoms = P(None, ("dom", "kb"))
    placed = (
        atoms,
        P(None, None, ("dom", "kb")),
        atoms,
        atoms,
        atoms,
        P(),
        P(None, "kb"),
        P(),
        P(),
        P(),
        P(),
        P(),
    )
    return jax.shard_map(
        shards,
        mesh=mesh,
        in_specs=placed,
        out_specs=(atoms, P(None, None, ("dom", "kb"))),
        check_vma=False,
    )
```

```python
import functools
import math

import jax
import jax.numpy as jnp
import numpy as np
from jax import lax
from jax.experimental import pallas as pl
from jax.experimental.pallas import tpu as pltpu
from jax.sharding import PartitionSpec as P

side_length = 6.0
slab_depth = 6.0
radial_reach = 6.0
distance_floor = 1.0
MESH = pl.DeviceIdType.MESH
f32 = jnp.float32
bf16 = jnp.bfloat16


def polynomial(function, degree):
    nodes = (np.cos((np.arange(degree + 1) + 0.5) * np.pi / (degree + 1)) + 1.0) / 2.0
    fitted = np.polynomial.polynomial.polyfit(nodes, function(nodes / 4.0), degree)
    return [float(value * 4.0**power) for power, value in enumerate(fitted)]


half_cos = polynomial(lambda w: np.sqrt(2.0) * np.cos(np.pi * np.sqrt(w)), 3)
half_sin = polynomial(lambda w: np.sqrt(2.0) * np.sin(np.pi * np.sqrt(w)) / np.sqrt(w), 3)


def evaluate(terms, w):
    value = terms[-1] * w + terms[-2]
    for term in terms[-3::-1]:
        value = value * w + term
    return value


def turn_tables(turns):
    part = turns - jnp.round(turns)
    w = part * part
    sine = part * evaluate(half_sin, w)
    cosine = evaluate(half_cos, w)
    return (1.0 - sine * sine).astype(bf16), (sine * cosine).astype(bf16)


def over_first(first_operand, second_operand):
    return lax.dot_general(
        first_operand, second_operand, (((0,), (0,)), ((), ())), preferred_element_type=f32
    )


def three_parts(value):
    high = value.astype(bf16)
    rest = value - high.astype(f32)
    middle = rest.astype(bf16)
    low = (rest - middle.astype(f32)).astype(bf16)
    return high.astype(f32), middle.astype(f32), low.astype(f32)


def kernel(
    sizes,
    feat_hbm,
    vec_hbm,
    pos_hbm,
    nbr_hbm,
    halo_hbm,
    lat_hbm,
    kfilter_hbm,
    node_weight_hbm,
    node_bias_hbm,
    message_weight_hbm,
    radial_weight_hbm,
    ewald_weight_hbm,
    out_all,
    feat,
    vec,
    pos,
    nbr,
    lat,
    kfilter,
    node_weight,
    node_bias,
    message_weight,
    radial_weight,
    ewald_weight,
    own_projected,
    group_feat,
    group_pos,
    side_rows,
    side_pos,
    side_halo,
    tables,
    near_totals,
    totals_out,
    totals_in,
    totals_all,
    chunk_filters,
    filtered,
    message_out,
    message_in_slots,
    source_rows,
    side_total,
    sent_total,
    stage_total,
    round_sems,
    local_sems,
    pos_sems,
    feat_sems,
    side_sem,
    stage_sems,
    send_sem,
):
    n_dom, n_kb, low_count, norm_scale = sizes
    dom, kb = lax.axis_index("dom"), lax.axis_index("kb")
    rank = dom * n_kb + kb
    slab_count = n_dom * n_kb
    channels, own = feat.shape
    slots = nbr.shape[0]
    width = kfilter.shape[1]
    members = n_dom // low_count
    pair = 2 if n_kb % 2 == 0 else 1
    pairs = n_kb // pair
    high, low = lax.div(dom, low_count), lax.rem(dom, low_count)
    peers = n_kb * low_count
    chunk = width // members

    def slot_between(target, source):
        return 1 + source - jnp.where(source > target, 1, 0)

    def member(number):
        return {"dom": number * low_count + low, "kb": kb}

    def peer(slot, sign=1):
        core, across, side = slot % pair, slot // pair % pairs, slot // n_kb
        place = lax.rem(lax.div(kb, pair) + sign * across + pairs, pairs)
        return {
            "dom": high * low_count + lax.rem(low + side, low_count),
            "kb": place * pair + lax.rem(lax.rem(kb, pair) + core, pair),
        }

    others = list(range(1, peers))

    def slab(steps):
        number = lax.rem(rank + steps + slab_count, slab_count)
        return {"dom": lax.div(number, n_kb), "kb": lax.rem(number, n_kb)}

    def remote(source, target, send_sem, recv_sem, device):
        return pltpu.make_async_remote_copy(
            src_ref=source,
            dst_ref=target,
            send_sem=send_sem,
            recv_sem=recv_sem,
            device_id=device,
            device_id_type=MESH,
        )

    def wait_bytes(ref, sem):
        pltpu.make_async_copy(ref, ref, sem).wait()

    barrier = pltpu.get_barrier_semaphore()
    targets = [
        jnp.where(high == 0, members - 1 - index, index + jnp.where(index >= high, 1, 0))
        for index in range(members - 1)
    ]
    greeted = [peer(slot) for slot in range(peers - 1, 0, -1)]
    beside = [(-1, high > 0), (1, high < members - 1)]
    beside_count = sum(jnp.where(there, 1, 0) for steps, there in beside)

    def tell_beside(sem):
        for steps, there in beside:

            @pl.when(there)
            def _(steps=steps):
                pl.semaphore_signal(
                    sem, inc=1, device_id=member(high + steps), device_id_type=MESH
                )

    for device in greeted:
        pl.semaphore_signal(barrier, inc=1, device_id=device, device_id_type=MESH)
    tell_beside(barrier)
    is_last = rank == slab_count - 1

    @pl.when(rank == 0)
    def _():
        pl.semaphore_signal(barrier, inc=1, device_id=slab(-1), device_id_type=MESH)

    start = pl.multiple_of(kb * (width * low_count) + low * width, math.gcd(width, 128))
    filter_start = pl.multiple_of(low * width, math.gcd(width, 128))
    staged = [
        (feat_hbm, feat),
        (ewald_weight_hbm, ewald_weight),
        (pos_hbm, pos),
        (lat_hbm.at[:, pl.ds(start, width)], lat),
        (kfilter_hbm.at[:, pl.ds(filter_start, width)], kfilter),
        (node_weight_hbm, node_weight),
        (node_bias_hbm, node_bias),
        (message_weight_hbm, message_weight),
        (nbr_hbm, nbr),
        (radial_weight_hbm, radial_weight),
        (vec_hbm, vec),
    ]
    local = [
        pltpu.make_async_copy(source, target, local_sems.at[0 if i < 4 else 1])
        for i, (source, target) in enumerate(staged)
    ]
    for copy in local:
        copy.start()

    for copy in local[:4]:
        copy.wait()
    own_projected[...] = over_first(ewald_weight[...], feat[...]).astype(bf16)
    pl.semaphore_wait(barrier, len(greeted) + beside_count + jnp.where(is_last, 1, 0))
    pos_copies = [
        remote(pos, group_pos.at[slot], send_sem.at[0], pos_sems.at[slot // pair], peer(slot))
        for slot in others
    ]
    feat_copies = [
        remote(
            own_projected,
            group_feat.at[slot],
            send_sem.at[0],
            feat_sems.at[0 if slot < pair else 1],
            peer(slot),
        )
        for slot in others
    ]
    for copy in pos_copies[::-1] + feat_copies[::-1]:
        copy.start()
    rounds = members - 1
    tell_beside(round_sems.at[0])

    def pass_round(number):
        pl.semaphore_wait(round_sems.at[number], beside_count)
        if number + 1 < rounds:
            tell_beside(round_sems.at[number + 1])

    around = [(0, 1, is_last), (1, -1, rank == 0)]
    inside = [
        (side, steps, lax.div(rank + steps + peers, peers) == high + 1)
        for side, steps in ((0, 1), (1, -1))
    ]
    across = [
        (side, steps, jnp.logical_not(jnp.logical_or(ends, within)))
        for (side, steps, ends), (_, _, within) in zip(around, inside)
    ]

    def send_sides(cases):
        for side, steps, chosen in cases:

            @pl.when(chosen)
            def _(side=side, steps=steps):
                send_side(side, steps)


    def send_side(side, steps):
        device = slab(steps)
        for copy in (
            remote(feat_hbm, side_rows.at[side, 0], send_sem.at[0], side_sem.at[0], device),
            remote(
                vec_hbm,
                side_rows.at[side, pl.ds(1, 3)],
                send_sem.at[0],
                side_sem.at[0],
                device,
            ),
            remote(pos_hbm, side_pos.at[side], send_sem.at[0], side_sem.at[0], device),
            remote(halo_hbm, side_halo.at[side], send_sem.at[0], side_sem.at[0], device),
        ):
            copy.start()

    send_sides(around[:1])
    lattice = lat[...].astype(f32)
    lattice_high = jnp.floor(lattice[2:3] * 0.0625) * 16.0
    lattice_low = lattice[2:3] - lattice_high
    lattice_parts = jnp.concatenate(
        [lattice[0:1]] * 3
        + [lattice[1:2]] * 3
        + [lattice_high] * 3
        + [lattice_low] * 3
        + [jnp.zeros((4, width), f32)],
        axis=0,
    ).astype(bf16)

    def position_parts(coords):
        rows = []
        for axis in (0, 1, 2, 2):
            rows += list(three_parts(coords[axis : axis + 1]))
        rows.append(jnp.zeros((4, coords.shape[1]), f32))
        return jnp.concatenate(rows, axis=0).astype(bf16)

    def make_tables(first, coords):
        turns = over_first(lattice_parts, position_parts(coords))
        cosine, sine = turn_tables(turns)
        columns = slice(first * own, first * own + coords.shape[1])
        for number in range(members):
            rows = slice(number * chunk, (number + 1) * chunk)
            tables[2 * number * chunk : (2 * number + 1) * chunk, columns] = cosine[rows]
            tables[(2 * number + 1) * chunk : 2 * (number + 1) * chunk, columns] = sine[rows]

    def totals_of(first, features):
        return lax.dot_general(
            features,
            tables[:, first * own : first * own + features.shape[1]],
            (((1,), (1,)), ((), ())),
            preferred_element_type=f32,
        )

    make_tables(0, pos[...])
    def batch_features(first, count):
        return jnp.concatenate(
            [own_projected[...] if slot == 0 else group_feat[slot] for slot in range(first, first + count)],
            axis=1,
        )

    def wait_features(first, count):
        begin = max(first, 1)
        wait_bytes(
            group_feat.at[pl.ds(begin, first + count - begin)], feat_sems.at[0 if first < pair else 1]
        )

    for slot in range(1, pair):
        wait_bytes(group_pos.at[slot], pos_sems.at[0])
        make_tables(slot, group_pos[slot])
    if pair > 1:
        wait_features(0, pair)
    near_totals[...] = totals_of(0, batch_features(0, pair))
    pass_round(0)
    send_sides(across)
    for first in range(pair, peers, pair):
        wait_bytes(group_pos.at[pl.ds(first, pair)], pos_sems.at[first // pair])
        make_tables(
            first,
            jnp.concatenate([group_pos[slot] for slot in range(first, first + pair)], axis=1),
        )
    wait_features(pair, peers - pair)
    totals = near_totals[...] + totals_of(pair, batch_features(pair, peers - pair))
    for number in range(members):
        totals_out[number] = totals[:, 2 * number * chunk : 2 * (number + 1) * chunk].astype(bf16)
    for number in range(1, rounds - 1):
        pass_round(number)
    for index in range(members - 1):
        number = jnp.where(
            index < high, lax.rem(high - index, jnp.maximum(high, 1)), index + 1
        )
        remote(
            totals_out.at[number],
            totals_in.at[slot_between(number, high)],
            send_sem.at[1],
            stage_sems.at[0],
            member(number),
        ).start()

    @pl.when(high > 0)
    def _():
        remote(
            totals_out.at[pl.ds(1, members - 1)],
            totals_all.at[high - 1],
            send_sem.at[1],
            stage_sems.at[3],
            member(0),
        ).start()

    send_sides(inside)
    if rounds > 1:
        pass_round(rounds - 1)
    send_sides(around[1:])

    for copy in local[4:]:
        copy.wait()
    for number in range(members):
        part = kfilter[:, number * chunk : (number + 1) * chunk] * norm_scale
        chunk_filters[number] = jnp.concatenate([part, part], axis=1)
    bias = jnp.broadcast_to(node_bias[...], (own, channels)).T

    def fill_sources(index, one_feat, one_vec):
        columns = slice(index * own, (index + 1) * own)
        value = over_first(node_weight[...], one_feat[...]) + bias
        hidden = (value / (1.0 + jnp.exp(-value))).astype(bf16)
        source_rows[: 3 * channels, columns] = over_first(message_weight[...], hidden).astype(bf16)
        source_rows[3 * channels :, columns] = one_vec[...].reshape(3 * channels, own)

    fill_sources(0, feat, vec)
    def send_filtered(number):
        remote(
            filtered.at[high],
            filtered.at[high],
            send_sem.at[1],
            stage_sems.at[1],
            member(number),
        ).start()

    wait_bytes(totals_in.at[pl.ds(1, members - 1)], stage_sems.at[0])
    total = totals_out[high].astype(f32)
    for slot in range(1, members):
        total = total + totals_in[slot].astype(f32)
    filtered[high] = (chunk_filters[high] * total).astype(bf16)

    @pl.when(high > 0)
    def _():
        for index in range(members - 2):
            send_filtered(1 + index + jnp.where(index + 1 >= high, 1, 0))

    @pl.when(high == 0)
    def _():
        for number in range(members - 1, 0, -1):
            send_filtered(number)

    @pl.when(high == 0)
    def _():
        wait_bytes(totals_all, stage_sems.at[3])
        for number in range(1, members):
            total = totals_out[number].astype(f32)
            for source in range(members - 1):
                total = total + totals_all[source, number - 1].astype(f32)
            filtered[number] = (chunk_filters[number] * total).astype(bf16)

    @pl.when(high > 0)
    def _():
        wait_bytes(filtered.at[pl.ds(1, members - 1)], stage_sems.at[1])

    spectrum = jnp.concatenate([filtered[number] for number in range(members)], axis=1)
    def messages_of(first, last):
        return jnp.dot(
            spectrum, tables[:, first * own : last * own], preferred_element_type=f32
        )

    def send_message(slot, value):
        message_out[slot] = value.astype(bf16)
        remote(
            message_out.at[slot],
            message_in_slots.at[slot],
            send_sem.at[0],
            stage_sems.at[2],
            peer(slot, -1),
        ).start()

    group = pair * (2 if peers % (2 * pair) == 0 else 1)
    for first in range(peers - group, -1, -group):
        values = messages_of(first, first + group)
        for slot in range(first + group - 1, first - 1, -1):
            value = values[:, (slot - first) * own : (slot - first + 1) * own]
            if slot > 0:
                send_message(slot, value)
            else:
                result = value
    wait_bytes(side_total, side_sem.at[0])
    for side in range(2):
        fill_sources(1 + side, side_rows.at[side, 0], side_rows.at[side, pl.ds(1, 3)])
    ids = nbr[...]
    reach = side_halo.shape[2]

    def picked(row, index):
        return jnp.take_along_axis(
            jnp.broadcast_to(row, (slots, row.shape[1])), index, axis=1, mode="promise_in_bounds"
        )

    below_slot = jnp.clip(ids - own, 0, reach - 1)
    above_slot = jnp.clip(ids - (own + reach), 0, reach - 1)
    own_atom = jnp.clip(ids, 0, own - 1)
    below_atom = picked(side_halo[0, 0:1], below_slot)
    above_atom = picked(side_halo[1, 1:2], above_slot)
    is_own = ids < own
    is_below = ids < own + reach
    used = ids < own + 2 * reach
    atoms = jnp.where(
        is_own,
        ids,
        jnp.where(is_below, below_atom + own, jnp.where(used, above_atom + 2 * own, 3 * own)),
    )
    cartesian = []
    for axis in range(3):
        taken = jnp.where(
            is_own,
            picked(pos[axis : axis + 1], own_atom),
            jnp.where(
                is_below,
                picked(side_pos[0, axis : axis + 1], below_atom),
                picked(side_pos[1, axis : axis + 1], above_atom),
            ),
        )
        taken = jnp.where(used, taken, 0.0)
        offset = taken - pos[axis : axis + 1]
        offset = offset - jnp.floor(offset + 0.5)
        cartesian.append(offset * (side_length if axis < 2 else slab_depth * slab_count))
    distance = jnp.sqrt(
        cartesian[0] * cartesian[0] + cartesian[1] * cartesian[1] + cartesian[2] * cartesian[2]
    )
    limit = jnp.maximum(distance, distance_floor)
    direction = [part / limit for part in cartesian]

    radial_count = radial_weight.shape[0]
    spread = 1.5 * radial_reach / radial_count
    centers = lax.broadcasted_iota(jnp.int32, (radial_count, own), 0).astype(f32) * (
        radial_reach / (radial_count - 1)
    )
    numbers = lax.broadcasted_iota(jnp.int32, (3 * own, own), 0)

    def edges(j, sums):
        row = slice(j, j + 1)
        chosen = jnp.where(numbers == atoms[row], 1.0, 0.0).astype(bf16)
        gathered = jnp.dot(source_rows[...], chosen, preferred_element_type=f32)
        scaled = (distance[row] - centers) * (1.0 / spread)
        radial = jnp.exp(-(scaled * scaled)).astype(bf16)
        terms = gathered[: 3 * channels] * over_first(radial_weight[...], radial)
        first = terms[:channels]
        second = terms[channels : 2 * channels]
        third = terms[2 * channels :]
        new = [sums[0] + first]
        for axis in range(3):
            begin = (3 + axis) * channels
            new.append(
                sums[1 + axis]
                + gathered[begin : begin + channels] * second
                + third * direction[axis][row]
            )
        return new

    sums = [jnp.zeros((channels, own), f32)] * 4
    half = slots // 2
    for j in range(half):
        sums = edges(j, sums)

    for j in range(half, slots):
        sums = edges(j, sums)
    for axis in range(3):
        out_all[1 + axis] = (vec[axis].astype(f32) + sums[1 + axis]).astype(bf16)
    result = result + feat[...].astype(f32) + sums[0]

    wait_bytes(message_in_slots.at[pl.ds(1, peers - 1)], stage_sems.at[2])
    for d in range(1, peers):
        result = result + message_in_slots[d].astype(f32)
    out_all[0] = result.astype(bf16)
    wait_bytes(sent_total, send_sem.at[0])
    @pl.when(high > 0)
    def _():
        wait_bytes(stage_total.at[pl.ds(0, 3 * members - 4)], send_sem.at[1])

    @pl.when(high == 0)
    def _():
        wait_bytes(stage_total.at[pl.ds(0, 2 * members - 2)], send_sem.at[1])


def split_kernel(both, out_feat, out_vec, sems):
    feat_copy = pltpu.make_async_copy(both.at[0], out_feat, sems.at[0])
    vec_copy = pltpu.make_async_copy(both.at[pl.ds(1, 3)], out_vec, sems.at[0])
    feat_copy.start()
    vec_copy.start()
    feat_copy.wait()
    vec_copy.wait()


def shards(
    features,
    vectors,
    positions,
    neighbours,
    halo_lists,
    lattice,
    kspace_filter,
    node_weight,
    node_bias,
    message_weight,
    radial_weight,
    ewald_weight,
):
    n_dom, n_kb = lax.axis_size("dom"), lax.axis_size("kb")
    channels, own = features.shape
    reach = halo_lists.shape[1]
    width = kspace_filter.shape[1]
    low_count = 2 if n_dom % 2 == 0 else 1
    members, peers = n_dom // low_count, n_kb * low_count
    width = width // low_count
    chunk = width // members
    pair = 2 if n_kb % 2 == 0 else 1
    norm_scale = 1.0 / math.sqrt(lattice.shape[1] * own * n_dom * n_kb)
    row_bytes = 128 * 4
    block_bytes = channels * own * 2
    side_bytes = 2 * (4 * block_bytes + 3 * own * 4 + 2 * reach * 4)
    sent_bytes = side_bytes + (peers - 1) * (3 * own * 4 + 2 * block_bytes)
    vmem = pl.BlockSpec(memory_space=pltpu.VMEM)
    hbm = pl.BlockSpec(memory_space=pltpu.HBM)
    dma = pltpu.SemaphoreType.DMA
    bias_row = node_bias[None, :]

    def like(array):
        return pltpu.VMEM(array.shape, array.dtype)

    both = pl.pallas_call(
        functools.partial(kernel, (n_dom, n_kb, low_count, norm_scale)),
        out_shape=pltpu.VMEM((4, channels, own), bf16),
        in_specs=[hbm] * 12,
        out_specs=vmem,
        scratch_shapes=[
            like(features),
            like(vectors),
            like(positions),
            like(neighbours),
            pltpu.VMEM((3, width), jnp.int32),
            pltpu.VMEM((channels, width), f32),
            like(node_weight),
            like(bias_row),
            like(message_weight),
            like(radial_weight),
            like(ewald_weight),
            like(features),
            pltpu.VMEM((peers, channels, own), bf16),
            pltpu.VMEM((peers, 3, own), f32),
            pltpu.VMEM((2, 4, channels, own), bf16),
            pltpu.VMEM((2, 3, own), f32),
            pltpu.VMEM((2, 2, reach), jnp.int32),
            pltpu.VMEM((2 * width, peers * own), bf16),
            pltpu.VMEM((channels, 2 * width), f32),
            pltpu.VMEM((members, channels, 2 * chunk), bf16),
            pltpu.VMEM((members, channels, 2 * chunk), bf16),
            pltpu.VMEM((members - 1, members - 1, channels, 2 * chunk), bf16),
            pltpu.VMEM((members, channels, 2 * chunk), f32),
            pltpu.VMEM((members, channels, 2 * chunk), bf16),
            pltpu.VMEM((peers, channels, own), bf16),
            pltpu.VMEM((peers, channels, own), bf16),
            pltpu.VMEM((6 * channels, 3 * own), bf16),
            pltpu.VMEM((side_bytes // row_bytes, 1, 128), f32),
            pltpu.VMEM((sent_bytes // row_bytes, 1, 128), f32),
            pltpu.VMEM((3 * members, channels, 2 * chunk), bf16),
            pltpu.SemaphoreType.REGULAR((members - 1,)),
            dma((2,)),
            dma((peers // pair,)),
            dma((2,)),
            dma((1,)),
            dma((4,)),
            dma((2,)),
        ],
        compiler_params=pltpu.CompilerParams(collective_id=0, has_side_effects=True),
    )(
        features,
        vectors,
        positions,
        neighbours,
        halo_lists,
        lattice,
        kspace_filter,
        node_weight,
        bias_row,
        message_weight,
        radial_weight,
        ewald_weight,
    )
    return pl.pallas_call(
        split_kernel,
        out_shape=(
            jax.ShapeDtypeStruct(features.shape, bf16),
            jax.ShapeDtypeStruct(vectors.shape, bf16),
        ),
        in_specs=[vmem],
        out_specs=(pl.BlockSpec(memory_space=pl.ANY),) * 2,
        scratch_shapes=[dma((1,))],
    )(pltpu.with_memory_space_constraint(both, pltpu.VMEM))


def solution(mesh):
    atoms = P(None, ("dom", "kb"))
    placed = (
        atoms,
        P(None, None, ("dom", "kb")),
        atoms,
        atoms,
        atoms,
        P(),
        P(None, "kb"),
        P(),
        P(),
        P(),
        P(),
        P(),
    )
    return jax.shard_map(
        shards,
        mesh=mesh,
        in_specs=placed,
        out_specs=(atoms, P(None, None, ("dom", "kb"))),
        check_vma=False,
    )
```

```python
import functools
import math

import jax
import jax.numpy as jnp
import numpy as np
from jax import lax
from jax.experimental import pallas as pl
from jax.experimental.pallas import tpu as pltpu
from jax.sharding import PartitionSpec as P

side_length = 6.0
slab_depth = 6.0
radial_reach = 6.0
distance_floor = 1.0
MESH = pl.DeviceIdType.MESH
f32 = jnp.float32
bf16 = jnp.bfloat16


def polynomial(function, degree):
    nodes = (np.cos((np.arange(degree + 1) + 0.5) * np.pi / (degree + 1)) + 1.0) / 2.0
    fitted = np.polynomial.polynomial.polyfit(nodes, function(nodes / 4.0), degree)
    return [float(value * 4.0**power) for power, value in enumerate(fitted)]


half_cos = polynomial(lambda w: np.sqrt(2.0) * np.cos(np.pi * np.sqrt(w)), 3)
half_sin = polynomial(lambda w: np.sqrt(2.0) * np.sin(np.pi * np.sqrt(w)) / np.sqrt(w), 3)


def evaluate(terms, w):
    value = terms[-1] * w + terms[-2]
    for term in terms[-3::-1]:
        value = value * w + term
    return value


def turn_tables(turns):
    part = turns - jnp.round(turns)
    w = part * part
    sine = part * evaluate(half_sin, w)
    cosine = evaluate(half_cos, w)
    return (1.0 - sine * sine).astype(bf16), (sine * cosine).astype(bf16)


def over_first(first_operand, second_operand):
    return lax.dot_general(
        first_operand, second_operand, (((0,), (0,)), ((), ())), preferred_element_type=f32
    )


def three_parts(value):
    high = value.astype(bf16)
    rest = value - high.astype(f32)
    middle = rest.astype(bf16)
    low = (rest - middle.astype(f32)).astype(bf16)
    return high.astype(f32), middle.astype(f32), low.astype(f32)


def kernel(
    sizes,
    feat_hbm,
    vec_hbm,
    pos_hbm,
    nbr_hbm,
    halo_hbm,
    lat_hbm,
    kfilter_hbm,
    node_weight_hbm,
    node_bias_hbm,
    message_weight_hbm,
    radial_weight_hbm,
    ewald_weight_hbm,
    out_all,
    feat,
    vec,
    pos,
    nbr,
    lat,
    kfilter,
    node_weight,
    node_bias,
    message_weight,
    radial_weight,
    ewald_weight,
    own_projected,
    group_feat,
    group_pos,
    side_rows,
    side_pos,
    side_halo,
    tables,
    near_totals,
    totals_out,
    totals_in,
    totals_all,
    chunk_filters,
    filtered,
    message_out,
    message_in_slots,
    source_rows,
    side_total,
    sent_total,
    stage_total,
    round_sems,
    local_sems,
    pos_sems,
    feat_sems,
    side_sem,
    stage_sems,
    send_sem,
):
    n_dom, n_kb, low_count, norm_scale = sizes
    dom, kb = lax.axis_index("dom"), lax.axis_index("kb")
    rank = dom * n_kb + kb
    slab_count = n_dom * n_kb
    channels, own = feat.shape
    slots = nbr.shape[0]
    width = kfilter.shape[1]
    members = n_dom // low_count
    pair = 2 if n_kb % 2 == 0 else 1
    pairs = n_kb // pair
    high, low = lax.div(dom, low_count), lax.rem(dom, low_count)
    peers = n_kb * low_count
    chunk = width // members

    def slot_between(target, source):
        return 1 + source - jnp.where(source > target, 1, 0)

    def member(number):
        return {"dom": number * low_count + low, "kb": kb}

    def peer(slot, sign=1):
        core, across, side = slot % pair, slot // pair % pairs, slot // n_kb
        place = lax.rem(lax.div(kb, pair) + sign * across + pairs, pairs)
        return {
            "dom": high * low_count + lax.rem(low + side, low_count),
            "kb": place * pair + lax.rem(lax.rem(kb, pair) + core, pair),
        }

    others = list(range(1, peers))

    def slab(steps):
        number = lax.rem(rank + steps + slab_count, slab_count)
        return {"dom": lax.div(number, n_kb), "kb": lax.rem(number, n_kb)}

    def remote(source, target, send_sem, recv_sem, device):
        return pltpu.make_async_remote_copy(
            src_ref=source,
            dst_ref=target,
            send_sem=send_sem,
            recv_sem=recv_sem,
            device_id=device,
            device_id_type=MESH,
        )

    def wait_bytes(ref, sem):
        pltpu.make_async_copy(ref, ref, sem).wait()

    barrier = pltpu.get_barrier_semaphore()
    targets = [
        jnp.where(high == 0, members - 1 - index, index + jnp.where(index >= high, 1, 0))
        for index in range(members - 1)
    ]
    greeted = [peer(slot) for slot in range(peers - 1, 0, -1)]
    beside = [(-1, high > 0), (1, high < members - 1)]
    beside_count = sum(jnp.where(there, 1, 0) for steps, there in beside)

    def tell_beside(sem):
        for steps, there in beside:

            @pl.when(there)
            def _(steps=steps):
                pl.semaphore_signal(
                    sem, inc=1, device_id=member(high + steps), device_id_type=MESH
                )

    for device in greeted:
        pl.semaphore_signal(barrier, inc=1, device_id=device, device_id_type=MESH)
    tell_beside(barrier)
    is_last = rank == slab_count - 1

    @pl.when(rank == 0)
    def _():
        pl.semaphore_signal(barrier, inc=1, device_id=slab(-1), device_id_type=MESH)

    start = pl.multiple_of(kb * (width * low_count) + low * width, math.gcd(width, 128))
    filter_start = pl.multiple_of(low * width, math.gcd(width, 128))
    staged = [
        (feat_hbm, feat),
        (ewald_weight_hbm, ewald_weight),
        (pos_hbm, pos),
        (lat_hbm.at[:, pl.ds(start, width)], lat),
        (kfilter_hbm.at[:, pl.ds(filter_start, width)], kfilter),
        (node_weight_hbm, node_weight),
        (node_bias_hbm, node_bias),
        (message_weight_hbm, message_weight),
        (nbr_hbm, nbr),
        (radial_weight_hbm, radial_weight),
        (vec_hbm, vec),
    ]
    local = [
        pltpu.make_async_copy(source, target, local_sems.at[0 if i < 4 else 1])
        for i, (source, target) in enumerate(staged)
    ]
    for copy in local:
        copy.start()

    for copy in local[:4]:
        copy.wait()
    own_projected[...] = over_first(ewald_weight[...], feat[...]).astype(bf16)
    pl.semaphore_wait(barrier, len(greeted) + beside_count + jnp.where(is_last, 1, 0))
    pos_copies = [
        remote(pos, group_pos.at[slot], send_sem.at[0], pos_sems.at[slot // pair], peer(slot))
        for slot in others
    ]
    feat_copies = [
        remote(
            own_projected,
            group_feat.at[slot],
            send_sem.at[0],
            feat_sems.at[0 if slot < pair else 1],
            peer(slot),
        )
        for slot in others
    ]
    for copy in pos_copies[::-1] + feat_copies[::-1]:
        copy.start()
    rounds = members - 1
    tell_beside(round_sems.at[0])

    def pass_round(number):
        pl.semaphore_wait(round_sems.at[number], beside_count)
        if number + 1 < rounds:
            tell_beside(round_sems.at[number + 1])

    around = [(0, 1, is_last), (1, -1, rank == 0)]
    inside = [
        (side, steps, lax.div(rank + steps + peers, peers) == high + 1)
        for side, steps in ((0, 1), (1, -1))
    ]
    across = [
        (side, steps, jnp.logical_not(jnp.logical_or(ends, within)))
        for (side, steps, ends), (_, _, within) in zip(around, inside)
    ]

    def send_sides(cases):
        for side, steps, chosen in cases:

            @pl.when(chosen)
            def _(side=side, steps=steps):
                send_side(side, steps)


    def send_side(side, steps):
        device = slab(steps)
        for copy in (
            remote(feat_hbm, side_rows.at[side, 0], send_sem.at[0], side_sem.at[0], device),
            remote(
                vec_hbm,
                side_rows.at[side, pl.ds(1, 3)],
                send_sem.at[0],
                side_sem.at[0],
                device,
            ),
            remote(pos_hbm, side_pos.at[side], send_sem.at[0], side_sem.at[0], device),
            remote(halo_hbm, side_halo.at[side], send_sem.at[0], side_sem.at[0], device),
        ):
            copy.start()

    send_sides(around[:1])
    lattice = lat[...].astype(f32)
    lattice_high = jnp.floor(lattice[2:3] * 0.0625) * 16.0
    lattice_low = lattice[2:3] - lattice_high
    lattice_parts = jnp.concatenate(
        [lattice[0:1]] * 3
        + [lattice[1:2]] * 3
        + [lattice_high] * 3
        + [lattice_low] * 3
        + [jnp.zeros((4, width), f32)],
        axis=0,
    ).astype(bf16)

    def position_parts(coords):
        rows = []
        for axis in (0, 1, 2, 2):
            rows += list(three_parts(coords[axis : axis + 1]))
        rows.append(jnp.zeros((4, coords.shape[1]), f32))
        return jnp.concatenate(rows, axis=0).astype(bf16)

    def make_tables(first, coords):
        turns = over_first(lattice_parts, position_parts(coords))
        cosine, sine = turn_tables(turns)
        span = coords.shape[1]
        columns = pl.ds(pl.multiple_of(first * own, span), span)
        for number in range(members):
            rows = slice(number * chunk, (number + 1) * chunk)
            tables[2 * number * chunk : (2 * number + 1) * chunk, columns] = cosine[rows]
            tables[(2 * number + 1) * chunk : 2 * (number + 1) * chunk, columns] = sine[rows]

    def totals_of(first, features):
        return lax.dot_general(
            features,
            tables[:, first * own : first * own + features.shape[1]],
            (((1,), (1,)), ((), ())),
            preferred_element_type=f32,
        )

    make_tables(0, pos[...])
    def batch_features(first, count):
        return jnp.concatenate(
            [own_projected[...] if slot == 0 else group_feat[slot] for slot in range(first, first + count)],
            axis=1,
        )

    def wait_features(first, count):
        begin = max(first, 1)
        wait_bytes(
            group_feat.at[pl.ds(begin, first + count - begin)], feat_sems.at[0 if first < pair else 1]
        )

    for slot in range(1, pair):
        wait_bytes(group_pos.at[slot], pos_sems.at[0])
        make_tables(slot, group_pos[slot])
    if pair > 1:
        wait_features(0, pair)
    near_totals[...] = totals_of(0, batch_features(0, pair))
    pass_round(0)
    send_sides(across)
    order = list(range(1, peers // pair))
    if pairs == 2 and low_count == 2:
        place = lax.div(kb, pair)
        aligned = place == low
        order = [
            jnp.where(jnp.logical_and(place == 0, low == 1), 2, 1),
            jnp.where(aligned, 2, 3),
            jnp.where(aligned, 3, jnp.where(low == 1, 1, 2)),
        ]
    for batch in order:
        slots_of = [batch * pair + core for core in range(pair)]
        wait_bytes(
            group_pos.at[pl.ds(batch * pair, pair)],
            pos_sems.at[batch],
        )
        make_tables(
            batch * pair, jnp.concatenate([group_pos[slot] for slot in slots_of], axis=1)
        )
    wait_features(pair, peers - pair)
    totals = near_totals[...] + totals_of(pair, batch_features(pair, peers - pair))
    for number in range(members):
        totals_out[number] = totals[:, 2 * number * chunk : 2 * (number + 1) * chunk].astype(bf16)
    for number in range(1, rounds - 1):
        pass_round(number)
    def send_totals(number):
        remote(
            totals_out.at[number],
            totals_in.at[slot_between(number, high)],
            send_sem.at[1],
            stage_sems.at[0],
            member(number),
        ).start()

    for index in range(members - 1):
        number = jnp.where(
            index < high, lax.rem(high - index, jnp.maximum(high, 1)), index + 1
        )

        @pl.when(jnp.logical_or(number != 1, high <= 1))
        def _(number=number):
            send_totals(number)

    @pl.when(high > 0)
    def _():
        remote(
            totals_out.at[pl.ds(1, members - 1)],
            totals_all.at[high - 1],
            send_sem.at[1],
            stage_sems.at[3],
            member(0),
        ).start()

    @pl.when(high > 1)
    def _():
        send_totals(1)

    send_sides(inside)
    if rounds > 1:
        pass_round(rounds - 1)
    send_sides(around[1:])

    for copy in local[4:]:
        copy.wait()
    for number in range(members):
        part = kfilter[:, number * chunk : (number + 1) * chunk] * norm_scale
        chunk_filters[number] = jnp.concatenate([part, part], axis=1)
    bias = jnp.broadcast_to(node_bias[...], (own, channels)).T

    def fill_sources(index, one_feat, one_vec):
        columns = slice(index * own, (index + 1) * own)
        value = over_first(node_weight[...], one_feat[...]) + bias
        hidden = (value / (1.0 + jnp.exp(-value))).astype(bf16)
        source_rows[: 3 * channels, columns] = over_first(message_weight[...], hidden).astype(bf16)
        source_rows[3 * channels :, columns] = one_vec[...].reshape(3 * channels, own)

    fill_sources(0, feat, vec)
    def send_filtered(number):
        remote(
            filtered.at[high],
            filtered.at[high],
            send_sem.at[1],
            stage_sems.at[1],
            member(number),
        ).start()

    wait_bytes(totals_in.at[pl.ds(1, members - 1)], stage_sems.at[0])
    total = totals_out[high].astype(f32)
    for slot in range(1, members):
        total = total + totals_in[slot].astype(f32)
    filtered[high] = (chunk_filters[high] * total).astype(bf16)

    @pl.when(high > 0)
    def _():
        for index in range(members - 2):
            send_filtered(1 + index + jnp.where(index + 1 >= high, 1, 0))

    @pl.when(high == 0)
    def _():
        for number in range(members - 1, 0, -1):
            send_filtered(number)

    @pl.when(high == 0)
    def _():
        wait_bytes(totals_all, stage_sems.at[3])
        for number in range(1, members):
            total = totals_out[number].astype(f32)
            for source in range(members - 1):
                total = total + totals_all[source, number - 1].astype(f32)
            filtered[number] = (chunk_filters[number] * total).astype(bf16)

    @pl.when(high > 0)
    def _():
        wait_bytes(filtered.at[pl.ds(1, members - 1)], stage_sems.at[1])

    spectrum = jnp.concatenate([filtered[number] for number in range(members)], axis=1)
    def messages_of(first, last):
        return jnp.dot(
            spectrum, tables[:, first * own : last * own], preferred_element_type=f32
        )

    def send_message(slot, value):
        message_out[slot] = value.astype(bf16)
        remote(
            message_out.at[slot],
            message_in_slots.at[slot],
            send_sem.at[0],
            stage_sems.at[2],
            peer(slot, -1),
        ).start()

    group = pair * (2 if peers % (2 * pair) == 0 else 1)
    for first in range(peers - group, -1, -group):
        values = messages_of(first, first + group)
        for slot in range(first + group - 1, first - 1, -1):
            value = values[:, (slot - first) * own : (slot - first + 1) * own]
            if slot > 0:
                send_message(slot, value)
            else:
                result = value
    wait_bytes(side_total, side_sem.at[0])
    for side in range(2):
        fill_sources(1 + side, side_rows.at[side, 0], side_rows.at[side, pl.ds(1, 3)])
    ids = nbr[...]
    reach = side_halo.shape[2]

    def picked(row, index):
        return jnp.take_along_axis(
            jnp.broadcast_to(row, (slots, row.shape[1])), index, axis=1, mode="promise_in_bounds"
        )

    below_slot = jnp.clip(ids - own, 0, reach - 1)
    above_slot = jnp.clip(ids - (own + reach), 0, reach - 1)
    own_atom = jnp.clip(ids, 0, own - 1)
    below_atom = picked(side_halo[0, 0:1], below_slot)
    above_atom = picked(side_halo[1, 1:2], above_slot)
    is_own = ids < own
    is_below = ids < own + reach
    used = ids < own + 2 * reach
    atoms = jnp.where(
        is_own,
        ids,
        jnp.where(is_below, below_atom + own, jnp.where(used, above_atom + 2 * own, 3 * own)),
    )
    cartesian = []
    for axis in range(3):
        taken = jnp.where(
            is_own,
            picked(pos[axis : axis + 1], own_atom),
            jnp.where(
                is_below,
                picked(side_pos[0, axis : axis + 1], below_atom),
                picked(side_pos[1, axis : axis + 1], above_atom),
            ),
        )
        taken = jnp.where(used, taken, 0.0)
        offset = taken - pos[axis : axis + 1]
        offset = offset - jnp.floor(offset + 0.5)
        cartesian.append(offset * (side_length if axis < 2 else slab_depth * slab_count))
    distance = jnp.sqrt(
        cartesian[0] * cartesian[0] + cartesian[1] * cartesian[1] + cartesian[2] * cartesian[2]
    )
    limit = jnp.maximum(distance, distance_floor)
    direction = [part / limit for part in cartesian]

    radial_count = radial_weight.shape[0]
    spread = 1.5 * radial_reach / radial_count
    centers = lax.broadcasted_iota(jnp.int32, (radial_count, own), 0).astype(f32) * (
        radial_reach / (radial_count - 1)
    )
    numbers = lax.broadcasted_iota(jnp.int32, (3 * own, own), 0)

    def edges(j, sums):
        row = slice(j, j + 1)
        chosen = jnp.where(numbers == atoms[row], 1.0, 0.0).astype(bf16)
        gathered = jnp.dot(source_rows[...], chosen, preferred_element_type=f32)
        scaled = (distance[row] - centers) * (1.0 / spread)
        radial = jnp.exp(-(scaled * scaled)).astype(bf16)
        terms = gathered[: 3 * channels] * over_first(radial_weight[...], radial)
        first = terms[:channels]
        second = terms[channels : 2 * channels]
        third = terms[2 * channels :]
        new = [sums[0] + first]
        for axis in range(3):
            begin = (3 + axis) * channels
            new.append(
                sums[1 + axis]
                + gathered[begin : begin + channels] * second
                + third * direction[axis][row]
            )
        return new

    sums = [jnp.zeros((channels, own), f32)] * 4
    half = slots // 2
    for j in range(half):
        sums = edges(j, sums)

    for j in range(half, slots):
        sums = edges(j, sums)
    for axis in range(3):
        out_all[1 + axis] = (vec[axis].astype(f32) + sums[1 + axis]).astype(bf16)
    result = result + feat[...].astype(f32) + sums[0]

    wait_bytes(message_in_slots.at[pl.ds(1, peers - 1)], stage_sems.at[2])
    for d in range(1, peers):
        result = result + message_in_slots[d].astype(f32)
    out_all[0] = result.astype(bf16)
    wait_bytes(sent_total, send_sem.at[0])
    @pl.when(high > 0)
    def _():
        wait_bytes(stage_total.at[pl.ds(0, 3 * members - 4)], send_sem.at[1])

    @pl.when(high == 0)
    def _():
        wait_bytes(stage_total.at[pl.ds(0, 2 * members - 2)], send_sem.at[1])


def split_kernel(both, out_feat, out_vec, sems):
    feat_copy = pltpu.make_async_copy(both.at[0], out_feat, sems.at[0])
    vec_copy = pltpu.make_async_copy(both.at[pl.ds(1, 3)], out_vec, sems.at[0])
    feat_copy.start()
    vec_copy.start()
    feat_copy.wait()
    vec_copy.wait()


def shards(
    features,
    vectors,
    positions,
    neighbours,
    halo_lists,
    lattice,
    kspace_filter,
    node_weight,
    node_bias,
    message_weight,
    radial_weight,
    ewald_weight,
):
    n_dom, n_kb = lax.axis_size("dom"), lax.axis_size("kb")
    channels, own = features.shape
    reach = halo_lists.shape[1]
    width = kspace_filter.shape[1]
    low_count = 2 if n_dom % 2 == 0 else 1
    members, peers = n_dom // low_count, n_kb * low_count
    width = width // low_count
    chunk = width // members
    pair = 2 if n_kb % 2 == 0 else 1
    norm_scale = 1.0 / math.sqrt(lattice.shape[1] * own * n_dom * n_kb)
    row_bytes = 128 * 4
    block_bytes = channels * own * 2
    side_bytes = 2 * (4 * block_bytes + 3 * own * 4 + 2 * reach * 4)
    sent_bytes = side_bytes + (peers - 1) * (3 * own * 4 + 2 * block_bytes)
    vmem = pl.BlockSpec(memory_space=pltpu.VMEM)
    hbm = pl.BlockSpec(memory_space=pltpu.HBM)
    dma = pltpu.SemaphoreType.DMA
    bias_row = node_bias[None, :]

    def like(array):
        return pltpu.VMEM(array.shape, array.dtype)

    both = pl.pallas_call(
        functools.partial(kernel, (n_dom, n_kb, low_count, norm_scale)),
        out_shape=pltpu.VMEM((4, channels, own), bf16),
        in_specs=[hbm] * 12,
        out_specs=vmem,
        scratch_shapes=[
            like(features),
            like(vectors),
            like(positions),
            like(neighbours),
            pltpu.VMEM((3, width), jnp.int32),
            pltpu.VMEM((channels, width), f32),
            like(node_weight),
            like(bias_row),
            like(message_weight),
            like(radial_weight),
            like(ewald_weight),
            like(features),
            pltpu.VMEM((peers, channels, own), bf16),
            pltpu.VMEM((peers, 3, own), f32),
            pltpu.VMEM((2, 4, channels, own), bf16),
            pltpu.VMEM((2, 3, own), f32),
            pltpu.VMEM((2, 2, reach), jnp.int32),
            pltpu.VMEM((2 * width, peers * own), bf16),
            pltpu.VMEM((channels, 2 * width), f32),
            pltpu.VMEM((members, channels, 2 * chunk), bf16),
            pltpu.VMEM((members, channels, 2 * chunk), bf16),
            pltpu.VMEM((members - 1, members - 1, channels, 2 * chunk), bf16),
            pltpu.VMEM((members, channels, 2 * chunk), f32),
            pltpu.VMEM((members, channels, 2 * chunk), bf16),
            pltpu.VMEM((peers, channels, own), bf16),
            pltpu.VMEM((peers, channels, own), bf16),
            pltpu.VMEM((6 * channels, 3 * own), bf16),
            pltpu.VMEM((side_bytes // row_bytes, 1, 128), f32),
            pltpu.VMEM((sent_bytes // row_bytes, 1, 128), f32),
            pltpu.VMEM((3 * members, channels, 2 * chunk), bf16),
            pltpu.SemaphoreType.REGULAR((members - 1,)),
            dma((2,)),
            dma((peers // pair,)),
            dma((2,)),
            dma((1,)),
            dma((4,)),
            dma((2,)),
        ],
        compiler_params=pltpu.CompilerParams(collective_id=0, has_side_effects=True),
    )(
        features,
        vectors,
        positions,
        neighbours,
        halo_lists,
        lattice,
        kspace_filter,
        node_weight,
        bias_row,
        message_weight,
        radial_weight,
        ewald_weight,
    )
    return pl.pallas_call(
        split_kernel,
        out_shape=(
            jax.ShapeDtypeStruct(features.shape, bf16),
            jax.ShapeDtypeStruct(vectors.shape, bf16),
        ),
        in_specs=[vmem],
        out_specs=(pl.BlockSpec(memory_space=pl.ANY),) * 2,
        scratch_shapes=[dma((1,))],
    )(pltpu.with_memory_space_constraint(both, pltpu.VMEM))


def solution(mesh):
    atoms = P(None, ("dom", "kb"))
    placed = (
        atoms,
        P(None, None, ("dom", "kb")),
        atoms,
        atoms,
        atoms,
        P(),
        P(None, "kb"),
        P(),
        P(),
        P(),
        P(),
        P(),
    )
    return jax.shard_map(
        shards,
        mesh=mesh,
        in_specs=placed,
        out_specs=(atoms, P(None, None, ("dom", "kb"))),
        check_vma=False,
    )
```

```python
import functools
import math

import jax
import jax.numpy as jnp
import numpy as np
from jax import lax
from jax.experimental import pallas as pl
from jax.experimental.pallas import tpu as pltpu
from jax.sharding import PartitionSpec as P

side_length = 6.0
slab_depth = 6.0
radial_reach = 6.0
distance_floor = 1.0
MESH = pl.DeviceIdType.MESH
f32 = jnp.float32
bf16 = jnp.bfloat16


def polynomial(function, degree):
    nodes = (np.cos((np.arange(degree + 1) + 0.5) * np.pi / (degree + 1)) + 1.0) / 2.0
    fitted = np.polynomial.polynomial.polyfit(nodes, function(nodes / 4.0), degree)
    return [float(value * 4.0**power) for power, value in enumerate(fitted)]


half_cos = polynomial(lambda w: np.sqrt(2.0) * np.cos(np.pi * np.sqrt(w)), 3)
half_sin = polynomial(lambda w: np.sqrt(2.0) * np.sin(np.pi * np.sqrt(w)) / np.sqrt(w), 3)


def evaluate(terms, w):
    value = terms[-1] * w + terms[-2]
    for term in terms[-3::-1]:
        value = value * w + term
    return value


def turn_tables(turns):
    part = turns - jnp.round(turns)
    w = part * part
    sine = part * evaluate(half_sin, w)
    cosine = evaluate(half_cos, w)
    return (1.0 - sine * sine).astype(bf16), (sine * cosine).astype(bf16)


def over_first(first_operand, second_operand):
    return lax.dot_general(
        first_operand, second_operand, (((0,), (0,)), ((), ())), preferred_element_type=f32
    )


def three_parts(value):
    high = value.astype(bf16)
    rest = value - high.astype(f32)
    middle = rest.astype(bf16)
    low = (rest - middle.astype(f32)).astype(bf16)
    return high.astype(f32), middle.astype(f32), low.astype(f32)


def kernel(
    sizes,
    feat_hbm,
    vec_hbm,
    pos_hbm,
    nbr_hbm,
    halo_hbm,
    lat_hbm,
    kfilter_hbm,
    node_weight_hbm,
    node_bias_hbm,
    message_weight_hbm,
    radial_weight_hbm,
    ewald_weight_hbm,
    out_all,
    feat,
    vec,
    pos,
    nbr,
    lat,
    kfilter,
    node_weight,
    node_bias,
    message_weight,
    radial_weight,
    ewald_weight,
    own_projected,
    group_feat,
    group_pos,
    side_rows,
    side_pos,
    side_halo,
    tables,
    near_totals,
    totals_out,
    totals_in,
    totals_all,
    chunk_filters,
    filtered,
    message_out,
    message_in_slots,
    source_rows,
    side_total,
    sent_total,
    stage_total,
    round_sems,
    local_sems,
    pos_sems,
    feat_sems,
    side_sem,
    stage_sems,
    send_sem,
):
    n_dom, n_kb, low_count, norm_scale = sizes
    dom, kb = lax.axis_index("dom"), lax.axis_index("kb")
    rank = dom * n_kb + kb
    slab_count = n_dom * n_kb
    channels, own = feat.shape
    slots = nbr.shape[0]
    width = kfilter.shape[1]
    members = n_dom // low_count
    pair = 2 if n_kb % 2 == 0 else 1
    pairs = n_kb // pair
    high, low = lax.div(dom, low_count), lax.rem(dom, low_count)
    peers = n_kb * low_count
    chunk = width // members

    def slot_between(target, source):
        return 1 + source - jnp.where(source > target, 1, 0)

    def member(number):
        return {"dom": number * low_count + low, "kb": kb}

    def peer(slot, sign=1):
        core, across, side = slot % pair, slot // pair % pairs, slot // n_kb
        place = lax.rem(lax.div(kb, pair) + sign * across + pairs, pairs)
        return {
            "dom": high * low_count + lax.rem(low + side, low_count),
            "kb": place * pair + lax.rem(lax.rem(kb, pair) + core, pair),
        }

    others = list(range(1, peers))

    def slab(steps):
        number = lax.rem(rank + steps + slab_count, slab_count)
        return {"dom": lax.div(number, n_kb), "kb": lax.rem(number, n_kb)}

    def remote(source, target, send_sem, recv_sem, device):
        return pltpu.make_async_remote_copy(
            src_ref=source,
            dst_ref=target,
            send_sem=send_sem,
            recv_sem=recv_sem,
            device_id=device,
            device_id_type=MESH,
        )

    def wait_bytes(ref, sem):
        pltpu.make_async_copy(ref, ref, sem).wait()

    barrier = pltpu.get_barrier_semaphore()
    targets = [
        jnp.where(high == 0, members - 1 - index, index + jnp.where(index >= high, 1, 0))
        for index in range(members - 1)
    ]
    greeted = [peer(slot) for slot in range(peers - 1, 0, -1)]
    beside = [(-1, high > 0), (1, high < members - 1)]
    beside_count = sum(jnp.where(there, 1, 0) for steps, there in beside)

    def tell_beside(sem):
        for steps, there in beside:

            @pl.when(there)
            def _(steps=steps):
                pl.semaphore_signal(
                    sem, inc=1, device_id=member(high + steps), device_id_type=MESH
                )

    for device in greeted:
        pl.semaphore_signal(barrier, inc=1, device_id=device, device_id_type=MESH)
    tell_beside(barrier)
    is_last = rank == slab_count - 1

    @pl.when(rank == 0)
    def _():
        pl.semaphore_signal(barrier, inc=1, device_id=slab(-1), device_id_type=MESH)

    start = pl.multiple_of(kb * (width * low_count) + low * width, math.gcd(width, 128))
    filter_start = pl.multiple_of(low * width, math.gcd(width, 128))
    staged = [
        (feat_hbm, feat),
        (ewald_weight_hbm, ewald_weight),
        (pos_hbm, pos),
        (lat_hbm.at[:, pl.ds(start, width)], lat),
        (kfilter_hbm.at[:, pl.ds(filter_start, width)], kfilter),
        (node_weight_hbm, node_weight),
        (node_bias_hbm, node_bias),
        (message_weight_hbm, message_weight),
        (nbr_hbm, nbr),
        (radial_weight_hbm, radial_weight),
        (vec_hbm, vec),
    ]
    local = [
        pltpu.make_async_copy(source, target, local_sems.at[0 if i < 4 else 1])
        for i, (source, target) in enumerate(staged)
    ]
    for copy in local:
        copy.start()

    for copy in local[:4]:
        copy.wait()
    own_projected[...] = over_first(ewald_weight[...], feat[...]).astype(bf16)
    pl.semaphore_wait(barrier, len(greeted) + beside_count + jnp.where(is_last, 1, 0))
    pos_copies = [
        remote(pos, group_pos.at[slot], send_sem.at[0], pos_sems.at[slot // pair], peer(slot))
        for slot in others
    ]
    feat_copies = [
        remote(
            own_projected,
            group_feat.at[slot],
            send_sem.at[0],
            feat_sems.at[0 if slot < pair else 1],
            peer(slot),
        )
        for slot in others
    ]
    for copy in pos_copies[::-1] + feat_copies[::-1]:
        copy.start()
    rounds = members - 1
    tell_beside(round_sems.at[0])

    def pass_round(number):
        pl.semaphore_wait(round_sems.at[number], beside_count)
        if number + 1 < rounds:
            tell_beside(round_sems.at[number + 1])

    around = [(0, 1, is_last), (1, -1, rank == 0)]
    inside = [
        (side, steps, lax.div(rank + steps + peers, peers) == high + 1)
        for side, steps in ((0, 1), (1, -1))
    ]
    across = [
        (side, steps, jnp.logical_not(jnp.logical_or(ends, within)))
        for (side, steps, ends), (_, _, within) in zip(around, inside)
    ]

    def send_sides(cases):
        for side, steps, chosen in cases:

            @pl.when(chosen)
            def _(side=side, steps=steps):
                send_side(side, steps)


    def send_side(side, steps):
        device = slab(steps)
        for copy in (
            remote(feat_hbm, side_rows.at[side, 0], send_sem.at[0], side_sem.at[0], device),
            remote(
                vec_hbm,
                side_rows.at[side, pl.ds(1, 3)],
                send_sem.at[0],
                side_sem.at[0],
                device,
            ),
            remote(pos_hbm, side_pos.at[side], send_sem.at[0], side_sem.at[0], device),
            remote(halo_hbm, side_halo.at[side], send_sem.at[0], side_sem.at[0], device),
        ):
            copy.start()

    send_sides(around[:1])
    lattice = lat[...].astype(f32)
    lattice_high = jnp.floor(lattice[2:3] * 0.0625) * 16.0
    lattice_low = lattice[2:3] - lattice_high
    lattice_parts = jnp.concatenate(
        [lattice[0:1]] * 3
        + [lattice[1:2]] * 3
        + [lattice_high] * 3
        + [lattice_low] * 3
        + [jnp.zeros((4, width), f32)],
        axis=0,
    ).astype(bf16)

    def position_parts(coords):
        rows = []
        for axis in (0, 1, 2, 2):
            rows += list(three_parts(coords[axis : axis + 1]))
        rows.append(jnp.zeros((4, coords.shape[1]), f32))
        return jnp.concatenate(rows, axis=0).astype(bf16)

    def make_tables(first, coords):
        turns = over_first(lattice_parts, position_parts(coords))
        cosine, sine = turn_tables(turns)
        span = coords.shape[1]
        columns = pl.ds(pl.multiple_of(first * own, span), span)
        for number in range(members):
            rows = slice(number * chunk, (number + 1) * chunk)
            tables[2 * number * chunk : (2 * number + 1) * chunk, columns] = cosine[rows]
            tables[(2 * number + 1) * chunk : 2 * (number + 1) * chunk, columns] = sine[rows]

    def totals_of(first, features):
        return lax.dot_general(
            features,
            tables[:, first * own : first * own + features.shape[1]],
            (((1,), (1,)), ((), ())),
            preferred_element_type=f32,
        )

    make_tables(0, pos[...])
    def batch_features(first, count):
        return jnp.concatenate(
            [own_projected[...] if slot == 0 else group_feat[slot] for slot in range(first, first + count)],
            axis=1,
        )

    def wait_features(first, count):
        begin = max(first, 1)
        wait_bytes(
            group_feat.at[pl.ds(begin, first + count - begin)], feat_sems.at[0 if first < pair else 1]
        )

    for slot in range(1, pair):
        wait_bytes(group_pos.at[slot], pos_sems.at[0])
        make_tables(slot, group_pos[slot])
    if pair > 1:
        wait_features(0, pair)
    near_totals[...] = totals_of(0, batch_features(0, pair))
    pass_round(0)
    send_sides(across)
    order = list(range(1, peers // pair))
    if pairs == 2 and low_count == 2:
        place = lax.div(kb, pair)
        aligned = place == low
        order = [
            jnp.where(jnp.logical_and(place == 0, low == 1), 2, 1),
            jnp.where(aligned, 2, 3),
            jnp.where(aligned, 3, jnp.where(low == 1, 1, 2)),
        ]
    for batch in order:
        slots_of = [batch * pair + core for core in range(pair)]
        wait_bytes(
            group_pos.at[pl.ds(batch * pair, pair)],
            pos_sems.at[batch],
        )
        make_tables(
            batch * pair, jnp.concatenate([group_pos[slot] for slot in slots_of], axis=1)
        )
    wait_features(pair, peers - pair)
    totals = near_totals[...] + totals_of(pair, batch_features(pair, peers - pair))
    for number in range(members):
        totals_out[number] = totals[:, 2 * number * chunk : 2 * (number + 1) * chunk].astype(bf16)
    for number in range(1, rounds - 1):
        pass_round(number)
    def send_totals(number):
        remote(
            totals_out.at[number],
            totals_in.at[slot_between(number, high)],
            send_sem.at[1],
            stage_sems.at[0],
            member(number),
        ).start()

    for index in range(members - 1):
        number = jnp.where(
            index < high, lax.rem(high - index, jnp.maximum(high, 1)), index + 1
        )

        between = jnp.logical_and(number > 0, number < high)

        @pl.when(jnp.logical_not(between))
        def _(number=number):
            send_totals(number)

    @pl.when(high > 0)
    def _():
        remote(
            totals_out.at[pl.ds(1, members - 1)],
            totals_all.at[high - 1],
            send_sem.at[1],
            stage_sems.at[3],
            member(0),
        ).start()

    for step in range(1, members - 1):
        number = high - step

        @pl.when(number > 0)
        def _(number=number):
            send_totals(number)

    send_sides(inside)
    if rounds > 1:
        pass_round(rounds - 1)
    send_sides(around[1:])

    for copy in local[4:]:
        copy.wait()
    for number in range(members):
        part = kfilter[:, number * chunk : (number + 1) * chunk] * norm_scale
        chunk_filters[number] = jnp.concatenate([part, part], axis=1)
    bias = jnp.broadcast_to(node_bias[...], (own, channels)).T

    def fill_sources(index, one_feat, one_vec):
        columns = slice(index * own, (index + 1) * own)
        value = over_first(node_weight[...], one_feat[...]) + bias
        hidden = (value / (1.0 + jnp.exp(-value))).astype(bf16)
        source_rows[: 3 * channels, columns] = over_first(message_weight[...], hidden).astype(bf16)
        source_rows[3 * channels :, columns] = one_vec[...].reshape(3 * channels, own)

    fill_sources(0, feat, vec)
    def send_filtered(number):
        remote(
            filtered.at[high],
            filtered.at[high],
            send_sem.at[1],
            stage_sems.at[1],
            member(number),
        ).start()

    wait_bytes(totals_in.at[pl.ds(1, members - 1)], stage_sems.at[0])
    total = totals_out[high].astype(f32)
    for slot in range(1, members):
        total = total + totals_in[slot].astype(f32)
    filtered[high] = (chunk_filters[high] * total).astype(bf16)

    @pl.when(high > 0)
    def _():
        for index in range(members - 2):
            send_filtered(1 + index + jnp.where(index + 1 >= high, 1, 0))

    @pl.when(high == 0)
    def _():
        for number in range(members - 1, 0, -1):
            send_filtered(number)

    @pl.when(high == 0)
    def _():
        wait_bytes(totals_all, stage_sems.at[3])
        for number in range(1, members):
            total = totals_out[number].astype(f32)
            for source in range(members - 1):
                total = total + totals_all[source, number - 1].astype(f32)
            filtered[number] = (chunk_filters[number] * total).astype(bf16)

    @pl.when(high > 0)
    def _():
        wait_bytes(filtered.at[pl.ds(1, members - 1)], stage_sems.at[1])

    spectrum = jnp.concatenate([filtered[number] for number in range(members)], axis=1)
    def messages_of(first, last):
        return jnp.dot(
            spectrum, tables[:, first * own : last * own], preferred_element_type=f32
        )

    def send_message(slot, value):
        message_out[slot] = value.astype(bf16)
        remote(
            message_out.at[slot],
            message_in_slots.at[slot],
            send_sem.at[0],
            stage_sems.at[2],
            peer(slot, -1),
        ).start()

    group = pair * (2 if peers % (2 * pair) == 0 else 1)
    for first in range(peers - group, -1, -group):
        values = messages_of(first, first + group)
        for slot in range(first + group - 1, first - 1, -1):
            value = values[:, (slot - first) * own : (slot - first + 1) * own]
            if slot > 0:
                send_message(slot, value)
            else:
                result = value
    wait_bytes(side_total, side_sem.at[0])
    for side in range(2):
        fill_sources(1 + side, side_rows.at[side, 0], side_rows.at[side, pl.ds(1, 3)])
    ids = nbr[...]
    reach = side_halo.shape[2]

    def picked(row, index):
        return jnp.take_along_axis(
            jnp.broadcast_to(row, (slots, row.shape[1])), index, axis=1, mode="promise_in_bounds"
        )

    below_slot = jnp.clip(ids - own, 0, reach - 1)
    above_slot = jnp.clip(ids - (own + reach), 0, reach - 1)
    own_atom = jnp.clip(ids, 0, own - 1)
    below_atom = picked(side_halo[0, 0:1], below_slot)
    above_atom = picked(side_halo[1, 1:2], above_slot)
    is_own = ids < own
    is_below = ids < own + reach
    used = ids < own + 2 * reach
    atoms = jnp.where(
        is_own,
        ids,
        jnp.where(is_below, below_atom + own, jnp.where(used, above_atom + 2 * own, 3 * own)),
    )
    cartesian = []
    for axis in range(3):
        taken = jnp.where(
            is_own,
            picked(pos[axis : axis + 1], own_atom),
            jnp.where(
                is_below,
                picked(side_pos[0, axis : axis + 1], below_atom),
                picked(side_pos[1, axis : axis + 1], above_atom),
            ),
        )
        taken = jnp.where(used, taken, 0.0)
        offset = taken - pos[axis : axis + 1]
        offset = offset - jnp.floor(offset + 0.5)
        cartesian.append(offset * (side_length if axis < 2 else slab_depth * slab_count))
    distance = jnp.sqrt(
        cartesian[0] * cartesian[0] + cartesian[1] * cartesian[1] + cartesian[2] * cartesian[2]
    )
    limit = jnp.maximum(distance, distance_floor)
    direction = [part / limit for part in cartesian]

    radial_count = radial_weight.shape[0]
    spread = 1.5 * radial_reach / radial_count
    centers = lax.broadcasted_iota(jnp.int32, (radial_count, own), 0).astype(f32) * (
        radial_reach / (radial_count - 1)
    )
    numbers = lax.broadcasted_iota(jnp.int32, (3 * own, own), 0)

    def edges(j, sums):
        row = slice(j, j + 1)
        chosen = jnp.where(numbers == atoms[row], 1.0, 0.0).astype(bf16)
        gathered = jnp.dot(source_rows[...], chosen, preferred_element_type=f32)
        scaled = (distance[row] - centers) * (1.0 / spread)
        radial = jnp.exp(-(scaled * scaled)).astype(bf16)
        terms = gathered[: 3 * channels] * over_first(radial_weight[...], radial)
        first = terms[:channels]
        second = terms[channels : 2 * channels]
        third = terms[2 * channels :]
        new = [sums[0] + first]
        for axis in range(3):
            begin = (3 + axis) * channels
            new.append(
                sums[1 + axis]
                + gathered[begin : begin + channels] * second
                + third * direction[axis][row]
            )
        return new

    sums = [jnp.zeros((channels, own), f32)] * 4
    half = slots // 2
    for j in range(half):
        sums = edges(j, sums)

    for j in range(half, slots):
        sums = edges(j, sums)
    for axis in range(3):
        out_all[1 + axis] = (vec[axis].astype(f32) + sums[1 + axis]).astype(bf16)
    result = result + feat[...].astype(f32) + sums[0]

    wait_bytes(message_in_slots.at[pl.ds(1, peers - 1)], stage_sems.at[2])
    for d in range(1, peers):
        result = result + message_in_slots[d].astype(f32)
    out_all[0] = result.astype(bf16)
    wait_bytes(sent_total, send_sem.at[0])
    @pl.when(high > 0)
    def _():
        wait_bytes(stage_total.at[pl.ds(0, 3 * members - 4)], send_sem.at[1])

    @pl.when(high == 0)
    def _():
        wait_bytes(stage_total.at[pl.ds(0, 2 * members - 2)], send_sem.at[1])


def split_kernel(both, out_feat, out_vec, sems):
    feat_copy = pltpu.make_async_copy(both.at[0], out_feat, sems.at[0])
    vec_copy = pltpu.make_async_copy(both.at[pl.ds(1, 3)], out_vec, sems.at[0])
    feat_copy.start()
    vec_copy.start()
    feat_copy.wait()
    vec_copy.wait()


def shards(
    features,
    vectors,
    positions,
    neighbours,
    halo_lists,
    lattice,
    kspace_filter,
    node_weight,
    node_bias,
    message_weight,
    radial_weight,
    ewald_weight,
):
    n_dom, n_kb = lax.axis_size("dom"), lax.axis_size("kb")
    channels, own = features.shape
    reach = halo_lists.shape[1]
    width = kspace_filter.shape[1]
    low_count = 2 if n_dom % 2 == 0 else 1
    members, peers = n_dom // low_count, n_kb * low_count
    width = width // low_count
    chunk = width // members
    pair = 2 if n_kb % 2 == 0 else 1
    norm_scale = 1.0 / math.sqrt(lattice.shape[1] * own * n_dom * n_kb)
    row_bytes = 128 * 4
    block_bytes = channels * own * 2
    side_bytes = 2 * (4 * block_bytes + 3 * own * 4 + 2 * reach * 4)
    sent_bytes = side_bytes + (peers - 1) * (3 * own * 4 + 2 * block_bytes)
    vmem = pl.BlockSpec(memory_space=pltpu.VMEM)
    hbm = pl.BlockSpec(memory_space=pltpu.HBM)
    dma = pltpu.SemaphoreType.DMA
    bias_row = node_bias[None, :]

    def like(array):
        return pltpu.VMEM(array.shape, array.dtype)

    both = pl.pallas_call(
        functools.partial(kernel, (n_dom, n_kb, low_count, norm_scale)),
        out_shape=pltpu.VMEM((4, channels, own), bf16),
        in_specs=[hbm] * 12,
        out_specs=vmem,
        scratch_shapes=[
            like(features),
            like(vectors),
            like(positions),
            like(neighbours),
            pltpu.VMEM((3, width), jnp.int32),
            pltpu.VMEM((channels, width), f32),
            like(node_weight),
            like(bias_row),
            like(message_weight),
            like(radial_weight),
            like(ewald_weight),
            like(features),
            pltpu.VMEM((peers, channels, own), bf16),
            pltpu.VMEM((peers, 3, own), f32),
            pltpu.VMEM((2, 4, channels, own), bf16),
            pltpu.VMEM((2, 3, own), f32),
            pltpu.VMEM((2, 2, reach), jnp.int32),
            pltpu.VMEM((2 * width, peers * own), bf16),
            pltpu.VMEM((channels, 2 * width), f32),
            pltpu.VMEM((members, channels, 2 * chunk), bf16),
            pltpu.VMEM((members, channels, 2 * chunk), bf16),
            pltpu.VMEM((members - 1, members - 1, channels, 2 * chunk), bf16),
            pltpu.VMEM((members, channels, 2 * chunk), f32),
            pltpu.VMEM((members, channels, 2 * chunk), bf16),
            pltpu.VMEM((peers, channels, own), bf16),
            pltpu.VMEM((peers, channels, own), bf16),
            pltpu.VMEM((6 * channels, 3 * own), bf16),
            pltpu.VMEM((side_bytes // row_bytes, 1, 128), f32),
            pltpu.VMEM((sent_bytes // row_bytes, 1, 128), f32),
            pltpu.VMEM((3 * members, channels, 2 * chunk), bf16),
            pltpu.SemaphoreType.REGULAR((members - 1,)),
            dma((2,)),
            dma((peers // pair,)),
            dma((2,)),
            dma((1,)),
            dma((4,)),
            dma((2,)),
        ],
        compiler_params=pltpu.CompilerParams(collective_id=0, has_side_effects=True),
    )(
        features,
        vectors,
        positions,
        neighbours,
        halo_lists,
        lattice,
        kspace_filter,
        node_weight,
        bias_row,
        message_weight,
        radial_weight,
        ewald_weight,
    )
    return pl.pallas_call(
        split_kernel,
        out_shape=(
            jax.ShapeDtypeStruct(features.shape, bf16),
            jax.ShapeDtypeStruct(vectors.shape, bf16),
        ),
        in_specs=[vmem],
        out_specs=(pl.BlockSpec(memory_space=pl.ANY),) * 2,
        scratch_shapes=[dma((1,))],
    )(pltpu.with_memory_space_constraint(both, pltpu.VMEM))


def solution(mesh):
    atoms = P(None, ("dom", "kb"))
    placed = (
        atoms,
        P(None, None, ("dom", "kb")),
        atoms,
        atoms,
        atoms,
        P(),
        P(None, "kb"),
        P(),
        P(),
        P(),
        P(),
        P(),
    )
    return jax.shard_map(
        shards,
        mesh=mesh,
        in_specs=placed,
        out_specs=(atoms, P(None, None, ("dom", "kb"))),
        check_vma=False,
    )
```

```python
import functools
import math

import jax
import jax.numpy as jnp
import numpy as np
from jax import lax
from jax.experimental import pallas as pl
from jax.experimental.pallas import tpu as pltpu
from jax.sharding import PartitionSpec as P

side_length = 6.0
slab_depth = 6.0
radial_reach = 6.0
distance_floor = 1.0
MESH = pl.DeviceIdType.MESH
f32 = jnp.float32
bf16 = jnp.bfloat16


def polynomial(function, degree):
    nodes = (np.cos((np.arange(degree + 1) + 0.5) * np.pi / (degree + 1)) + 1.0) / 2.0
    fitted = np.polynomial.polynomial.polyfit(nodes, function(nodes / 4.0), degree)
    return [float(value * 4.0**power) for power, value in enumerate(fitted)]


half_cos = polynomial(lambda w: np.sqrt(2.0) * np.cos(np.pi * np.sqrt(w)), 3)
half_sin = polynomial(lambda w: np.sqrt(2.0) * np.sin(np.pi * np.sqrt(w)) / np.sqrt(w), 3)


def evaluate(terms, w):
    value = terms[-1] * w + terms[-2]
    for term in terms[-3::-1]:
        value = value * w + term
    return value


def turn_tables(turns):
    part = turns - jnp.round(turns)
    w = part * part
    sine = part * evaluate(half_sin, w)
    cosine = evaluate(half_cos, w)
    return (1.0 - sine * sine).astype(bf16), (sine * cosine).astype(bf16)


def over_first(first_operand, second_operand):
    return lax.dot_general(
        first_operand, second_operand, (((0,), (0,)), ((), ())), preferred_element_type=f32
    )


def three_parts(value):
    high = value.astype(bf16)
    rest = value - high.astype(f32)
    middle = rest.astype(bf16)
    low = (rest - middle.astype(f32)).astype(bf16)
    return high.astype(f32), middle.astype(f32), low.astype(f32)


def kernel(
    sizes,
    feat_hbm,
    vec_hbm,
    pos_hbm,
    nbr_hbm,
    halo_hbm,
    lat_hbm,
    kfilter_hbm,
    node_weight_hbm,
    node_bias_hbm,
    message_weight_hbm,
    radial_weight_hbm,
    ewald_weight_hbm,
    out_all,
    feat,
    vec,
    pos,
    nbr,
    lat,
    kfilter,
    node_weight,
    node_bias,
    message_weight,
    radial_weight,
    ewald_weight,
    own_projected,
    group_feat,
    group_pos,
    side_rows,
    side_pos,
    side_halo,
    tables,
    near_totals,
    totals_out,
    totals_in,
    totals_all,
    chunk_filters,
    filtered,
    message_out,
    message_in_slots,
    source_rows,
    side_total,
    sent_total,
    stage_total,
    round_sems,
    local_sems,
    pos_sems,
    feat_sems,
    side_sem,
    stage_sems,
    send_sem,
):
    n_dom, n_kb, low_count, norm_scale = sizes
    dom, kb = lax.axis_index("dom"), lax.axis_index("kb")
    rank = dom * n_kb + kb
    slab_count = n_dom * n_kb
    channels, own = feat.shape
    slots = nbr.shape[0]
    width = kfilter.shape[1]
    members = n_dom // low_count
    pair = 2 if n_kb % 2 == 0 else 1
    pairs = n_kb // pair
    high, low = lax.div(dom, low_count), lax.rem(dom, low_count)
    peers = n_kb * low_count
    chunk = width // members

    def slot_between(target, source):
        return 1 + source - jnp.where(source > target, 1, 0)

    def member(number):
        return {"dom": number * low_count + low, "kb": kb}

    def peer(slot, sign=1):
        core, across, side = slot % pair, slot // pair % pairs, slot // n_kb
        place = lax.rem(lax.div(kb, pair) + sign * across + pairs, pairs)
        return {
            "dom": high * low_count + lax.rem(low + side, low_count),
            "kb": place * pair + lax.rem(lax.rem(kb, pair) + core, pair),
        }

    others = list(range(1, peers))

    def slab(steps):
        number = lax.rem(rank + steps + slab_count, slab_count)
        return {"dom": lax.div(number, n_kb), "kb": lax.rem(number, n_kb)}

    def remote(source, target, send_sem, recv_sem, device):
        return pltpu.make_async_remote_copy(
            src_ref=source,
            dst_ref=target,
            send_sem=send_sem,
            recv_sem=recv_sem,
            device_id=device,
            device_id_type=MESH,
        )

    def wait_bytes(ref, sem):
        pltpu.make_async_copy(ref, ref, sem).wait()

    barrier = pltpu.get_barrier_semaphore()
    targets = [
        jnp.where(high == 0, members - 1 - index, index + jnp.where(index >= high, 1, 0))
        for index in range(members - 1)
    ]
    greeted = [peer(slot) for slot in range(peers - 1, 0, -1)]
    beside = [(-1, high > 0), (1, high < members - 1)]
    beside_count = sum(jnp.where(there, 1, 0) for steps, there in beside)

    def tell_beside(sem):
        for steps, there in beside:

            @pl.when(there)
            def _(steps=steps):
                pl.semaphore_signal(
                    sem, inc=1, device_id=member(high + steps), device_id_type=MESH
                )

    for device in greeted:
        pl.semaphore_signal(barrier, inc=1, device_id=device, device_id_type=MESH)
    tell_beside(barrier)
    is_last = rank == slab_count - 1

    @pl.when(rank == 0)
    def _():
        pl.semaphore_signal(barrier, inc=1, device_id=slab(-1), device_id_type=MESH)

    start = pl.multiple_of(kb * (width * low_count) + low * width, math.gcd(width, 128))
    filter_start = pl.multiple_of(low * width, math.gcd(width, 128))
    staged = [
        (feat_hbm, feat),
        (ewald_weight_hbm, ewald_weight),
        (pos_hbm, pos),
        (lat_hbm.at[:, pl.ds(start, width)], lat),
        (kfilter_hbm.at[:, pl.ds(filter_start, width)], kfilter),
        (node_weight_hbm, node_weight),
        (node_bias_hbm, node_bias),
        (message_weight_hbm, message_weight),
        (nbr_hbm, nbr),
        (radial_weight_hbm, radial_weight),
        (vec_hbm, vec),
    ]
    local = [
        pltpu.make_async_copy(source, target, local_sems.at[0 if i < 4 else 1])
        for i, (source, target) in enumerate(staged)
    ]
    for copy in local:
        copy.start()

    for copy in local[:4]:
        copy.wait()
    own_projected[...] = over_first(ewald_weight[...], feat[...]).astype(bf16)
    pl.semaphore_wait(barrier, len(greeted) + beside_count + jnp.where(is_last, 1, 0))
    pos_copies = [
        remote(pos, group_pos.at[slot], send_sem.at[0], pos_sems.at[slot // pair], peer(slot))
        for slot in others
    ]
    feat_copies = [
        remote(
            own_projected,
            group_feat.at[slot],
            send_sem.at[0],
            feat_sems.at[0 if slot < pair else 1],
            peer(slot),
        )
        for slot in others
    ]
    for copy in pos_copies[::-1] + feat_copies[::-1]:
        copy.start()
    rounds = members - 2
    tell_beside(round_sems.at[0])

    def pass_round(number):
        pl.semaphore_wait(round_sems.at[number], beside_count)
        if number + 1 < rounds:
            tell_beside(round_sems.at[number + 1])

    around = [(0, 1, is_last), (1, -1, rank == 0)]
    inside = [
        (side, steps, lax.div(rank + steps + peers, peers) == high + 1)
        for side, steps in ((0, 1), (1, -1))
    ]
    across = [
        (side, steps, jnp.logical_not(jnp.logical_or(ends, within)))
        for (side, steps, ends), (_, _, within) in zip(around, inside)
    ]

    def send_sides(cases):
        for side, steps, chosen in cases:

            @pl.when(chosen)
            def _(side=side, steps=steps):
                send_side(side, steps)


    def send_side(side, steps):
        device = slab(steps)
        for copy in (
            remote(feat_hbm, side_rows.at[side, 0], send_sem.at[0], side_sem.at[0], device),
            remote(
                vec_hbm,
                side_rows.at[side, pl.ds(1, 3)],
                send_sem.at[0],
                side_sem.at[0],
                device,
            ),
            remote(pos_hbm, side_pos.at[side], send_sem.at[0], side_sem.at[0], device),
            remote(halo_hbm, side_halo.at[side], send_sem.at[0], side_sem.at[0], device),
        ):
            copy.start()

    send_sides(around[:1])
    lattice = lat[...].astype(f32)
    lattice_high = jnp.floor(lattice[2:3] * 0.0625) * 16.0
    lattice_low = lattice[2:3] - lattice_high
    lattice_parts = jnp.concatenate(
        [lattice[0:1]] * 3
        + [lattice[1:2]] * 3
        + [lattice_high] * 3
        + [lattice_low] * 3
        + [jnp.zeros((4, width), f32)],
        axis=0,
    ).astype(bf16)

    def position_parts(coords):
        rows = []
        for axis in (0, 1, 2, 2):
            rows += list(three_parts(coords[axis : axis + 1]))
        rows.append(jnp.zeros((4, coords.shape[1]), f32))
        return jnp.concatenate(rows, axis=0).astype(bf16)

    def make_tables(first, coords):
        turns = over_first(lattice_parts, position_parts(coords))
        cosine, sine = turn_tables(turns)
        span = coords.shape[1]
        columns = pl.ds(pl.multiple_of(first * own, span), span)
        for number in range(members):
            rows = slice(number * chunk, (number + 1) * chunk)
            tables[2 * number * chunk : (2 * number + 1) * chunk, columns] = cosine[rows]
            tables[(2 * number + 1) * chunk : 2 * (number + 1) * chunk, columns] = sine[rows]

    def totals_of(first, features):
        return lax.dot_general(
            features,
            tables[:, first * own : first * own + features.shape[1]],
            (((1,), (1,)), ((), ())),
            preferred_element_type=f32,
        )

    make_tables(0, pos[...])
    def batch_features(first, count):
        return jnp.concatenate(
            [own_projected[...] if slot == 0 else group_feat[slot] for slot in range(first, first + count)],
            axis=1,
        )

    def wait_features(first, count):
        begin = max(first, 1)
        wait_bytes(
            group_feat.at[pl.ds(begin, first + count - begin)], feat_sems.at[0 if first < pair else 1]
        )

    for slot in range(1, pair):
        wait_bytes(group_pos.at[slot], pos_sems.at[0])
        make_tables(slot, group_pos[slot])
    if pair > 1:
        wait_features(0, pair)
    near_totals[...] = totals_of(0, batch_features(0, pair))
    pass_round(0)
    send_sides(across)
    order = list(range(1, peers // pair))
    if pairs == 2 and low_count == 2:
        place = lax.div(kb, pair)
        aligned = place == low
        order = [
            jnp.where(jnp.logical_and(place == 0, low == 1), 2, 1),
            jnp.where(aligned, 2, 3),
            jnp.where(aligned, 3, jnp.where(low == 1, 1, 2)),
        ]
    for batch in order:
        slots_of = [batch * pair + core for core in range(pair)]
        wait_bytes(
            group_pos.at[pl.ds(batch * pair, pair)],
            pos_sems.at[batch],
        )
        make_tables(
            batch * pair, jnp.concatenate([group_pos[slot] for slot in slots_of], axis=1)
        )
    wait_features(pair, peers - pair)
    totals = near_totals[...] + totals_of(pair, batch_features(pair, peers - pair))
    for number in range(members):
        totals_out[number] = totals[:, 2 * number * chunk : 2 * (number + 1) * chunk].astype(bf16)
    for number in range(1, rounds):
        pass_round(number)
    def send_totals(number):
        remote(
            totals_out.at[number],
            totals_in.at[slot_between(number, high)],
            send_sem.at[1],
            stage_sems.at[0],
            member(number),
        ).start()

    for index in range(members - 1):
        number = jnp.where(
            index < high, lax.rem(high - index, jnp.maximum(high, 1)), index + 1
        )

        between = jnp.logical_and(number > 0, number < high)

        @pl.when(jnp.logical_not(between))
        def _(number=number):
            send_totals(number)

    @pl.when(high > 0)
    def _():
        remote(
            totals_out.at[pl.ds(1, members - 1)],
            totals_all.at[high - 1],
            send_sem.at[1],
            stage_sems.at[3],
            member(0),
        ).start()

    for step in range(1, members - 1):
        number = high - step

        @pl.when(number > 0)
        def _(number=number):
            send_totals(number)

    send_sides(inside)
    for copy in local[4:]:
        copy.wait()
    for number in range(members):
        part = kfilter[:, number * chunk : (number + 1) * chunk] * norm_scale
        chunk_filters[number] = jnp.concatenate([part, part], axis=1)
    bias = jnp.broadcast_to(node_bias[...], (own, channels)).T

    def fill_sources(index, one_feat, one_vec):
        columns = slice(index * own, (index + 1) * own)
        value = over_first(node_weight[...], one_feat[...]) + bias
        hidden = (value / (1.0 + jnp.exp(-value))).astype(bf16)
        source_rows[: 3 * channels, columns] = over_first(message_weight[...], hidden).astype(bf16)
        source_rows[3 * channels :, columns] = one_vec[...].reshape(3 * channels, own)

    fill_sources(0, feat, vec)
    def send_filtered(number):
        remote(
            filtered.at[high],
            filtered.at[high],
            send_sem.at[1],
            stage_sems.at[1],
            member(number),
        ).start()

    wait_bytes(totals_in.at[pl.ds(1, members - 1)], stage_sems.at[0])
    total = totals_out[high].astype(f32)
    for slot in range(1, members):
        total = total + totals_in[slot].astype(f32)
    filtered[high] = (chunk_filters[high] * total).astype(bf16)

    @pl.when(high > 0)
    def _():
        for index in range(members - 2):
            send_filtered(1 + index + jnp.where(index + 1 >= high, 1, 0))

    @pl.when(high == 0)
    def _():
        for number in range(members - 1, 0, -1):
            send_filtered(number)

    send_sides(around[1:])
    @pl.when(high == 0)
    def _():
        wait_bytes(totals_all, stage_sems.at[3])
        for number in range(1, members):
            total = totals_out[number].astype(f32)
            for source in range(members - 1):
                total = total + totals_all[source, number - 1].astype(f32)
            filtered[number] = (chunk_filters[number] * total).astype(bf16)

    @pl.when(high > 0)
    def _():
        wait_bytes(filtered.at[pl.ds(1, members - 1)], stage_sems.at[1])

    spectrum = jnp.concatenate([filtered[number] for number in range(members)], axis=1)
    def messages_of(first, last):
        return jnp.dot(
            spectrum, tables[:, first * own : last * own], preferred_element_type=f32
        )

    def send_message(slot, value):
        message_out[slot] = value.astype(bf16)
        remote(
            message_out.at[slot],
            message_in_slots.at[slot],
            send_sem.at[0],
            stage_sems.at[2],
            peer(slot, -1),
        ).start()

    group = pair * (2 if peers % (2 * pair) == 0 else 1)
    for first in range(peers - group, -1, -group):
        values = messages_of(first, first + group)
        for slot in range(first + group - 1, first - 1, -1):
            value = values[:, (slot - first) * own : (slot - first + 1) * own]
            if slot > 0:
                send_message(slot, value)
            else:
                result = value
    wait_bytes(side_total, side_sem.at[0])
    for side in range(2):
        fill_sources(1 + side, side_rows.at[side, 0], side_rows.at[side, pl.ds(1, 3)])
    ids = nbr[...]
    reach = side_halo.shape[2]

    def picked(row, index):
        return jnp.take_along_axis(
            jnp.broadcast_to(row, (slots, row.shape[1])), index, axis=1, mode="promise_in_bounds"
        )

    below_slot = jnp.clip(ids - own, 0, reach - 1)
    above_slot = jnp.clip(ids - (own + reach), 0, reach - 1)
    own_atom = jnp.clip(ids, 0, own - 1)
    below_atom = picked(side_halo[0, 0:1], below_slot)
    above_atom = picked(side_halo[1, 1:2], above_slot)
    is_own = ids < own
    is_below = ids < own + reach
    used = ids < own + 2 * reach
    atoms = jnp.where(
        is_own,
        ids,
        jnp.where(is_below, below_atom + own, jnp.where(used, above_atom + 2 * own, 3 * own)),
    )
    cartesian = []
    for axis in range(3):
        taken = jnp.where(
            is_own,
            picked(pos[axis : axis + 1], own_atom),
            jnp.where(
                is_below,
                picked(side_pos[0, axis : axis + 1], below_atom),
                picked(side_pos[1, axis : axis + 1], above_atom),
            ),
        )
        taken = jnp.where(used, taken, 0.0)
        offset = taken - pos[axis : axis + 1]
        offset = offset - jnp.floor(offset + 0.5)
        cartesian.append(offset * (side_length if axis < 2 else slab_depth * slab_count))
    distance = jnp.sqrt(
        cartesian[0] * cartesian[0] + cartesian[1] * cartesian[1] + cartesian[2] * cartesian[2]
    )
    limit = jnp.maximum(distance, distance_floor)
    direction = [part / limit for part in cartesian]

    radial_count = radial_weight.shape[0]
    spread = 1.5 * radial_reach / radial_count
    centers = lax.broadcasted_iota(jnp.int32, (radial_count, own), 0).astype(f32) * (
        radial_reach / (radial_count - 1)
    )
    numbers = lax.broadcasted_iota(jnp.int32, (3 * own, own), 0)

    def edges(j, sums):
        row = slice(j, j + 1)
        chosen = jnp.where(numbers == atoms[row], 1.0, 0.0).astype(bf16)
        gathered = jnp.dot(source_rows[...], chosen, preferred_element_type=f32)
        scaled = (distance[row] - centers) * (1.0 / spread)
        radial = jnp.exp(-(scaled * scaled)).astype(bf16)
        terms = gathered[: 3 * channels] * over_first(radial_weight[...], radial)
        first = terms[:channels]
        second = terms[channels : 2 * channels]
        third = terms[2 * channels :]
        new = [sums[0] + first]
        for axis in range(3):
            begin = (3 + axis) * channels
            new.append(
                sums[1 + axis]
                + gathered[begin : begin + channels] * second
                + third * direction[axis][row]
            )
        return new

    sums = [jnp.zeros((channels, own), f32)] * 4
    half = slots // 2
    for j in range(half):
        sums = edges(j, sums)

    for j in range(half, slots):
        sums = edges(j, sums)
    for axis in range(3):
        out_all[1 + axis] = (vec[axis].astype(f32) + sums[1 + axis]).astype(bf16)
    result = result + feat[...].astype(f32) + sums[0]

    wait_bytes(message_in_slots.at[pl.ds(1, peers - 1)], stage_sems.at[2])
    for d in range(1, peers):
        result = result + message_in_slots[d].astype(f32)
    out_all[0] = result.astype(bf16)
    wait_bytes(sent_total, send_sem.at[0])
    @pl.when(high > 0)
    def _():
        wait_bytes(stage_total.at[pl.ds(0, 3 * members - 4)], send_sem.at[1])

    @pl.when(high == 0)
    def _():
        wait_bytes(stage_total.at[pl.ds(0, 2 * members - 2)], send_sem.at[1])


def split_kernel(both, out_feat, out_vec, sems):
    feat_copy = pltpu.make_async_copy(both.at[0], out_feat, sems.at[0])
    vec_copy = pltpu.make_async_copy(both.at[pl.ds(1, 3)], out_vec, sems.at[0])
    feat_copy.start()
    vec_copy.start()
    feat_copy.wait()
    vec_copy.wait()


def shards(
    features,
    vectors,
    positions,
    neighbours,
    halo_lists,
    lattice,
    kspace_filter,
    node_weight,
    node_bias,
    message_weight,
    radial_weight,
    ewald_weight,
):
    n_dom, n_kb = lax.axis_size("dom"), lax.axis_size("kb")
    channels, own = features.shape
    reach = halo_lists.shape[1]
    width = kspace_filter.shape[1]
    low_count = 2 if n_dom % 2 == 0 else 1
    members, peers = n_dom // low_count, n_kb * low_count
    width = width // low_count
    chunk = width // members
    pair = 2 if n_kb % 2 == 0 else 1
    norm_scale = 1.0 / math.sqrt(lattice.shape[1] * own * n_dom * n_kb)
    row_bytes = 128 * 4
    block_bytes = channels * own * 2
    side_bytes = 2 * (4 * block_bytes + 3 * own * 4 + 2 * reach * 4)
    sent_bytes = side_bytes + (peers - 1) * (3 * own * 4 + 2 * block_bytes)
    vmem = pl.BlockSpec(memory_space=pltpu.VMEM)
    hbm = pl.BlockSpec(memory_space=pltpu.HBM)
    dma = pltpu.SemaphoreType.DMA
    bias_row = node_bias[None, :]

    def like(array):
        return pltpu.VMEM(array.shape, array.dtype)

    both = pl.pallas_call(
        functools.partial(kernel, (n_dom, n_kb, low_count, norm_scale)),
        out_shape=pltpu.VMEM((4, channels, own), bf16),
        in_specs=[hbm] * 12,
        out_specs=vmem,
        scratch_shapes=[
            like(features),
            like(vectors),
            like(positions),
            like(neighbours),
            pltpu.VMEM((3, width), jnp.int32),
            pltpu.VMEM((channels, width), f32),
            like(node_weight),
            like(bias_row),
            like(message_weight),
            like(radial_weight),
            like(ewald_weight),
            like(features),
            pltpu.VMEM((peers, channels, own), bf16),
            pltpu.VMEM((peers, 3, own), f32),
            pltpu.VMEM((2, 4, channels, own), bf16),
            pltpu.VMEM((2, 3, own), f32),
            pltpu.VMEM((2, 2, reach), jnp.int32),
            pltpu.VMEM((2 * width, peers * own), bf16),
            pltpu.VMEM((channels, 2 * width), f32),
            pltpu.VMEM((members, channels, 2 * chunk), bf16),
            pltpu.VMEM((members, channels, 2 * chunk), bf16),
            pltpu.VMEM((members - 1, members - 1, channels, 2 * chunk), bf16),
            pltpu.VMEM((members, channels, 2 * chunk), f32),
            pltpu.VMEM((members, channels, 2 * chunk), bf16),
            pltpu.VMEM((peers, channels, own), bf16),
            pltpu.VMEM((peers, channels, own), bf16),
            pltpu.VMEM((6 * channels, 3 * own), bf16),
            pltpu.VMEM((side_bytes // row_bytes, 1, 128), f32),
            pltpu.VMEM((sent_bytes // row_bytes, 1, 128), f32),
            pltpu.VMEM((3 * members, channels, 2 * chunk), bf16),
            pltpu.SemaphoreType.REGULAR((members - 2,)),
            dma((2,)),
            dma((peers // pair,)),
            dma((2,)),
            dma((1,)),
            dma((4,)),
            dma((2,)),
        ],
        compiler_params=pltpu.CompilerParams(collective_id=0, has_side_effects=True),
    )(
        features,
        vectors,
        positions,
        neighbours,
        halo_lists,
        lattice,
        kspace_filter,
        node_weight,
        bias_row,
        message_weight,
        radial_weight,
        ewald_weight,
    )
    return pl.pallas_call(
        split_kernel,
        out_shape=(
            jax.ShapeDtypeStruct(features.shape, bf16),
            jax.ShapeDtypeStruct(vectors.shape, bf16),
        ),
        in_specs=[vmem],
        out_specs=(pl.BlockSpec(memory_space=pl.ANY),) * 2,
        scratch_shapes=[dma((1,))],
    )(pltpu.with_memory_space_constraint(both, pltpu.VMEM))


def solution(mesh):
    atoms = P(None, ("dom", "kb"))
    placed = (
        atoms,
        P(None, None, ("dom", "kb")),
        atoms,
        atoms,
        atoms,
        P(),
        P(None, "kb"),
        P(),
        P(),
        P(),
        P(),
        P(),
    )
    return jax.shard_map(
        shards,
        mesh=mesh,
        in_specs=placed,
        out_specs=(atoms, P(None, None, ("dom", "kb"))),
        check_vma=False,
    )
```

```python
import functools
import math

import jax
import jax.numpy as jnp
import numpy as np
from jax import lax
from jax.experimental import pallas as pl
from jax.experimental.pallas import tpu as pltpu
from jax.sharding import PartitionSpec as P

side_length = 6.0
slab_depth = 6.0
radial_reach = 6.0
distance_floor = 1.0
MESH = pl.DeviceIdType.MESH
f32 = jnp.float32
bf16 = jnp.bfloat16


def polynomial(function, degree):
    nodes = (np.cos((np.arange(degree + 1) + 0.5) * np.pi / (degree + 1)) + 1.0) / 2.0
    fitted = np.polynomial.polynomial.polyfit(nodes, function(nodes / 4.0), degree)
    return [float(value * 4.0**power) for power, value in enumerate(fitted)]


half_cos = polynomial(lambda w: np.sqrt(2.0) * np.cos(np.pi * np.sqrt(w)), 3)
half_sin = polynomial(lambda w: np.sqrt(2.0) * np.sin(np.pi * np.sqrt(w)) / np.sqrt(w), 3)


def evaluate(terms, w):
    value = terms[-1] * w + terms[-2]
    for term in terms[-3::-1]:
        value = value * w + term
    return value


def turn_tables(turns):
    part = turns - jnp.round(turns)
    w = part * part
    sine = part * evaluate(half_sin, w)
    cosine = evaluate(half_cos, w)
    return (1.0 - sine * sine).astype(bf16), (sine * cosine).astype(bf16)


def over_first(first_operand, second_operand):
    return lax.dot_general(
        first_operand, second_operand, (((0,), (0,)), ((), ())), preferred_element_type=f32
    )


def three_parts(value):
    high = value.astype(bf16)
    rest = value - high.astype(f32)
    middle = rest.astype(bf16)
    low = (rest - middle.astype(f32)).astype(bf16)
    return high.astype(f32), middle.astype(f32), low.astype(f32)


def kernel(
    sizes,
    feat_hbm,
    vec_hbm,
    pos_hbm,
    nbr_hbm,
    halo_hbm,
    lat_hbm,
    kfilter_hbm,
    node_weight_hbm,
    node_bias_hbm,
    message_weight_hbm,
    radial_weight_hbm,
    ewald_weight_hbm,
    out_all,
    feat,
    vec,
    pos,
    nbr,
    lat,
    kfilter,
    node_weight,
    node_bias,
    message_weight,
    radial_weight,
    ewald_weight,
    own_projected,
    group_feat,
    group_pos,
    side_rows,
    side_pos,
    side_halo,
    tables,
    near_totals,
    totals_out,
    totals_in,
    totals_all,
    chunk_filters,
    filtered,
    message_out,
    message_in_slots,
    source_rows,
    side_total,
    sent_total,
    stage_total,
    round_sems,
    local_sems,
    pos_sems,
    feat_sems,
    side_sem,
    stage_sems,
    send_sem,
):
    n_dom, n_kb, low_count, norm_scale = sizes
    dom, kb = lax.axis_index("dom"), lax.axis_index("kb")
    rank = dom * n_kb + kb
    slab_count = n_dom * n_kb
    channels, own = feat.shape
    slots = nbr.shape[0]
    width = kfilter.shape[1]
    members = n_dom // low_count
    pair = 2 if n_kb % 2 == 0 else 1
    pairs = n_kb // pair
    high, low = lax.div(dom, low_count), lax.rem(dom, low_count)
    peers = n_kb * low_count
    chunk = width // members

    def slot_between(target, source):
        return 1 + source - jnp.where(source > target, 1, 0)

    def member(number):
        return {"dom": number * low_count + low, "kb": kb}

    def peer(slot, sign=1):
        core, across, side = slot % pair, slot // pair % pairs, slot // n_kb
        place = lax.rem(lax.div(kb, pair) + sign * across + pairs, pairs)
        return {
            "dom": high * low_count + lax.rem(low + side, low_count),
            "kb": place * pair + lax.rem(lax.rem(kb, pair) + core, pair),
        }

    others = list(range(1, peers))

    def slab(steps):
        number = lax.rem(rank + steps + slab_count, slab_count)
        return {"dom": lax.div(number, n_kb), "kb": lax.rem(number, n_kb)}

    def remote(source, target, send_sem, recv_sem, device):
        return pltpu.make_async_remote_copy(
            src_ref=source,
            dst_ref=target,
            send_sem=send_sem,
            recv_sem=recv_sem,
            device_id=device,
            device_id_type=MESH,
        )

    def wait_bytes(ref, sem):
        pltpu.make_async_copy(ref, ref, sem).wait()

    barrier = pltpu.get_barrier_semaphore()
    targets = [
        jnp.where(high == 0, members - 1 - index, index + jnp.where(index >= high, 1, 0))
        for index in range(members - 1)
    ]
    greeted = [peer(slot) for slot in range(peers - 1, 0, -1)]
    beside = [(-1, high > 0), (1, high < members - 1)]
    beside_count = sum(jnp.where(there, 1, 0) for steps, there in beside)

    def tell_beside(sem):
        for steps, there in beside:

            @pl.when(there)
            def _(steps=steps):
                pl.semaphore_signal(
                    sem, inc=1, device_id=member(high + steps), device_id_type=MESH
                )

    for device in greeted:
        pl.semaphore_signal(barrier, inc=1, device_id=device, device_id_type=MESH)
    tell_beside(barrier)
    is_last = rank == slab_count - 1

    @pl.when(rank == 0)
    def _():
        pl.semaphore_signal(barrier, inc=1, device_id=slab(-1), device_id_type=MESH)

    start = pl.multiple_of(kb * (width * low_count) + low * width, math.gcd(width, 128))
    filter_start = pl.multiple_of(low * width, math.gcd(width, 128))
    staged = [
        (feat_hbm, feat),
        (ewald_weight_hbm, ewald_weight),
        (pos_hbm, pos),
        (lat_hbm.at[:, pl.ds(start, width)], lat),
        (kfilter_hbm.at[:, pl.ds(filter_start, width)], kfilter),
        (node_weight_hbm, node_weight),
        (node_bias_hbm, node_bias),
        (message_weight_hbm, message_weight),
        (nbr_hbm, nbr),
        (radial_weight_hbm, radial_weight),
        (vec_hbm, vec),
    ]
    local = [
        pltpu.make_async_copy(source, target, local_sems.at[0 if i < 2 else 1 if i < 4 else 2])
        for i, (source, target) in enumerate(staged)
    ]
    for copy in local:
        copy.start()

    for copy in local[2:4]:
        copy.wait()
    pl.semaphore_wait(barrier, len(greeted) + beside_count + jnp.where(is_last, 1, 0))
    pos_copies = [
        remote(pos, group_pos.at[slot], send_sem.at[0], pos_sems.at[slot // pair], peer(slot))
        for slot in others
    ]
    feat_copies = [
        remote(
            own_projected,
            group_feat.at[slot],
            send_sem.at[0],
            feat_sems.at[0 if slot < pair else 1],
            peer(slot),
        )
        for slot in others
    ]
    for copy in pos_copies[::-1]:
        copy.start()
    for copy in local[:2]:
        copy.wait()
    own_projected[...] = over_first(ewald_weight[...], feat[...]).astype(bf16)
    for copy in feat_copies[::-1]:
        copy.start()
    rounds = members - 2
    tell_beside(round_sems.at[0])

    def pass_round(number):
        pl.semaphore_wait(round_sems.at[number], beside_count)
        if number + 1 < rounds:
            tell_beside(round_sems.at[number + 1])

    around = [(0, 1, is_last), (1, -1, rank == 0)]
    inside = [
        (side, steps, lax.div(rank + steps + peers, peers) == high + 1)
        for side, steps in ((0, 1), (1, -1))
    ]
    across = [
        (side, steps, jnp.logical_not(jnp.logical_or(ends, within)))
        for (side, steps, ends), (_, _, within) in zip(around, inside)
    ]

    def send_sides(cases):
        for side, steps, chosen in cases:

            @pl.when(chosen)
            def _(side=side, steps=steps):
                send_side(side, steps)


    def send_side(side, steps):
        device = slab(steps)
        for copy in (
            remote(feat_hbm, side_rows.at[side, 0], send_sem.at[0], side_sem.at[0], device),
            remote(
                vec_hbm,
                side_rows.at[side, pl.ds(1, 3)],
                send_sem.at[0],
                side_sem.at[0],
                device,
            ),
            remote(pos_hbm, side_pos.at[side], send_sem.at[0], side_sem.at[0], device),
            remote(halo_hbm, side_halo.at[side], send_sem.at[0], side_sem.at[0], device),
        ):
            copy.start()

    send_sides(around[:1])
    lattice = lat[...].astype(f32)
    lattice_high = jnp.floor(lattice[2:3] * 0.0625) * 16.0
    lattice_low = lattice[2:3] - lattice_high
    lattice_parts = jnp.concatenate(
        [lattice[0:1]] * 3
        + [lattice[1:2]] * 3
        + [lattice_high] * 3
        + [lattice_low] * 3
        + [jnp.zeros((4, width), f32)],
        axis=0,
    ).astype(bf16)

    def position_parts(coords):
        rows = []
        for axis in (0, 1, 2, 2):
            rows += list(three_parts(coords[axis : axis + 1]))
        rows.append(jnp.zeros((4, coords.shape[1]), f32))
        return jnp.concatenate(rows, axis=0).astype(bf16)

    def make_tables(first, coords):
        turns = over_first(lattice_parts, position_parts(coords))
        cosine, sine = turn_tables(turns)
        span = coords.shape[1]
        columns = pl.ds(pl.multiple_of(first * own, span), span)
        for number in range(members):
            rows = slice(number * chunk, (number + 1) * chunk)
            tables[2 * number * chunk : (2 * number + 1) * chunk, columns] = cosine[rows]
            tables[(2 * number + 1) * chunk : 2 * (number + 1) * chunk, columns] = sine[rows]

    def totals_of(first, features):
        return lax.dot_general(
            features,
            tables[:, first * own : first * own + features.shape[1]],
            (((1,), (1,)), ((), ())),
            preferred_element_type=f32,
        )

    make_tables(0, pos[...])
    def batch_features(first, count):
        return jnp.concatenate(
            [own_projected[...] if slot == 0 else group_feat[slot] for slot in range(first, first + count)],
            axis=1,
        )

    def wait_features(first, count):
        begin = max(first, 1)
        wait_bytes(
            group_feat.at[pl.ds(begin, first + count - begin)], feat_sems.at[0 if first < pair else 1]
        )

    for slot in range(1, pair):
        wait_bytes(group_pos.at[slot], pos_sems.at[0])
        make_tables(slot, group_pos[slot])
    if pair > 1:
        wait_features(0, pair)
    near_totals[...] = totals_of(0, batch_features(0, pair))
    pass_round(0)
    send_sides(across)
    order = list(range(1, peers // pair))
    if pairs == 2 and low_count == 2:
        place = lax.div(kb, pair)
        aligned = place == low
        order = [
            jnp.where(jnp.logical_and(place == 0, low == 1), 2, 1),
            jnp.where(aligned, 2, 3),
            jnp.where(aligned, 3, jnp.where(low == 1, 1, 2)),
        ]
    for batch in order:
        slots_of = [batch * pair + core for core in range(pair)]
        wait_bytes(
            group_pos.at[pl.ds(batch * pair, pair)],
            pos_sems.at[batch],
        )
        make_tables(
            batch * pair, jnp.concatenate([group_pos[slot] for slot in slots_of], axis=1)
        )
    wait_features(pair, peers - pair)
    totals = near_totals[...] + totals_of(pair, batch_features(pair, peers - pair))
    for number in range(members):
        totals_out[number] = totals[:, 2 * number * chunk : 2 * (number + 1) * chunk].astype(bf16)
    for number in range(1, rounds):
        pass_round(number)
    def send_totals(number):
        remote(
            totals_out.at[number],
            totals_in.at[slot_between(number, high)],
            send_sem.at[1],
            stage_sems.at[0],
            member(number),
        ).start()

    for index in range(members - 1):
        number = jnp.where(
            index < high, lax.rem(high - index, jnp.maximum(high, 1)), index + 1
        )

        between = jnp.logical_and(number > 0, number < high)

        @pl.when(jnp.logical_not(between))
        def _(number=number):
            send_totals(number)

    @pl.when(high > 0)
    def _():
        remote(
            totals_out.at[pl.ds(1, members - 1)],
            totals_all.at[high - 1],
            send_sem.at[1],
            stage_sems.at[3],
            member(0),
        ).start()

    for step in range(1, members - 1):
        number = high - step

        @pl.when(number > 0)
        def _(number=number):
            send_totals(number)

    send_sides(inside)
    for copy in local[4:]:
        copy.wait()
    for number in range(members):
        part = kfilter[:, number * chunk : (number + 1) * chunk] * norm_scale
        chunk_filters[number] = jnp.concatenate([part, part], axis=1)
    bias = jnp.broadcast_to(node_bias[...], (own, channels)).T

    def fill_sources(index, one_feat, one_vec):
        columns = slice(index * own, (index + 1) * own)
        value = over_first(node_weight[...], one_feat[...]) + bias
        hidden = (value / (1.0 + jnp.exp(-value))).astype(bf16)
        source_rows[: 3 * channels, columns] = over_first(message_weight[...], hidden).astype(bf16)
        source_rows[3 * channels :, columns] = one_vec[...].reshape(3 * channels, own)

    fill_sources(0, feat, vec)
    def send_filtered(number):
        remote(
            filtered.at[high],
            filtered.at[high],
            send_sem.at[1],
            stage_sems.at[1],
            member(number),
        ).start()

    wait_bytes(totals_in.at[pl.ds(1, members - 1)], stage_sems.at[0])
    total = totals_out[high].astype(f32)
    for slot in range(1, members):
        total = total + totals_in[slot].astype(f32)
    filtered[high] = (chunk_filters[high] * total).astype(bf16)

    @pl.when(high > 0)
    def _():
        for index in range(members - 2):
            send_filtered(1 + index + jnp.where(index + 1 >= high, 1, 0))

    @pl.when(high == 0)
    def _():
        for number in range(members - 1, 0, -1):
            send_filtered(number)

    send_sides(around[1:])
    @pl.when(high == 0)
    def _():
        wait_bytes(totals_all, stage_sems.at[3])
        for number in range(1, members):
            total = totals_out[number].astype(f32)
            for source in range(members - 1):
                total = total + totals_all[source, number - 1].astype(f32)
            filtered[number] = (chunk_filters[number] * total).astype(bf16)

    @pl.when(high > 0)
    def _():
        wait_bytes(filtered.at[pl.ds(1, members - 1)], stage_sems.at[1])

    spectrum = jnp.concatenate([filtered[number] for number in range(members)], axis=1)
    def messages_of(first, last):
        return jnp.dot(
            spectrum, tables[:, first * own : last * own], preferred_element_type=f32
        )

    def send_message(slot, value):
        message_out[slot] = value.astype(bf16)
        remote(
            message_out.at[slot],
            message_in_slots.at[slot],
            send_sem.at[0],
            stage_sems.at[2],
            peer(slot, -1),
        ).start()

    group = pair * (2 if peers % (2 * pair) == 0 else 1)
    for first in range(peers - group, -1, -group):
        values = messages_of(first, first + group)
        for slot in range(first + group - 1, first - 1, -1):
            value = values[:, (slot - first) * own : (slot - first + 1) * own]
            if slot > 0:
                send_message(slot, value)
            else:
                result = value
    wait_bytes(side_total, side_sem.at[0])
    for side in range(2):
        fill_sources(1 + side, side_rows.at[side, 0], side_rows.at[side, pl.ds(1, 3)])
    ids = nbr[...]
    reach = side_halo.shape[2]

    def picked(row, index):
        return jnp.take_along_axis(
            jnp.broadcast_to(row, (slots, row.shape[1])), index, axis=1, mode="promise_in_bounds"
        )

    below_slot = jnp.clip(ids - own, 0, reach - 1)
    above_slot = jnp.clip(ids - (own + reach), 0, reach - 1)
    own_atom = jnp.clip(ids, 0, own - 1)
    below_atom = picked(side_halo[0, 0:1], below_slot)
    above_atom = picked(side_halo[1, 1:2], above_slot)
    is_own = ids < own
    is_below = ids < own + reach
    used = ids < own + 2 * reach
    atoms = jnp.where(
        is_own,
        ids,
        jnp.where(is_below, below_atom + own, jnp.where(used, above_atom + 2 * own, 3 * own)),
    )
    cartesian = []
    for axis in range(3):
        taken = jnp.where(
            is_own,
            picked(pos[axis : axis + 1], own_atom),
            jnp.where(
                is_below,
                picked(side_pos[0, axis : axis + 1], below_atom),
                picked(side_pos[1, axis : axis + 1], above_atom),
            ),
        )
        taken = jnp.where(used, taken, 0.0)
        offset = taken - pos[axis : axis + 1]
        offset = offset - jnp.floor(offset + 0.5)
        cartesian.append(offset * (side_length if axis < 2 else slab_depth * slab_count))
    distance = jnp.sqrt(
        cartesian[0] * cartesian[0] + cartesian[1] * cartesian[1] + cartesian[2] * cartesian[2]
    )
    limit = jnp.maximum(distance, distance_floor)
    direction = [part / limit for part in cartesian]

    radial_count = radial_weight.shape[0]
    spread = 1.5 * radial_reach / radial_count
    centers = lax.broadcasted_iota(jnp.int32, (radial_count, own), 0).astype(f32) * (
        radial_reach / (radial_count - 1)
    )
    numbers = lax.broadcasted_iota(jnp.int32, (3 * own, own), 0)

    def edges(j, sums):
        row = slice(j, j + 1)
        chosen = jnp.where(numbers == atoms[row], 1.0, 0.0).astype(bf16)
        gathered = jnp.dot(source_rows[...], chosen, preferred_element_type=f32)
        scaled = (distance[row] - centers) * (1.0 / spread)
        radial = jnp.exp(-(scaled * scaled)).astype(bf16)
        terms = gathered[: 3 * channels] * over_first(radial_weight[...], radial)
        first = terms[:channels]
        second = terms[channels : 2 * channels]
        third = terms[2 * channels :]
        new = [sums[0] + first]
        for axis in range(3):
            begin = (3 + axis) * channels
            new.append(
                sums[1 + axis]
                + gathered[begin : begin + channels] * second
                + third * direction[axis][row]
            )
        return new

    sums = [jnp.zeros((channels, own), f32)] * 4
    half = slots // 2
    for j in range(half):
        sums = edges(j, sums)

    for j in range(half, slots):
        sums = edges(j, sums)
    for axis in range(3):
        out_all[1 + axis] = (vec[axis].astype(f32) + sums[1 + axis]).astype(bf16)
    result = result + feat[...].astype(f32) + sums[0]

    wait_bytes(message_in_slots.at[pl.ds(1, peers - 1)], stage_sems.at[2])
    for d in range(1, peers):
        result = result + message_in_slots[d].astype(f32)
    out_all[0] = result.astype(bf16)
    wait_bytes(sent_total, send_sem.at[0])
    @pl.when(high > 0)
    def _():
        wait_bytes(stage_total.at[pl.ds(0, 3 * members - 4)], send_sem.at[1])

    @pl.when(high == 0)
    def _():
        wait_bytes(stage_total.at[pl.ds(0, 2 * members - 2)], send_sem.at[1])


def split_kernel(both, out_feat, out_vec, sems):
    feat_copy = pltpu.make_async_copy(both.at[0], out_feat, sems.at[0])
    vec_copy = pltpu.make_async_copy(both.at[pl.ds(1, 3)], out_vec, sems.at[0])
    feat_copy.start()
    vec_copy.start()
    feat_copy.wait()
    vec_copy.wait()


def shards(
    features,
    vectors,
    positions,
    neighbours,
    halo_lists,
    lattice,
    kspace_filter,
    node_weight,
    node_bias,
    message_weight,
    radial_weight,
    ewald_weight,
):
    n_dom, n_kb = lax.axis_size("dom"), lax.axis_size("kb")
    channels, own = features.shape
    reach = halo_lists.shape[1]
    width = kspace_filter.shape[1]
    low_count = 2 if n_dom % 2 == 0 else 1
    members, peers = n_dom // low_count, n_kb * low_count
    width = width // low_count
    chunk = width // members
    pair = 2 if n_kb % 2 == 0 else 1
    norm_scale = 1.0 / math.sqrt(lattice.shape[1] * own * n_dom * n_kb)
    row_bytes = 128 * 4
    block_bytes = channels * own * 2
    side_bytes = 2 * (4 * block_bytes + 3 * own * 4 + 2 * reach * 4)
    sent_bytes = side_bytes + (peers - 1) * (3 * own * 4 + 2 * block_bytes)
    vmem = pl.BlockSpec(memory_space=pltpu.VMEM)
    hbm = pl.BlockSpec(memory_space=pltpu.HBM)
    dma = pltpu.SemaphoreType.DMA
    bias_row = node_bias[None, :]

    def like(array):
        return pltpu.VMEM(array.shape, array.dtype)

    both = pl.pallas_call(
        functools.partial(kernel, (n_dom, n_kb, low_count, norm_scale)),
        out_shape=pltpu.VMEM((4, channels, own), bf16),
        in_specs=[hbm] * 12,
        out_specs=vmem,
        scratch_shapes=[
            like(features),
            like(vectors),
            like(positions),
            like(neighbours),
            pltpu.VMEM((3, width), jnp.int32),
            pltpu.VMEM((channels, width), f32),
            like(node_weight),
            like(bias_row),
            like(message_weight),
            like(radial_weight),
            like(ewald_weight),
            like(features),
            pltpu.VMEM((peers, channels, own), bf16),
            pltpu.VMEM((peers, 3, own), f32),
            pltpu.VMEM((2, 4, channels, own), bf16),
            pltpu.VMEM((2, 3, own), f32),
            pltpu.VMEM((2, 2, reach), jnp.int32),
            pltpu.VMEM((2 * width, peers * own), bf16),
            pltpu.VMEM((channels, 2 * width), f32),
            pltpu.VMEM((members, channels, 2 * chunk), bf16),
            pltpu.VMEM((members, channels, 2 * chunk), bf16),
            pltpu.VMEM((members - 1, members - 1, channels, 2 * chunk), bf16),
            pltpu.VMEM((members, channels, 2 * chunk), f32),
            pltpu.VMEM((members, channels, 2 * chunk), bf16),
            pltpu.VMEM((peers, channels, own), bf16),
            pltpu.VMEM((peers, channels, own), bf16),
            pltpu.VMEM((6 * channels, 3 * own), bf16),
            pltpu.VMEM((side_bytes // row_bytes, 1, 128), f32),
            pltpu.VMEM((sent_bytes // row_bytes, 1, 128), f32),
            pltpu.VMEM((3 * members, channels, 2 * chunk), bf16),
            pltpu.SemaphoreType.REGULAR((members - 2,)),
            dma((3,)),
            dma((peers // pair,)),
            dma((2,)),
            dma((1,)),
            dma((4,)),
            dma((2,)),
        ],
        compiler_params=pltpu.CompilerParams(collective_id=0, has_side_effects=True),
    )(
        features,
        vectors,
        positions,
        neighbours,
        halo_lists,
        lattice,
        kspace_filter,
        node_weight,
        bias_row,
        message_weight,
        radial_weight,
        ewald_weight,
    )
    return pl.pallas_call(
        split_kernel,
        out_shape=(
            jax.ShapeDtypeStruct(features.shape, bf16),
            jax.ShapeDtypeStruct(vectors.shape, bf16),
        ),
        in_specs=[vmem],
        out_specs=(pl.BlockSpec(memory_space=pl.ANY),) * 2,
        scratch_shapes=[dma((1,))],
    )(pltpu.with_memory_space_constraint(both, pltpu.VMEM))


def solution(mesh):
    atoms = P(None, ("dom", "kb"))
    placed = (
        atoms,
        P(None, None, ("dom", "kb")),
        atoms,
        atoms,
        atoms,
        P(),
        P(None, "kb"),
        P(),
        P(),
        P(),
        P(),
        P(),
    )
    return jax.shard_map(
        shards,
        mesh=mesh,
        in_specs=placed,
        out_specs=(atoms, P(None, None, ("dom", "kb"))),
        check_vma=False,
    )
```
